128 devices in a mesh: row: 8 (over x_hi, z), col: 16 (over y, x_lo, core).
Axes of the slice: x: 4 (x_hi: 2, x_lo: 2; x = x_hi * 2 + x_lo), y: 4, z: 4, core: 2. Of those that a mesh axis runs over, the one named last changes fastest.
Arguments:
- a_held: float32 [4096, 128, 128], P(('row', 'col')), may hold values from -0.5 to 0.5
- a_slot: int32 [4096], P(('row', 'col')), may hold values from 0 to 4095, as said below
- a_col: int32 [4096], P(('row', 'col')), may hold values from -1 to 15, as said below
- b_held: float32 [8192, 128, 128], P(('row', 'col')), may hold values from -6 to 6
- b_slot: int32 [8192], P(('row', 'col')), may hold values from 0 to 8191, as said below
- b_col: int32 [8192], P(('row', 'col')), may hold values from -1 to 15, as said below
- c_col: int32 [128, 96], P('row', 'col'), may hold values from -1 to 15, as said below
Outputs:
- product: float32 [128, 96, 128, 128], P('row', 'col')
The draws below stay inside these ranges and needn't reach their ends.
Inputs may be any that keep to these rules, and one draw needn't show every extreme that they name: `a_slot`: a permutation of 0 to 4095; one device holds at most 1 slots of one left panel, and some device holds exactly that many. `a_col`: the filled columns of one block row of a left panel are distinct; some block row of every panel has all 4 slots filled. `b_slot`: a permutation of 0 to 8191; one device holds at most 1 slots of one right panel, and some device holds exactly that many. `b_col`: the filled columns of one inner block row of a right panel are distinct; some block row of every panel has all 4 slots filled. `c_col`: the retained columns of one block row within one grid column are distinct, -1 marks an empty slot; every grid column has a block row with all 6 slots retained.
All inputs are finite; a program needn't handle non-finite values.
Results may differ from the reference program's by a relative error of at most 0.0003.
Values sent between devices are 32-bit elements; how exact they have to be, the bound alone decides.
A program may use at most 192 MiB of HBM per device.

```python
import jax
import jax.numpy as jnp
from jax import lax

BLOCK_EDGE = 128
RB = 16
KPB = 16
CB = 16
WA = 4
WB = 4
WC = 6
STEPS = 3
GRID_ROWS = 8
GRID_COLS = 16
PANELS_A = 64
PANELS_B = 128
SLOTS_A = 64
SLOTS_B = 64
HOLD_A = 32
HOLD_B = 64
DEVICES = 128


def block_pattern(random_seed_key, panel_list, slot_count, row_indices, window_width, window_span, grid_spacing):
    keys = jax.random.split(random_seed_key, 4)
    panel_order = jax.random.permutation(keys[0], panel_list).astype(jnp.int32)
    panel_indices = jnp.arange(panel_list, dtype=jnp.int32)[:, None]
    slot_indices = jnp.arange(slot_count, dtype=jnp.int32)[None, :]
    holder_rank = (grid_spacing * panel_order[:, None] + slot_indices) % (GRID_ROWS * GRID_COLS)
    entry_values = panel_indices * slot_count + slot_indices
    sorting_keys = (holder_rank * (panel_list * slot_count) + entry_values).reshape(-1)
    arrangement = jnp.argsort(sorting_keys, stable=True)
    slot_list = entry_values.reshape(-1)[arrangement].astype(jnp.int32)
    live_count = jax.random.randint(keys[1], (panel_list, row_indices), max(1, window_width - 1), window_width + 1)
    full_row = jax.random.randint(keys[2], (panel_list, 1), 0, row_indices)
    live_count = jnp.where(jnp.arange(row_indices)[None, :] == full_row, window_width, live_count)
    row_keys = jax.random.split(keys[3], panel_list * row_indices)
    chosen = jax.vmap(lambda row_key: jax.random.permutation(row_key, window_span)[:window_width])(row_keys)
    chosen = chosen.reshape(panel_list, row_indices, window_width)
    lane_index = jnp.arange(window_width)[None, None, :]
    column_indices = jnp.where(lane_index < live_count[:, :, None], chosen, -1).astype(jnp.int32).reshape(-1)
    return (slot_list, column_indices[slot_list])


def pattern_left(random_seed_key):
    grid_spacing = GRID_ROWS * GRID_COLS // PANELS_A
    return block_pattern(jax.random.fold_in(random_seed_key, 101), PANELS_A, SLOTS_A, RB, WA, KPB, grid_spacing)


def pattern_right(random_seed_key):
    return block_pattern(jax.random.fold_in(random_seed_key, 202), PANELS_B, SLOTS_B, KPB, WB, CB, 1)


def draw_a_slot(key, part):
    return pattern_left(key)[0]


def draw_a_col(key, part):
    return pattern_left(key)[1]


def draw_b_slot(key, part):
    return pattern_right(key)[0]


def draw_b_col(key, part):
    return pattern_right(key)[1]


def draw_c_col(key, part):
    keys = jax.random.split(jax.random.fold_in(key, 303), 3)
    total_rows = GRID_ROWS * RB
    live_count = jax.random.randint(keys[0], (total_rows, GRID_COLS), 1, WC + 1)
    full_row = jax.random.randint(keys[1], (1, GRID_COLS), 0, RB)
    row_index = jnp.arange(total_rows)[:, None] % RB
    live_count = jnp.where(row_index == full_row, WC, live_count)
    row_keys = jax.random.split(keys[2], total_rows * GRID_COLS)
    chosen = jax.vmap(lambda row_key: jax.random.permutation(row_key, CB)[:WC])(row_keys)
    chosen = chosen.reshape(total_rows, GRID_COLS, WC)
    lane_index = jnp.arange(WC)[None, None, :]
    column_indices = jnp.where(lane_index < live_count[:, :, None], chosen, -1).astype(jnp.int32)
    return column_indices.reshape(total_rows, GRID_COLS * WC)


def levels(rng, extent, shards, least, largest):
    level = 1.0
    for axis_at, shards_of in shards:
        steps = jax.random.uniform(jax.random.fold_in(jax.random.fold_in(rng, 6), axis_at), (shards_of,), jnp.float32, least / len(shards), largest / len(shards))
        level = level * jnp.repeat(jnp.exp(steps), extent[axis_at] // shards_of).reshape((-1,) + (1,) * (len(extent) - 1 - axis_at))
    return level


def normal_values(own_key, shape, spread, limit, shards=(), kind=jnp.bfloat16):
    values = jax.random.normal(own_key, shape, jnp.float32) * spread
    if len(shards) > 0:
        values = levels(own_key, shape, shards, -0.22, 0.18) * values
    return jnp.clip(values, min=-limit, max=limit).astype(kind)


def setup_inputs(seed: int = 0) -> dict:
    splits = jax.random.split(jax.random.key(seed), 8)
    return {
        "a_held": normal_values(splits[0], (DEVICES * HOLD_A, BLOCK_EDGE, BLOCK_EDGE), BLOCK_EDGE ** -0.5, 0.5, ((0, 128),), jnp.float32),
        "a_slot": draw_a_slot(jax.random.fold_in(splits[7], 71), 0),
        "a_col": draw_a_col(jax.random.fold_in(splits[7], 71), 0),
        "b_held": normal_values(splits[3], (DEVICES * HOLD_B, BLOCK_EDGE, BLOCK_EDGE), 1.0, 6.0, ((0, 128),), jnp.float32),
        "b_slot": draw_b_slot(jax.random.fold_in(splits[7], 71), 0),
        "b_col": draw_b_col(jax.random.fold_in(splits[7], 71), 0),
        "c_col": draw_c_col(jax.random.fold_in(splits[7], 71), 0),
    }


def place_every_block(held_blocks, slot_table, column_indices, panel_list, slot_count):
    block_values = jnp.zeros((panel_list * slot_count, BLOCK_EDGE, BLOCK_EDGE), jnp.float32).at[slot_table].set(held_blocks.astype(jnp.float32))
    block_labels = jnp.full((panel_list * slot_count,), -1, jnp.int32).at[slot_table].set(column_indices)
    return block_values, block_labels


def block_terms(left, left_cols, right, right_cols, kept):
    safe = jnp.maximum(left_cols, 0)
    chosen = jnp.take(right, safe, axis=0)
    chosen_cols = jnp.take(right_cols, safe, axis=0)
    pieces = jnp.einsum("rwij,rwvjl->rwvil", left, chosen, precision=lax.Precision.HIGHEST)
    match = (left_cols >= 0)[:, None, :, None] & (chosen_cols[:, None, :, :] == kept[:, :, None, None]) & (kept >= 0)[:, :, None, None]
    return jnp.einsum("rtwv,rwvil->rtil", match.astype(pieces.dtype), pieces, precision=lax.Precision.HIGHEST)


def reference(a_held, a_slot, a_col, b_held, b_slot, b_col, c_col):
    a_vals, a_labels = place_every_block(a_held, a_slot, a_col, PANELS_A, SLOTS_A)
    a_vals = a_vals.reshape(PANELS_A, RB, WA, BLOCK_EDGE, BLOCK_EDGE)
    a_labels = a_labels.reshape(PANELS_A, RB, WA)
    b_vals, b_labels = place_every_block(b_held, b_slot, b_col, PANELS_B, SLOTS_B)
    b_vals = b_vals.reshape(PANELS_B, KPB, WB, BLOCK_EDGE, BLOCK_EDGE)
    b_labels = b_labels.reshape(PANELS_B, KPB, WB)
    retained = c_col.reshape(GRID_ROWS, RB, GRID_COLS, WC).transpose(0, 2, 1, 3)

    def device_tile(position):
        grid_row = position // GRID_COLS
        grid_col = position % GRID_COLS
        kept = retained[grid_row, grid_col]
        accum = jnp.zeros((RB, WC, BLOCK_EDGE, BLOCK_EDGE), a_vals.dtype)
        for iteration in range(STEPS):
            inner = (grid_row + grid_col + iteration) % GRID_ROWS
            left_index = grid_row * GRID_ROWS + inner
            right_index = inner * GRID_COLS + grid_col
            accum = accum + block_terms(a_vals[left_index], a_labels[left_index], b_vals[right_index], b_labels[right_index], kept)
        return accum

    tiles = lax.map(device_tile, jnp.arange(GRID_ROWS * GRID_COLS, dtype=jnp.int32))
    tiles = tiles.reshape(GRID_ROWS, GRID_COLS, RB, WC, BLOCK_EDGE, BLOCK_EDGE).transpose(0, 2, 1, 3, 4, 5)
    return tiles.reshape(GRID_ROWS * RB, GRID_COLS * WC, BLOCK_EDGE, BLOCK_EDGE)
```

```python
import functools

import jax
import jax.numpy as jnp
from jax import lax
from jax.experimental import pallas as pl
from jax.experimental.pallas import tpu as pltpu
from jax.sharding import PartitionSpec as P

KPB = 16
WA = 4
WB = 4
STEPS = 3
HBM = pl.BlockSpec(memory_space=pl.ANY)


def shifted(value, axis, steps):
    count = lax.axis_size(axis)
    pairs = [(source, (source + steps) % count) for source in range(count)]
    return lax.ppermute(value, axis, pairs)


def pack_right_kernel(dest, held, out, sems):
    count = held.shape[0]

    def copy(entry):
        return pltpu.make_async_copy(held.at[entry], out.at[dest[entry]], sems.at[entry])

    pl.loop(0, count)(lambda entry: copy(entry).start())
    pl.loop(0, count)(lambda entry: copy(entry).wait())


def pack_left_kernel(copies, dest, held, out, sems):
    count = held.shape[0]
    part = out.shape[1]

    def copy(entry, half):
        return pltpu.make_async_copy(
            held.at[entry, pl.ds(half * part, part)],
            out.at[dest[half, entry]],
            sems.at[half, entry],
        )

    for half in range(copies):
        pl.loop(0, count)(lambda entry: copy(entry, half).start())
    for half in range(copies):
        pl.loop(0, count)(lambda entry: copy(entry, half).wait())


def collect_kernel(source, recv, out, sems):
    count = out.shape[0]

    def copy(slot):
        return pltpu.make_async_copy(recv.at[source[slot]], out.at[slot], sems.at[slot])

    pl.loop(0, count)(lambda slot: copy(slot).start())
    pl.loop(0, count)(lambda slot: copy(slot).wait())


SMEM = pl.BlockSpec(memory_space=pltpu.SMEM)


def pack_right(held, dest, devices):
    return pl.pallas_call(
        pack_right_kernel,
        out_shape=jax.ShapeDtypeStruct((devices,) + held.shape[1:], held.dtype),
        in_specs=[SMEM, HBM],
        out_specs=HBM,
        scratch_shapes=[pltpu.SemaphoreType.DMA((held.shape[0],))],
        name="pack_right",
    )(dest, held)


def pack_left(held, dest, devices):
    copies = dest.shape[0]
    count, rows, cols = held.shape
    return pl.pallas_call(
        functools.partial(pack_left_kernel, copies),
        out_shape=jax.ShapeDtypeStruct((devices, rows // copies, cols), held.dtype),
        in_specs=[SMEM, HBM],
        out_specs=HBM,
        scratch_shapes=[pltpu.SemaphoreType.DMA((copies, count))],
        name="pack_left",
    )(dest, held)


def collect(recv, source):
    return pl.pallas_call(
        collect_kernel,
        out_shape=jax.ShapeDtypeStruct(source.shape + recv.shape[1:], recv.dtype),
        in_specs=[SMEM, HBM],
        out_specs=HBM,
        scratch_shapes=[pltpu.SemaphoreType.DMA(source.shape)],
        name="collect",
    )(source, recv)


def split(value):
    high = value.astype(jnp.bfloat16)
    low = (value - high.astype(jnp.float32)).astype(jnp.bfloat16)
    return high, low


def product_kernel(steps, width, index, order, *refs):
    halves = refs[: 2 * steps]
    rights = refs[2 * steps : 3 * steps]
    out = refs[3 * steps]
    buf, high, low, sems = refs[3 * steps + 1 :]
    row = pl.program_id(0)
    slots = rights[0].shape[0]
    edge = out.shape[-1]
    group = buf.shape[1]
    chunks = steps * slots // group

    @pl.when(row == 0)
    def _():
        per = slots // group

        def copy(at):
            return pltpu.make_async_copy(
                rights[at // per].at[pl.ds((at % per) * group, group)], buf.at[at % 2], sems.at[at % 2]
            )

        copy(0).start()
        for at in range(chunks):
            if at + 1 < chunks:
                copy(at + 1).start()
            copy(at).wait()
            step, first = at // per, (at % per) * group

            def body(slot):
                hi, lo = split(buf[at % 2, slot])
                high[step, first + slot] = hi
                low[step, first + slot] = lo

            pl.loop(0, group)(body)
        for step in range(steps):
            high[step, slots] = jnp.zeros((edge, edge), jnp.bfloat16)
            low[step, slots] = jnp.zeros((edge, edge), jnp.bfloat16)

    for kept in range(width):
        out[0, kept] = jnp.zeros((edge, edge), jnp.float32)
    for step in range(steps):
        swap = order[step]
        for slot in range(WA):
            first, second = halves[2 * step][slot], halves[2 * step + 1][slot]
            left = jnp.concatenate(
                [jnp.where(swap > 0, second, first), jnp.where(swap > 0, first, second)], axis=0
            )
            a_hi, a_lo = split(left)
            both = jnp.concatenate([a_hi, a_lo], axis=1)
            for kept in range(width):
                at = index[((row * steps + step) * WA + slot) * width + kept]
                b_hi = high[step, at]
                b_lo = low[step, at]
                out[0, kept] += jnp.dot(
                    both, jnp.concatenate([b_hi, b_hi], axis=0), preferred_element_type=jnp.float32
                ) + jnp.dot(a_hi, b_lo, preferred_element_type=jnp.float32)


def products(index, order, halves, rights, rows, width):
    steps = len(rights)
    slots, edge, _ = rights[0].shape
    part = halves[0].shape[1]
    group = 16
    left_spec = pl.BlockSpec((WA, part, edge), lambda row, *_: (row, 0, 0))
    return pl.pallas_call(
        functools.partial(product_kernel, steps, width),
        grid_spec=pltpu.PrefetchScalarGridSpec(
            num_scalar_prefetch=2,
            grid=(rows,),
            in_specs=[left_spec] * len(halves) + [HBM] * steps,
            out_specs=pl.BlockSpec((1, width, edge, edge), lambda row, *_: (row, 0, 0, 0)),
            scratch_shapes=[
                pltpu.VMEM((2, group, edge, edge), jnp.float32),
                pltpu.VMEM((steps, slots + 1, edge, edge), jnp.bfloat16),
                pltpu.VMEM((steps, slots + 1, edge, edge), jnp.bfloat16),
                pltpu.SemaphoreType.DMA((2,)),
            ],
        ),
        out_shape=jax.ShapeDtypeStruct((rows, width, edge, edge), jnp.float32),
        compiler_params=pltpu.CompilerParams(
            dimension_semantics=("arbitrary",), vmem_limit_bytes=40 * 1024 * 1024
        ),
        name="products",
    )(index, order, *halves, *rights)


def on_device(a_held, a_slot, a_col, b_held, b_slot, b_col, c_col):
    grid_rows = lax.axis_size("row")
    grid_cols = lax.axis_size("col")
    devices = grid_rows * grid_cols
    copies = grid_cols // grid_rows
    i = lax.axis_index("row")
    c = lax.axis_index("col")
    rows, width = c_col.shape
    hold_a, hold_b = a_slot.shape[0], b_slot.shape[0]
    slots_a, slots_b = rows * WA, KPB * WB

    panel = a_slot // slots_a
    at_row, inner = panel // grid_rows, panel % grid_rows
    dest = at_row * grid_cols + (inner - at_row - 1) % grid_rows
    dest_left = dest[None, :] + grid_rows * jnp.arange(copies, dtype=jnp.int32)[:, None]
    panel = b_slot // slots_b
    inner, at_col = panel // grid_cols, panel % grid_cols
    dest_right = ((inner - at_col - 1) % grid_rows) * grid_cols + at_col

    labels = lax.all_gather(jnp.concatenate([a_slot, a_col, b_slot, b_col]), ("row", "col"))
    parts = [hold_a, 2 * hold_a, 2 * hold_a + hold_b]
    all_a, all_acol, all_b, all_bcol = (part.reshape(-1) for part in jnp.split(labels, parts, axis=1))

    k = (i + c + jnp.arange(STEPS, dtype=jnp.int32)) % grid_rows

    def look_up(panels, slots, table, columns, hold):
        wanted = panels[:, None] * slots + jnp.arange(slots, dtype=jnp.int32)[None, :]
        holder = jnp.arange(table.shape[0], dtype=jnp.int32) // hold
        code = holder * 32 + columns + 1
        found = jnp.sum(jnp.where(table[None, None, :] == wanted[:, :, None], code, 0), axis=2)
        return found // 32, found % 32 - 1

    src_left, col_left = look_up(i * grid_rows + k, slots_a, all_a, all_acol, hold_a)
    src_right, col_right = look_up(k * grid_cols + c, slots_b, all_b, all_bcol, hold_b)

    u = jnp.arange(slots_b, dtype=jnp.int32)
    lefts = col_left.reshape(STEPS, rows, WA).transpose(1, 0, 2)[:, :, :, None, None]
    hit = (
        (lefts == (u // WB))
        & (col_right[None, :, None, None, :] == c_col[:, None, None, :, None])
        & (c_col >= 0)[:, None, None, :, None]
    )
    index = slots_b - jnp.sum(jnp.where(hit, slots_b - u, 0), axis=4)
    index = index.reshape(-1).astype(jnp.int32)

    send_left = pack_left(a_held, dest_left, devices)
    send_right = pack_right(b_held, dest_right, devices)
    recv_left = lax.all_to_all(send_left, ("row", "col"), split_axis=0, concat_axis=0, tiled=True)
    recv_right = lax.all_to_all(send_right, ("row", "col"), split_axis=0, concat_axis=0, tiled=True)

    own = collect(recv_left, src_left[1])
    other = shifted(own, "col", grid_rows)
    right = collect(recv_right, src_right[1])
    halves = [
        shifted(own, "col", 1),
        shifted(other, "col", 1),
        own,
        other,
        shifted(own, "col", -1),
        shifted(other, "col", -1),
    ]
    rights = [shifted(right, "row", 1), right, shifted(right, "row", -1)]
    homes = (c + jnp.arange(-1, 2, dtype=jnp.int32)) % grid_cols
    order = (homes >= grid_rows).astype(jnp.int32)
    return products(index, order, halves, rights, rows, width)


def solution(mesh):
    return jax.shard_map(
        on_device,
        mesh=mesh,
        in_specs=(
            P(("row", "col"), None, None),
            P(("row", "col")),
            P(("row", "col")),
            P(("row", "col"), None, None),
            P(("row", "col")),
            P(("row", "col")),
            P("row", "col"),
        ),
        out_specs=P("row", "col", None, None),
        check_vma=False,
    )
```

```python
import functools

import jax
import jax.numpy as jnp
from jax import lax
from jax.experimental import pallas as pl
from jax.experimental.pallas import tpu as pltpu
from jax.sharding import PartitionSpec as P

KPB = 16
WA = 4
WB = 4
STEPS = 3
HBM = pl.BlockSpec(memory_space=pl.ANY)


def shifted(value, axis, steps):
    count = lax.axis_size(axis)
    pairs = [(source, (source + steps) % count) for source in range(count)]
    return lax.ppermute(value, axis, pairs)


def permuted(value, axis, target):
    count = lax.axis_size(axis)
    return lax.ppermute(value, axis, [(at, target(at) % count) for at in range(count)])


def relay(count, load, store):
    pl.loop(0, count)(lambda at: load(at).start())

    def body(at):
        load(at).wait()
        store(at)

    pl.loop(0, count)(body)


def pack_right_kernel(dest, held, out, buf, sems):
    count = held.shape[0]

    def load(at):
        return pltpu.make_async_copy(held.at[at], buf.at[at], sems.at[0, at])

    def save(at):
        return pltpu.make_async_copy(buf.at[at], out.at[dest[at]], sems.at[1, at])

    relay(count, load, lambda at: save(at).start())
    pl.loop(0, count)(lambda at: save(at).wait())


def pack_left_kernel(copies, dest, held, out, buf, sems):
    count = held.shape[0]
    part = out.shape[1]

    def load(at):
        return pltpu.make_async_copy(held.at[at], buf.at[at], sems.at[0, at])

    def save(at, half):
        return pltpu.make_async_copy(
            buf.at[at, pl.ds(half * part, part)], out.at[dest[half, at]], sems.at[1 + half, at]
        )

    def store(at):
        for half in range(copies):
            save(at, half).start()

    relay(count, load, store)
    for half in range(copies):
        pl.loop(0, count)(lambda at: save(at, half).wait())


def collect_kernel(source, recv, out, buf, sems):
    count = out.shape[0]

    def load(at):
        return pltpu.make_async_copy(recv.at[source[at]], buf.at[at], sems.at[0, at])

    def save(at):
        return pltpu.make_async_copy(buf.at[at], out.at[at], sems.at[1, at])

    relay(count, load, lambda at: save(at).start())
    pl.loop(0, count)(lambda at: save(at).wait())


SMEM = pl.BlockSpec(memory_space=pltpu.SMEM)


def pack_right(held, dest, devices):
    return pl.pallas_call(
        pack_right_kernel,
        out_shape=jax.ShapeDtypeStruct((devices,) + held.shape[1:], held.dtype),
        in_specs=[SMEM, HBM],
        out_specs=HBM,
        scratch_shapes=[
            pltpu.VMEM(held.shape, held.dtype),
            pltpu.SemaphoreType.DMA((2, held.shape[0])),
        ],
        name="pack_right",
    )(dest, held)


def pack_left(held, dest, devices):
    copies = dest.shape[0]
    count, rows, cols = held.shape
    return pl.pallas_call(
        functools.partial(pack_left_kernel, copies),
        out_shape=jax.ShapeDtypeStruct((devices, rows // copies, cols), held.dtype),
        in_specs=[SMEM, HBM],
        out_specs=HBM,
        scratch_shapes=[
            pltpu.VMEM(held.shape, held.dtype),
            pltpu.SemaphoreType.DMA((1 + copies, count)),
        ],
        name="pack_left",
    )(dest, held)


def collect(recv, source):
    return pl.pallas_call(
        collect_kernel,
        out_shape=jax.ShapeDtypeStruct(source.shape + recv.shape[1:], recv.dtype),
        in_specs=[SMEM, HBM],
        out_specs=HBM,
        scratch_shapes=[
            pltpu.VMEM(source.shape + recv.shape[1:], recv.dtype),
            pltpu.SemaphoreType.DMA((2,) + source.shape),
        ],
        name="collect",
    )(source, recv)


def split(value):
    high = value.astype(jnp.bfloat16)
    low = (value - high.astype(jnp.float32)).astype(jnp.bfloat16)
    return high, low


def product_kernel(steps, width, index, order, *refs):
    halves = refs[: 2 * steps]
    rights = refs[2 * steps : 3 * steps]
    out = refs[3 * steps]
    buf, high, low, sems = refs[3 * steps + 1 :]
    row = pl.program_id(0)
    slots = rights[0].shape[0]
    edge = out.shape[-1]
    group = buf.shape[1]
    chunks = steps * slots // group

    @pl.when(row == 0)
    def _():
        per = slots // group

        def copy(at):
            return pltpu.make_async_copy(
                rights[at // per].at[pl.ds((at % per) * group, group)], buf.at[at % 2], sems.at[at % 2]
            )

        copy(0).start()
        for at in range(chunks):
            if at + 1 < chunks:
                copy(at + 1).start()
            copy(at).wait()
            step, first = at // per, (at % per) * group

            def body(slot):
                hi, lo = split(buf[at % 2, slot])
                high[step * (slots + 1) + first + slot] = hi
                low[step * (slots + 1) + first + slot] = lo

            pl.loop(0, group)(body)
        for step in range(steps):
            high[step * (slots + 1) + slots] = jnp.zeros((edge, edge), jnp.bfloat16)
            low[step * (slots + 1) + slots] = jnp.zeros((edge, edge), jnp.bfloat16)

    for kept in range(width):
        out[0, kept] = jnp.zeros((edge, edge), jnp.float32)
    for step in range(steps):
        swap = order[step]
        for slot in range(WA):
            first, second = halves[2 * step][slot], halves[2 * step + 1][slot]
            left = jnp.concatenate(
                [jnp.where(swap > 0, second, first), jnp.where(swap > 0, first, second)], axis=0
            )
            a_hi, a_lo = split(left)
            both = jnp.concatenate([a_hi, a_lo], axis=1)
            for kept in range(width):
                at = index[((row * steps + step) * WA + slot) * width + kept]
                b_hi = high[at]
                b_lo = low[at]
                out[0, kept] += jnp.dot(
                    both, jnp.concatenate([b_hi, b_hi], axis=0), preferred_element_type=jnp.float32
                ) + jnp.dot(a_hi, b_lo, preferred_element_type=jnp.float32)


def products(index, order, halves, rights, rows, width):
    steps = len(rights)
    slots, edge, _ = rights[0].shape
    part = halves[0].shape[1]
    group = 16
    left_spec = pl.BlockSpec((WA, part, edge), lambda row, *_: (row, 0, 0))
    return pl.pallas_call(
        functools.partial(product_kernel, steps, width),
        grid_spec=pltpu.PrefetchScalarGridSpec(
            num_scalar_prefetch=2,
            grid=(rows,),
            in_specs=[left_spec] * len(halves) + [HBM] * steps,
            out_specs=pl.BlockSpec((1, width, edge, edge), lambda row, *_: (row, 0, 0, 0)),
            scratch_shapes=[
                pltpu.VMEM((2, group, edge, edge), jnp.float32),
                pltpu.VMEM((steps * (slots + 1), edge, edge), jnp.bfloat16),
                pltpu.VMEM((steps * (slots + 1), edge, edge), jnp.bfloat16),
                pltpu.SemaphoreType.DMA((2,)),
            ],
        ),
        out_shape=jax.ShapeDtypeStruct((rows, width, edge, edge), jnp.float32),
        compiler_params=pltpu.CompilerParams(
            dimension_semantics=("arbitrary",), vmem_limit_bytes=40 * 1024 * 1024
        ),
        name="products",
    )(index, order, *halves, *rights)


def on_device(a_held, a_slot, a_col, b_held, b_slot, b_col, c_col):
    grid_rows = lax.axis_size("row")
    grid_cols = lax.axis_size("col")
    devices = grid_rows * grid_cols
    copies = grid_cols // grid_rows
    i = lax.axis_index("row")
    c = lax.axis_index("col")
    rows, width = c_col.shape
    hold_a, hold_b = a_slot.shape[0], b_slot.shape[0]
    slots_a, slots_b = rows * WA, KPB * WB

    panel = a_slot // slots_a
    at_row, inner = panel // grid_rows, panel % grid_rows
    dest = at_row * grid_cols + (inner - at_row - 1) % grid_rows
    dest_left = dest[None, :] + grid_rows * jnp.arange(copies, dtype=jnp.int32)[:, None]
    panel = b_slot // slots_b
    inner, at_col = panel // grid_cols, panel % grid_cols
    dest_right = ((inner - at_col - 1) % grid_rows) * grid_cols + at_col

    labels = jnp.concatenate([a_slot, a_col, b_slot, b_col])
    labels = jnp.broadcast_to(labels[None, :], (devices,) + labels.shape)
    labels = lax.all_to_all(labels, ("row", "col"), split_axis=0, concat_axis=0, tiled=True)
    parts = [hold_a, 2 * hold_a, 2 * hold_a + hold_b]
    all_a, all_acol, all_b, all_bcol = (part.reshape(-1) for part in jnp.split(labels, parts, axis=1))

    side = 2 * (c % 2) - 1
    turns = jnp.stack([jnp.int32(1), 1 - side, 1 + side])
    k = (i + c + turns) % grid_rows

    def look_up(panels, slots, table, columns, hold):
        wanted = panels[:, None] * slots + jnp.arange(slots, dtype=jnp.int32)[None, :]
        holder = jnp.arange(table.shape[0], dtype=jnp.int32) // hold
        code = holder * 32 + columns + 1
        found = jnp.sum(jnp.where(table[None, None, :] == wanted[:, :, None], code, 0), axis=2)
        return found // 32, found % 32 - 1

    src_left, col_left = look_up(i * grid_rows + k, slots_a, all_a, all_acol, hold_a)
    src_right, col_right = look_up(k * grid_cols + c, slots_b, all_b, all_bcol, hold_b)

    u = jnp.arange(slots_b, dtype=jnp.int32)
    lefts = col_left.reshape(STEPS, rows, WA).transpose(1, 0, 2)[:, :, :, None, None]
    hit = (
        (lefts == (u // WB))
        & (col_right[None, :, None, None, :] == c_col[:, None, None, :, None])
        & (c_col >= 0)[:, None, None, :, None]
    )
    index = slots_b - jnp.sum(jnp.where(hit, slots_b - u, 0), axis=4)
    place = jnp.stack([jnp.int32(0), 1 + (1 - side) // 2, 1 + (1 + side) // 2])
    index = (index + (place * (slots_b + 1))[None, :, None, None]).reshape(-1).astype(jnp.int32)

    send_left = pack_left(a_held, dest_left, devices)
    send_right = pack_right(b_held, dest_right, devices)
    recv_left = lax.all_to_all(send_left, ("row", "col"), split_axis=0, concat_axis=0, tiled=True)
    recv_right = lax.all_to_all(send_right, ("row", "col"), split_axis=0, concat_axis=0, tiled=True)

    own = collect(recv_left, src_left[0])
    right = collect(recv_right, src_right[0])
    other = shifted(own, "col", grid_rows)
    cross = permuted(own, "col", lambda at: ((at - 1) ^ 1) + 1)
    halves = [
        own,
        other,
        permuted(own, "col", lambda at: at ^ 1),
        permuted(other, "col", lambda at: at ^ 1),
        cross,
        shifted(cross, "col", grid_rows),
    ]
    rights = [right, shifted(right, "row", 1), shifted(right, "row", -1)]
    homes = (c + jnp.stack([jnp.int32(0), -side, side])) % grid_cols
    order = (homes >= grid_rows).astype(jnp.int32)
    return products(index, order, halves, rights, rows, width)


def solution(mesh):
    return jax.shard_map(
        on_device,
        mesh=mesh,
        in_specs=(
            P(("row", "col"), None, None),
            P(("row", "col")),
            P(("row", "col")),
            P(("row", "col"), None, None),
            P(("row", "col")),
            P(("row", "col")),
            P("row", "col"),
        ),
        out_specs=P("row", "col", None, None),
        check_vma=False,
    )
```

```python
import functools

import jax
import jax.numpy as jnp
from jax import lax
from jax.experimental import pallas as pl
from jax.experimental.pallas import tpu as pltpu
from jax.sharding import PartitionSpec as P

KPB = 16
WA = 4
WB = 4
STEPS = 3
HBM = pl.BlockSpec(memory_space=pl.ANY)


def shifted(value, axis, steps):
    count = lax.axis_size(axis)
    pairs = [(source, (source + steps) % count) for source in range(count)]
    return lax.ppermute(value, axis, pairs)


def permuted(value, axis, target):
    count = lax.axis_size(axis)
    return lax.ppermute(value, axis, [(at, target(at) % count) for at in range(count)])


def relay(count, load, store):
    pl.loop(0, count)(lambda at: load(at).start())

    def body(at):
        load(at).wait()
        store(at)

    pl.loop(0, count)(body)


def pack_right_kernel(dest, held, out, buf, sems):
    count = held.shape[0]

    def load(at):
        return pltpu.make_async_copy(held.at[at], buf.at[at], sems.at[0, at])

    def save(at):
        return pltpu.make_async_copy(buf.at[at], out.at[dest[at]], sems.at[1, at])

    relay(count, load, lambda at: save(at).start())
    pl.loop(0, count)(lambda at: save(at).wait())


def pack_left_kernel(copies, part, dest, held, labels, out, buf, sems, mark_sems):
    count = held.shape[0]
    devices = out.shape[0]

    def mark(at):
        return pltpu.make_async_copy(labels, out.at[at, pl.ds(part, 8)], mark_sems.at[at])

    def load(at):
        return pltpu.make_async_copy(held.at[at], buf.at[at], sems.at[0, at])

    def save(at, half):
        return pltpu.make_async_copy(
            buf.at[at, pl.ds(half * part, part)],
            out.at[dest[half, at], pl.ds(0, part)],
            sems.at[1 + half, at],
        )

    def store(at):
        for half in range(copies):
            save(at, half).start()

    relay(count, load, store)
    pl.loop(0, devices)(lambda at: mark(at).start())
    for half in range(copies):
        pl.loop(0, count)(lambda at: save(at, half).wait())
    pl.loop(0, devices)(lambda at: mark(at).wait())


def collect_kernel(source, recv, *refs):
    buf, sems = refs[-2:]
    count, rows, _ = buf.shape
    outs = refs[:-2]
    chunk = count // len(outs)

    def load(at):
        return pltpu.make_async_copy(
            recv.at[source[at], pl.ds(0, rows)], buf.at[at], sems.at[at]
        )

    pl.loop(0, count)(lambda at: load(at).start())
    saves = [
        pltpu.make_async_copy(buf.at[pl.ds(part * chunk, chunk)], out, sems.at[count + part])
        for part, out in enumerate(outs)
    ]
    for part, save in enumerate(saves):
        pl.loop(part * chunk, (part + 1) * chunk)(lambda at: load(at).wait())
        save.start()
    for save in saves:
        save.wait()


SMEM = pl.BlockSpec(memory_space=pltpu.SMEM)


def pack_right(held, dest, devices):
    return pl.pallas_call(
        pack_right_kernel,
        out_shape=jax.ShapeDtypeStruct((devices,) + held.shape[1:], held.dtype),
        in_specs=[SMEM, HBM],
        out_specs=HBM,
        scratch_shapes=[
            pltpu.VMEM(held.shape, held.dtype),
            pltpu.SemaphoreType.DMA((2, held.shape[0])),
        ],
        name="pack_right",
    )(dest, held)


def pack_left(held, dest, labels, devices):
    copies = dest.shape[0]
    count, rows, cols = held.shape
    part = rows // copies
    return pl.pallas_call(
        functools.partial(pack_left_kernel, copies, part),
        out_shape=jax.ShapeDtypeStruct((devices, part + 8, cols), held.dtype),
        in_specs=[SMEM, HBM, pl.BlockSpec(memory_space=pltpu.VMEM)],
        out_specs=HBM,
        scratch_shapes=[
            pltpu.VMEM(held.shape, held.dtype),
            pltpu.SemaphoreType.DMA((1 + copies, count)),
            pltpu.SemaphoreType.DMA((devices,)),
        ],
        name="pack_left",
    )(dest, held, labels)


def collect(recv, source, rows, chunks):
    count, cols = source.shape[0], recv.shape[2]
    part = jax.ShapeDtypeStruct((count // chunks, rows, cols), recv.dtype)
    return pl.pallas_call(
        collect_kernel,
        out_shape=[part] * chunks,
        in_specs=[SMEM, HBM],
        out_specs=[HBM] * chunks,
        scratch_shapes=[
            pltpu.VMEM((count, rows, cols), recv.dtype),
            pltpu.SemaphoreType.DMA((count + chunks,)),
        ],
        name="collect",
    )(source, recv)


def split(value):
    high = value.astype(jnp.bfloat16)
    low = (value - high.astype(jnp.float32)).astype(jnp.bfloat16)
    return high, low


def product_kernel(pieces, parts, first, unroll, counts, items, order, *refs):
    lefts = refs[: 2 * pieces]
    rights = refs[2 * pieces : 2 * pieces + parts]
    refs = refs[2 * pieces + parts :]
    if not first:
        before, refs = refs[0], refs[1:]
    out, left_buf, right_buf, total, load_sems, out_sem = refs
    outs, edge, _ = out.shape
    slots_a = lefts[0].shape[0]
    slots_b = rights[0].shape[0]

    loads = [
        pltpu.make_async_copy(source, left_buf.at[at], load_sems.at[at])
        for at, source in enumerate(lefts)
    ] + [
        pltpu.make_async_copy(
            source, right_buf.at[pl.ds(at * slots_b, slots_b)], load_sems.at[2 * pieces + at]
        )
        for at, source in enumerate(rights)
    ]
    if not first:
        restore = pltpu.make_async_copy(before, total.at[pl.ds(0, outs)], out_sem)
        restore.start()
    for load in loads:
        load.start()
    if first:

        def clear(at):
            total[at] = jnp.zeros((edge, edge), jnp.float32)

        pl.loop(0, outs)(clear)
    else:
        restore.wait()
    for load in loads:
        load.wait()

    def step(at):
        codes = [items[at * unroll + lane] for lane in range(unroll)]
        sums = []
        for code in codes:
            slot_a = code // 16384
            slot_b = (code // 128) % 128
            piece = slot_a // slots_a
            swap = order[piece]
            slot_a = slot_a % slots_a
            left = jnp.concatenate(
                [
                    left_buf[2 * piece + swap, slot_a],
                    left_buf[2 * piece + 1 - swap, slot_a],
                ],
                axis=0,
            )
            a_hi, a_lo = split(left)
            b_hi, b_lo = split(right_buf[slot_b])
            sums.append(
                jnp.dot(
                    jnp.concatenate([a_hi, a_lo], axis=1),
                    jnp.concatenate([b_hi, b_hi], axis=0),
                    preferred_element_type=jnp.float32,
                )
                + jnp.dot(a_hi, b_lo, preferred_element_type=jnp.float32)
            )
        for code, value in zip(codes, sums):
            total[code % 128] += value

    pl.loop(0, counts[0])(step)
    save = pltpu.make_async_copy(total.at[pl.ds(0, outs)], out, out_sem)
    save.start()
    save.wait()


UNROLL = 8
CHUNKS = 2


def products(counts, items, order, halves, rights, before, outs):
    pieces, parts = len(halves) // 2, len(rights)
    slots_b, edge, _ = rights[0].shape
    slots_a, part, _ = halves[0].shape
    first = before is None
    extra = [] if first else [before]
    return pl.pallas_call(
        functools.partial(product_kernel, pieces, parts, first, UNROLL),
        out_shape=jax.ShapeDtypeStruct((outs, edge, edge), jnp.float32),
        in_specs=[SMEM] * 3 + [HBM] * (2 * pieces + parts + len(extra)),
        out_specs=HBM,
        scratch_shapes=[
            pltpu.VMEM((2 * pieces, slots_a, part, edge), jnp.float32),
            pltpu.VMEM((parts * slots_b, edge, edge), jnp.float32),
            pltpu.VMEM((outs + 1, edge, edge), jnp.float32),
            pltpu.SemaphoreType.DMA((2 * pieces + parts,)),
            pltpu.SemaphoreType.DMA,
        ],
        compiler_params=pltpu.CompilerParams(vmem_limit_bytes=40 * 1024 * 1024),
        cost_estimate=pl.CostEstimate(
            flops=pieces * 600_000_000, bytes_accessed=pieces * 8_000_000, transcendentals=0
        ),
        name="products",
    )(counts, items, order, *halves, *rights, *extra)


def work_list(lefts, rights, places, kept, first_row):
    rows, width = kept.shape
    pieces, inner, _ = rights.shape
    outs = rows * width
    slots = rows * WA
    rel = lefts - first_row
    here = rel[:, :, None] == jnp.arange(inner, dtype=jnp.int32)
    chosen = (
        jnp.sum(jnp.where(here[:, :, :, None], rights[:, None, :, :] + 1, 0), axis=2) - 1
    )
    at_row = jnp.repeat(kept, WA, axis=0)
    match = (chosen[:, :, :, None] == at_row[None, :, None, :]) & (chosen >= 0)[:, :, :, None]
    target = jnp.sum(jnp.where(match, jnp.arange(width, dtype=jnp.int32) + 1, 0), axis=3) - 1
    live = target >= 0
    slot = jnp.arange(slots, dtype=jnp.int32)[None, :, None]
    slot_a = slot + slots * jnp.arange(pieces, dtype=jnp.int32)[:, None, None]
    slot_b = (places[:, None, None] * inner + rel[:, :, None]) * WB + jnp.arange(WB, dtype=jnp.int32)
    code = slot_a * 16384 + slot_b * 128 + slot // WA * width + target
    live, code = live.reshape(-1), code.reshape(-1)
    spot = jnp.cumsum(live.astype(jnp.int32)) - 1
    place = jnp.arange(live.shape[0], dtype=jnp.int32)
    here = live[None, :] & (spot[None, :] == place[:, None])
    packed = jnp.sum(jnp.where(here, code[None, :] - outs, 0), axis=1) + outs
    count = (jnp.sum(live.astype(jnp.int32)) + UNROLL - 1) // UNROLL
    return count[None], packed


def on_device(a_held, a_slot, a_col, b_held, b_slot, b_col, c_col):
    grid_rows = lax.axis_size("row")
    grid_cols = lax.axis_size("col")
    devices = grid_rows * grid_cols
    copies = grid_cols // grid_rows
    i = lax.axis_index("row")
    c = lax.axis_index("col")
    rows, width = c_col.shape
    hold_a, hold_b = a_slot.shape[0], b_slot.shape[0]
    slots_a, slots_b = rows * WA, KPB * WB

    panel = a_slot // slots_a
    at_row, inner = panel // grid_rows, panel % grid_rows
    dest = at_row * grid_cols + (inner - at_row - 1) % grid_rows
    dest_left = dest[None, :] + grid_rows * jnp.arange(copies, dtype=jnp.int32)[:, None]
    panel = b_slot // slots_b
    inner, at_col = panel // grid_cols, panel % grid_cols
    dest_right = ((inner - at_col - 1) % grid_rows) * grid_cols + at_col

    edge = a_held.shape[1]
    labels = jnp.concatenate([a_slot, a_col, b_slot, b_col]).astype(jnp.float32)
    tile = jnp.pad(labels, (0, 8 * edge - labels.shape[0])).reshape(8, edge)
    send_left = pack_left(a_held, dest_left, tile, devices)
    send_right = pack_right(b_held, dest_right, devices)
    recv_left = lax.all_to_all(send_left, ("row", "col"), split_axis=0, concat_axis=0, tiled=True)
    recv_right = lax.all_to_all(send_right, ("row", "col"), split_axis=0, concat_axis=0, tiled=True)

    labels = recv_left[:, edge // copies :, :].reshape(devices, -1)[:, : labels.shape[0]]
    labels = labels.astype(jnp.int32)
    parts = [hold_a, 2 * hold_a, 2 * hold_a + hold_b]
    all_a, all_acol, all_b, all_bcol = (part.reshape(-1) for part in jnp.split(labels, parts, axis=1))

    side = 2 * (c % 2) - 1
    turns = jnp.stack([jnp.int32(1), 1 - side, 1 + side])
    k = (i + c + turns) % grid_rows

    def look_up(panels, slots, table, columns, hold):
        wanted = panels[:, None] * slots + jnp.arange(slots, dtype=jnp.int32)[None, :]
        holder = jnp.arange(table.shape[0], dtype=jnp.int32) // hold
        code = holder * 32 + columns + 1
        found = jnp.sum(jnp.where(table[None, None, :] == wanted[:, :, None], code, 0), axis=2)
        return found // 32, found % 32 - 1

    src_left, col_left = look_up(i * grid_rows + k, slots_a, all_a, all_acol, hold_a)
    src_right, col_right = look_up(k * grid_cols + c, slots_b, all_b, all_bcol, hold_b)

    (own,) = collect(recv_left, src_left[0], edge // copies, 1)
    right = collect(recv_right, src_right[0], edge, CHUNKS)
    other = shifted(own, "col", grid_rows)
    cross = permuted(own, "col", lambda at: ((at - 1) ^ 1) + 1)
    mate_first = permuted(own, "col", lambda at: at ^ 1)
    mate_second = permuted(other, "col", lambda at: at ^ 1)
    cross_second = shifted(cross, "col", grid_rows)
    homes = (c + jnp.stack([jnp.int32(0), -side, side])) % grid_cols
    order = (homes >= grid_rows).astype(jnp.int32)

    outs = rows * width
    tables = col_right.reshape(STEPS, KPB, WB)
    count, items = work_list(col_left[:1], tables[:1], jnp.zeros((1,), jnp.int32), c_col, 0)
    total = products(count, items, order[:1], [own, other], right, None, outs)
    places = jnp.stack([(1 - side) // 2, (1 + side) // 2])
    lefts = [mate_first, mate_second, cross, cross_second]
    chunk = slots_b // CHUNKS
    for at in range(CHUNKS):
        shifts = [shifted(right[at], "row", 1), shifted(right[at], "row", -1)]
        first, last = at * chunk // WB, (at + 1) * chunk // WB
        count, items = work_list(col_left[1:], tables[1:, first:last], places, c_col, first)
        total = products(count, items, order[1:], lefts, shifts, total, outs)
    return total.reshape(rows, width, edge, edge)


def solution(mesh):
    return jax.shard_map(
        on_device,
        mesh=mesh,
        in_specs=(
            P(("row", "col"), None, None),
            P(("row", "col")),
            P(("row", "col")),
            P(("row", "col"), None, None),
            P(("row", "col")),
            P(("row", "col")),
            P("row", "col"),
        ),
        out_specs=P("row", "col", None, None),
        check_vma=False,
    )
```

```python
import functools

import jax
import jax.numpy as jnp
from jax import lax
from jax.experimental import pallas as pl
from jax.experimental.pallas import tpu as pltpu
from jax.sharding import PartitionSpec as P

KPB = 16
WA = 4
WB = 4
STEPS = 3
HBM = pl.BlockSpec(memory_space=pl.ANY)


def shifted(value, axis, steps):
    count = lax.axis_size(axis)
    pairs = [(source, (source + steps) % count) for source in range(count)]
    return lax.ppermute(value, axis, pairs)


def permuted(value, axis, target):
    count = lax.axis_size(axis)
    return lax.ppermute(value, axis, [(at, target(at) % count) for at in range(count)])


def pack_kernel(pieces, dest, held, *refs):
    labels = refs[0] if len(refs) > 3 else None
    out, buf, sems = refs[-3:]
    count, rows, _ = held.shape
    devices = out.shape[0]
    part = rows // pieces

    def load(at):
        return pltpu.make_async_copy(held.at[at], buf.at[at], sems.at[at])

    def save(at, piece):
        return pltpu.make_async_copy(
            buf.at[at, pl.ds(piece * part, part)],
            out.at[dest[piece, at], pl.ds(0, part)],
            sems.at[(1 + piece) * count + at],
        )

    def mark(at):
        return pltpu.make_async_copy(
            labels, out.at[at, pl.ds(part, 8)], sems.at[(1 + pieces) * count + at]
        )

    pl.loop(0, count)(lambda at: load(at).start())
    if labels is not None:
        pl.loop(0, devices)(lambda at: mark(at).start())

    def body(at):
        load(at).wait()
        for piece in range(pieces):
            save(at, piece).start()

    pl.loop(0, count)(body)
    for piece in range(pieces):
        pl.loop(0, count)(lambda at: save(at, piece).wait())
    if labels is not None:
        pl.loop(0, devices)(lambda at: mark(at).wait())


def collect_kernel(source, recv, *refs):
    buf, sems = refs[-2:]
    count, rows, _ = buf.shape
    outs = refs[:-2]
    chunk = count // len(outs)

    def load(at):
        return pltpu.make_async_copy(
            recv.at[source[at], pl.ds(0, rows)], buf.at[at], sems.at[at]
        )

    pl.loop(0, count)(lambda at: load(at).start())
    saves = [
        pltpu.make_async_copy(buf.at[pl.ds(part * chunk, chunk)], out, sems.at[count + part])
        for part, out in enumerate(outs)
    ]
    for part, save in enumerate(saves):
        pl.loop(part * chunk, (part + 1) * chunk)(lambda at: load(at).wait())
        save.start()
    for save in saves:
        save.wait()


SMEM = pl.BlockSpec(memory_space=pltpu.SMEM)


def pack(held, dest, devices, labels=None):
    pieces = dest.shape[0]
    count, rows, cols = held.shape
    part = rows // pieces
    marks = [] if labels is None else [labels]
    return pl.pallas_call(
        functools.partial(pack_kernel, pieces),
        out_shape=jax.ShapeDtypeStruct((devices, part + 8 * len(marks), cols), held.dtype),
        in_specs=[SMEM, HBM] + [pl.BlockSpec(memory_space=pltpu.VMEM)] * len(marks),
        out_specs=HBM,
        scratch_shapes=[
            pltpu.VMEM(held.shape, held.dtype),
            pltpu.SemaphoreType.DMA(((1 + pieces) * count + devices,)),
        ],
        name="pack",
    )(dest, held, *marks)


def collect(recv, source, rows, chunks):
    count, cols = source.shape[0], recv.shape[2]
    part = jax.ShapeDtypeStruct((count // chunks, rows, cols), recv.dtype)
    return pl.pallas_call(
        collect_kernel,
        out_shape=[part] * chunks,
        in_specs=[SMEM, HBM],
        out_specs=[HBM] * chunks,
        scratch_shapes=[
            pltpu.VMEM((count, rows, cols), recv.dtype),
            pltpu.SemaphoreType.DMA((count + chunks,)),
        ],
        name="collect",
    )(source, recv)


def split(value):
    high = value.astype(jnp.bfloat16)
    low = (value - high.astype(jnp.float32)).astype(jnp.bfloat16)
    return high, low


def product_kernel(pieces, parts, first, unroll, counts, items, order, *refs):
    lefts = refs[: 2 * pieces]
    rights = refs[2 * pieces : 2 * pieces + parts]
    refs = refs[2 * pieces + parts :]
    if not first:
        before, refs = refs[0], refs[1:]
    out, left_buf, right_buf, total, load_sems, out_sem = refs
    outs, edge, _ = out.shape
    slots_a = lefts[0].shape[0]
    slots_b = rights[0].shape[0]

    loads = [
        pltpu.make_async_copy(source, left_buf.at[at], load_sems.at[at])
        for at, source in enumerate(lefts)
    ] + [
        pltpu.make_async_copy(
            source, right_buf.at[pl.ds(at * slots_b, slots_b)], load_sems.at[2 * pieces + at]
        )
        for at, source in enumerate(rights)
    ]
    if not first:
        restore = pltpu.make_async_copy(before, total.at[pl.ds(0, outs)], out_sem)
        restore.start()
    for load in loads:
        load.start()
    if first:

        def clear(at):
            total[at] = jnp.zeros((edge, edge), jnp.float32)

        pl.loop(0, outs)(clear)
    else:
        restore.wait()
    for load in loads:
        load.wait()

    def step(at):
        codes = [items[at * unroll + lane] for lane in range(unroll)]
        sums = []
        for code in codes:
            slot_a = code // 16384
            slot_b = (code // 128) % 128
            piece = slot_a // slots_a
            swap = order[piece]
            slot_a = slot_a % slots_a
            left = jnp.concatenate(
                [
                    left_buf[2 * piece + swap, slot_a],
                    left_buf[2 * piece + 1 - swap, slot_a],
                ],
                axis=0,
            )
            a_hi, a_lo = split(left)
            b_hi, b_lo = split(right_buf[slot_b])
            sums.append(
                jnp.dot(
                    jnp.concatenate([a_hi, a_lo], axis=1),
                    jnp.concatenate([b_hi, b_hi], axis=0),
                    preferred_element_type=jnp.float32,
                )
                + jnp.dot(a_hi, b_lo, preferred_element_type=jnp.float32)
            )
        for code, value in zip(codes, sums):
            total[code % 128] += value

    pl.loop(0, counts[0])(step)
    save = pltpu.make_async_copy(total.at[pl.ds(0, outs)], out, out_sem)
    save.start()
    save.wait()


UNROLL = 8
CHUNKS = 2


def products(counts, items, order, halves, rights, before, outs):
    pieces, parts = len(halves) // 2, len(rights)
    slots_b, edge, _ = rights[0].shape
    slots_a, part, _ = halves[0].shape
    first = before is None
    extra = [] if first else [before]
    return pl.pallas_call(
        functools.partial(product_kernel, pieces, parts, first, UNROLL),
        out_shape=jax.ShapeDtypeStruct((outs, edge, edge), jnp.float32),
        in_specs=[SMEM] * 3 + [HBM] * (2 * pieces + parts + len(extra)),
        out_specs=HBM,
        scratch_shapes=[
            pltpu.VMEM((2 * pieces, slots_a, part, edge), jnp.float32),
            pltpu.VMEM((parts * slots_b, edge, edge), jnp.float32),
            pltpu.VMEM((outs + 1, edge, edge), jnp.float32),
            pltpu.SemaphoreType.DMA((2 * pieces + parts,)),
            pltpu.SemaphoreType.DMA,
        ],
        compiler_params=pltpu.CompilerParams(vmem_limit_bytes=40 * 1024 * 1024),
        cost_estimate=pl.CostEstimate(
            flops=pieces * 600_000_000, bytes_accessed=pieces * 8_000_000, transcendentals=0
        ),
        name="products",
    )(counts, items, order, *halves, *rights, *extra)


def work_list(lefts, rights, places, kept, first_row):
    rows, width = kept.shape
    pieces, inner, _ = rights.shape
    outs = rows * width
    slots = rows * WA
    rel = lefts - first_row
    here = rel[:, :, None] == jnp.arange(inner, dtype=jnp.int32)
    chosen = (
        jnp.sum(jnp.where(here[:, :, :, None], rights[:, None, :, :] + 1, 0), axis=2) - 1
    )
    at_row = jnp.repeat(kept, WA, axis=0)
    match = (chosen[:, :, :, None] == at_row[None, :, None, :]) & (chosen >= 0)[:, :, :, None]
    target = jnp.sum(jnp.where(match, jnp.arange(width, dtype=jnp.int32) + 1, 0), axis=3) - 1
    live = target >= 0
    slot = jnp.arange(slots, dtype=jnp.int32)[None, :, None]
    slot_a = slot + slots * jnp.arange(pieces, dtype=jnp.int32)[:, None, None]
    slot_b = (places[:, None, None] * inner + rel[:, :, None]) * WB + jnp.arange(WB, dtype=jnp.int32)
    code = slot_a * 16384 + slot_b * 128 + slot // WA * width + target
    live, code = live.reshape(-1), code.reshape(-1)
    spot = jnp.cumsum(live.astype(jnp.int32)) - 1
    place = jnp.arange(live.shape[0], dtype=jnp.int32)
    here = live[None, :] & (spot[None, :] == place[:, None])
    packed = jnp.sum(jnp.where(here, code[None, :] - outs, 0), axis=1) + outs
    count = (jnp.sum(live.astype(jnp.int32)) + UNROLL - 1) // UNROLL
    return count[None], packed


def on_device(a_held, a_slot, a_col, b_held, b_slot, b_col, c_col):
    grid_rows = lax.axis_size("row")
    grid_cols = lax.axis_size("col")
    devices = grid_rows * grid_cols
    copies = grid_cols // grid_rows
    i = lax.axis_index("row")
    c = lax.axis_index("col")
    rows, width = c_col.shape
    hold_a, hold_b = a_slot.shape[0], b_slot.shape[0]
    slots_a, slots_b = rows * WA, KPB * WB

    panel = a_slot // slots_a
    at_row, inner = panel // grid_rows, panel % grid_rows
    dest = at_row * grid_cols + (inner - at_row - 1) % grid_rows
    dest_left = dest[None, :] + grid_rows * jnp.arange(copies, dtype=jnp.int32)[:, None]
    panel = b_slot // slots_b
    inner, at_col = panel // grid_cols, panel % grid_cols
    dest_right = ((inner - at_col - 1) % grid_rows) * grid_cols + at_col

    edge = a_held.shape[1]
    labels = jnp.concatenate([a_slot, a_col, b_slot, b_col]).astype(jnp.float32)
    tile = jnp.pad(labels, (0, 8 * edge - labels.shape[0])).reshape(8, edge)
    send_right = pack(b_held, dest_right[None, :], devices, tile)
    send_left = pack(a_held, dest_left, devices)
    recv_right = lax.all_to_all(send_right, ("row", "col"), split_axis=0, concat_axis=0, tiled=True)
    recv_right, send_left = lax.optimization_barrier((recv_right, send_left))
    recv_left = lax.all_to_all(send_left, ("row", "col"), split_axis=0, concat_axis=0, tiled=True)

    labels = recv_right[:, edge:, :].reshape(devices, -1)[:, : labels.shape[0]]
    labels = labels.astype(jnp.int32)
    parts = [hold_a, 2 * hold_a, 2 * hold_a + hold_b]
    all_a, all_acol, all_b, all_bcol = (part.reshape(-1) for part in jnp.split(labels, parts, axis=1))

    side = 2 * (c % 2) - 1
    turns = jnp.stack([jnp.int32(1), 1 - side, 1 + side])
    k = (i + c + turns) % grid_rows

    def look_up(panels, slots, table, columns, hold):
        wanted = panels[:, None] * slots + jnp.arange(slots, dtype=jnp.int32)[None, :]
        holder = jnp.arange(table.shape[0], dtype=jnp.int32) // hold
        code = holder * 32 + columns + 1
        found = jnp.sum(jnp.where(table[None, None, :] == wanted[:, :, None], code, 0), axis=2)
        return found // 32, found % 32 - 1

    src_left, col_left = look_up(i * grid_rows + k, slots_a, all_a, all_acol, hold_a)
    src_right, col_right = look_up(k * grid_cols + c, slots_b, all_b, all_bcol, hold_b)

    (own,) = collect(recv_left, src_left[0], edge // copies, 1)
    right = collect(recv_right, src_right[0], edge, CHUNKS)
    other = shifted(own, "col", grid_rows)
    cross = permuted(own, "col", lambda at: ((at - 1) ^ 1) + 1)
    mate_first = permuted(own, "col", lambda at: at ^ 1)
    mate_second = permuted(other, "col", lambda at: at ^ 1)
    cross_second = shifted(cross, "col", grid_rows)
    homes = (c + jnp.stack([jnp.int32(0), -side, side])) % grid_cols
    order = (homes >= grid_rows).astype(jnp.int32)

    outs = rows * width
    tables = col_right.reshape(STEPS, KPB, WB)
    count, items = work_list(col_left[:1], tables[:1], jnp.zeros((1,), jnp.int32), c_col, 0)
    total = products(count, items, order[:1], [own, other], right, None, outs)
    places = jnp.stack([(1 - side) // 2, (1 + side) // 2])
    lefts = [mate_first, mate_second, cross, cross_second]
    chunk = slots_b // CHUNKS
    for at in range(CHUNKS):
        shifts = [shifted(right[at], "row", 1), shifted(right[at], "row", -1)]
        first, last = at * chunk // WB, (at + 1) * chunk // WB
        count, items = work_list(col_left[1:], tables[1:, first:last], places, c_col, first)
        total = products(count, items, order[1:], lefts, shifts, total, outs)
    return total.reshape(rows, width, edge, edge)


def solution(mesh):
    return jax.shard_map(
        on_device,
        mesh=mesh,
        in_specs=(
            P(("row", "col"), None, None),
            P(("row", "col")),
            P(("row", "col")),
            P(("row", "col"), None, None),
            P(("row", "col")),
            P(("row", "col")),
            P("row", "col"),
        ),
        out_specs=P("row", "col", None, None),
        check_vma=False,
    )
```

```python
import functools

import jax
import jax.numpy as jnp
from jax import lax
from jax.experimental import pallas as pl
from jax.experimental.pallas import tpu as pltpu
from jax.sharding import PartitionSpec as P

KPB = 16
WA = 4
WB = 4
STEPS = 3
HBM = pl.BlockSpec(memory_space=pl.ANY)


def shifted(value, axis, steps):
    count = lax.axis_size(axis)
    pairs = [(source, (source + steps) % count) for source in range(count)]
    return lax.ppermute(value, axis, pairs)


def permuted(value, axis, target):
    count = lax.axis_size(axis)
    return lax.ppermute(value, axis, [(at, target(at) % count) for at in range(count)])


def pack_kernel(pieces, dest, held, *refs):
    outs, buf, sems = refs[:-2], refs[-2], refs[-1]
    count, rows, _ = held.shape
    part = rows // pieces

    def load(at):
        return pltpu.make_async_copy(held.at[at], buf.at[at], sems.at[at])

    def save(at, piece):
        return pltpu.make_async_copy(
            buf.at[at, pl.ds(piece * part, part)],
            outs[piece % len(outs)].at[dest[piece, at]],
            sems.at[(1 + piece) * count + at],
        )

    pl.loop(0, count)(lambda at: load(at).start())

    def body(at):
        load(at).wait()
        for piece in range(pieces):
            save(at, piece).start()

    pl.loop(0, count)(body)
    for piece in range(pieces):
        pl.loop(0, count)(lambda at: save(at, piece).wait())


SMEM = pl.BlockSpec(memory_space=pltpu.SMEM)
VMEM = pl.BlockSpec(memory_space=pltpu.VMEM)


def pack(held, dest, devices, outs):
    pieces = dest.shape[0]
    count, rows, cols = held.shape
    shape = jax.ShapeDtypeStruct((devices, rows // pieces, cols), held.dtype)
    return pl.pallas_call(
        functools.partial(pack_kernel, pieces),
        out_shape=[shape] * outs,
        in_specs=[SMEM, HBM],
        out_specs=[HBM] * outs,
        scratch_shapes=[
            pltpu.VMEM(held.shape, held.dtype),
            pltpu.SemaphoreType.DMA(((1 + pieces) * count,)),
        ],
        name="pack",
    )(dest, held)


ORDERS = (("x", "y", "z"), ("y", "z", "x"), ("z", "x", "y"))
STEPS_FIRST = (1, 2, 6, 3, 7, 4, 5)
STEPS_LATER = (1, 3, 2)
RING = 4
CORES = 2


def my_place():
    row, col = lax.axis_index("row"), lax.axis_index("col")
    return {
        "x": row // RING * 2 + col // CORES % 2,
        "y": col // RING,
        "z": row % RING,
        "core": col % CORES,
    }


def coords_of(place):
    row = place["x"] // 2 * RING + place["z"]
    col = place["y"] * RING + place["x"] % 2 * CORES + place["core"]
    return row, col


def exchange_kernel(*refs):
    parts = len(ORDERS)
    sends, refs = refs[:parts], refs[parts:]
    tile, refs = refs[0], refs[1:]
    stages = [refs[3 * part : 3 * part + 3] for part in range(parts)]
    labels = refs[3 * parts]
    first_recv, second_recv, third_recv, send_sems, label_send, label_recv = refs[3 * parts + 1 :]
    place = my_place()

    def moved(axis, steps, flip):
        there = dict(place)
        there[axis] = (place[axis] + steps) % RING
        there["core"] = (place["core"] + flip) % CORES
        return there

    def copy(source, target, send_sem, recv_sem, there):
        return pltpu.make_async_remote_copy(
            src_ref=source,
            dst_ref=target,
            send_sem=send_sem,
            recv_sem=recv_sem,
            device_id=coords_of(there),
            device_id_type=pl.DeviceIdType.MESH,
        )

    def spot(there, axis):
        return there[axis] * CORES + there["core"]

    def arrived(like, sem):
        pltpu.make_async_copy(like, like, sem).wait()

    peers = [moved("x", 0, 1)]
    for axis in ("x", "y", "z"):
        for steps in range(1, RING):
            for flip in range(CORES):
                peers.append(moved(axis, steps, flip))
    barrier = pltpu.get_barrier_semaphore()
    for there in peers:
        pl.semaphore_signal(
            barrier, inc=1, device_id=coords_of(there), device_id_type=pl.DeviceIdType.MESH
        )
    pl.semaphore_wait(barrier, len(peers))

    x, y, z = spot(place, "x"), place["y"], place["z"]
    labels[z, y, x] = tile[...]
    for steps in STEPS_FIRST:
        copy(
            labels.at[z, y, x],
            labels.at[z, y, x],
            label_send.at[0],
            label_recv.at[0],
            moved("x", steps // CORES, steps % CORES),
        ).start()
    for steps in STEPS_FIRST:
        for part, (one, two, three) in enumerate(ORDERS):
            there = moved(one, steps // CORES, steps % CORES)
            copy(
                sends[part].at[spot(there, one)],
                stages[part][0].at[spot(place, one)],
                send_sems.at[part, 0],
                first_recv.at[part, steps],
                there,
            ).start()
    arrived(labels.at[0, 0, pl.ds(0, 7)], label_recv.at[0])
    for steps in STEPS_LATER:
        copy(
            labels.at[z, y], labels.at[z, y], label_send.at[1], label_recv.at[1], moved("y", steps, 0)
        ).start()
    arrived(labels.at[0, pl.ds(0, 3)], label_recv.at[1])
    for steps in STEPS_LATER:
        copy(
            labels.at[z], labels.at[z], label_send.at[2], label_recv.at[2], moved("z", steps, 0)
        ).start()

    for steps in (0,) + STEPS_FIRST:
        for part, (one, two, three) in enumerate(ORDERS):
            origin = spot(moved(one, RING - steps // CORES, steps % CORES), one)
            if steps:
                source = stages[part][0]
                arrived(source.at[0], first_recv.at[part, steps])
            else:
                source = sends[part]
            for later in STEPS_LATER:
                there = moved(two, later, 0)
                copy(
                    source.at[origin, there[two]],
                    stages[part][1].at[place[two], origin],
                    send_sems.at[part, 1],
                    second_recv.at[part, later],
                    there,
                ).start()

    def last(part, source, target, there):
        copy(source, target, send_sems.at[part, 2], third_recv.at[part], there).start()

    for part, (one, two, three) in enumerate(ORDERS):
        for steps in (0,) + STEPS_FIRST:
            origin = spot(moved(one, RING - steps // CORES, steps % CORES), one)
            source = stages[part][0] if steps else sends[part]
            for later in STEPS_LATER:
                there = moved(three, later, 0)
                last(
                    part,
                    source.at[origin, place[two], there[three]],
                    stages[part][2].at[place[three], place[two], origin],
                    there,
                )
    for steps in STEPS_LATER:
        for part, (one, two, three) in enumerate(ORDERS):
            origin = moved(two, RING - steps, 0)[two]
            arrived(stages[part][1].at[0], second_recv.at[part, steps])
            for later in STEPS_LATER:
                there = moved(three, later, 0)
                last(
                    part,
                    stages[part][1].at[origin, :, there[three]],
                    stages[part][2].at[place[three], origin],
                    there,
                )
    for part in range(parts):
        arrived(stages[part][2].at[pl.ds(0, 3)], third_recv.at[part])
        arrived(sends[part].at[pl.ds(0, 7)], send_sems.at[part, 0])
        arrived(stages[part][2].at[pl.ds(0, 3)], send_sems.at[part, 1])
        arrived(stages[part][2].at[pl.ds(0, 3)], send_sems.at[part, 2])
    arrived(labels.at[pl.ds(0, 3)], label_recv.at[2])
    arrived(labels.at[0, 0, pl.ds(0, 7)], label_send.at[0])
    arrived(labels.at[0, pl.ds(0, 3)], label_send.at[1])
    arrived(labels.at[pl.ds(0, 3)], label_send.at[2])


def exchange(sends, tile):
    parts = len(sends)
    _, rows, cols = sends[0].shape
    kind = sends[0].dtype
    block = (rows, cols)
    eight = RING * CORES
    shapes = [
        (eight, RING, RING) + block,
        (RING, eight, RING) + block,
        (RING, RING, eight) + block,
    ]
    outs = pl.pallas_call(
        exchange_kernel,
        out_shape=[jax.ShapeDtypeStruct(shape, kind) for shape in shapes] * parts
        + [jax.ShapeDtypeStruct((RING, RING, eight) + tile.shape, tile.dtype)],
        in_specs=[HBM] * parts + [VMEM],
        out_specs=[HBM] * (3 * parts) + [VMEM],
        scratch_shapes=[
            pltpu.SemaphoreType.DMA((parts, eight)),
            pltpu.SemaphoreType.DMA((parts, RING)),
            pltpu.SemaphoreType.DMA((parts,)),
            pltpu.SemaphoreType.DMA((parts, 3)),
            pltpu.SemaphoreType.DMA((3,)),
            pltpu.SemaphoreType.DMA((3,)),
        ],
        compiler_params=pltpu.CompilerParams(
            collective_id=0, has_side_effects=True, vmem_limit_bytes=40 * 1024 * 1024
        ),
        name="exchange",
    )(*(send.reshape((eight, RING, RING) + block) for send in sends), tile)
    flat = [out.reshape((-1,) + block) for out in outs[: 3 * parts]]
    groups = [
        [sends[part]] + flat[3 * part : 3 * part + 3] for part in range(parts)
    ]
    return groups, outs[-1]


def place_in_send(place, order):
    one, two, three = (place[axis] for axis in order)
    return ((one * CORES + place["core"]) * RING + two) * RING + three


def place_received(origin, here, order):
    one, two, three = ((origin[axis], here[axis]) for axis in order)
    first = one[0] * CORES + origin["core"]
    same_first = (one[0] == one[1]) & (origin["core"] == here["core"])
    same_two, same_three = two[0] == two[1], three[0] == three[1]
    early = (first * RING + two[0]) * RING + three[0]
    middle = (two[0] * RING * CORES + first) * RING + three[0]
    late = (three[0] * RING + two[0]) * RING * CORES + first
    buffer = jnp.where(
        same_three, jnp.where(same_two, jnp.where(same_first, 0, 1), 2), 3
    )
    at = jnp.where(buffer == 3, late, jnp.where(buffer == 2, middle, early))
    return buffer * 128 + at


def place_of(device):
    row, col = device // (RING * RING), device % (RING * RING)
    return {
        "x": row // RING * 2 + col // CORES % 2,
        "y": col // RING,
        "z": row % RING,
        "core": col % CORES,
    }


def collect_kernel(pieces, source, *refs):
    groups = [refs[4 * piece : 4 * piece + 4] for piece in range(pieces)]
    buf, sems = refs[-2:]
    outs = refs[4 * pieces : -2]
    count, rows, _ = buf.shape
    part = rows // pieces
    chunk = count // len(outs)

    def target(at, piece):
        return buf.at[at, pl.ds(piece * part, part)]

    def load(at):
        for piece, group in enumerate(groups):
            code = source[piece, at]
            for which, ref in enumerate(group):

                @pl.when(code // 128 == which)
                def _():
                    pltpu.make_async_copy(
                        ref.at[code % 128], target(at, piece), sems.at[piece * count + at]
                    ).start()

    def loaded(at):
        for piece, group in enumerate(groups):
            pltpu.make_async_copy(
                group[3].at[0], target(at, piece), sems.at[piece * count + at]
            ).wait()

    pl.loop(0, count)(load)
    saves = [
        pltpu.make_async_copy(
            buf.at[pl.ds(part * chunk, chunk)], out, sems.at[pieces * count + part]
        )
        for part, out in enumerate(outs)
    ]
    for at, save in enumerate(saves):
        pl.loop(at * chunk, (at + 1) * chunk)(loaded)
        save.start()
    for save in saves:
        save.wait()


def collect(groups, source, chunks):
    pieces = len(groups)
    count = source.shape[1]
    _, rows, cols = groups[0][0].shape
    kind = groups[0][0].dtype
    part = jax.ShapeDtypeStruct((count // chunks, pieces * rows, cols), kind)
    return pl.pallas_call(
        functools.partial(collect_kernel, pieces),
        out_shape=[part] * chunks,
        in_specs=[SMEM] + [HBM] * (4 * pieces),
        out_specs=[HBM] * chunks,
        scratch_shapes=[
            pltpu.VMEM((count, pieces * rows, cols), kind),
            pltpu.SemaphoreType.DMA((pieces * count + chunks,)),
        ],
        name="collect",
    )(source, *(ref for group in groups for ref in group))


def split(value):
    high = value.astype(jnp.bfloat16)
    low = (value - high.astype(jnp.float32)).astype(jnp.bfloat16)
    return high, low


def product_kernel(pieces, parts, first, unroll, counts, items, order, *refs):
    lefts = refs[: 2 * pieces]
    rights = refs[2 * pieces : 2 * pieces + parts]
    refs = refs[2 * pieces + parts :]
    if not first:
        before, refs = refs[0], refs[1:]
    out, left_buf, right_buf, total, load_sems, out_sem = refs
    outs, edge, _ = out.shape
    slots_a = lefts[0].shape[0]
    slots_b = rights[0].shape[0]

    loads = [
        pltpu.make_async_copy(source, left_buf.at[at], load_sems.at[at])
        for at, source in enumerate(lefts)
    ] + [
        pltpu.make_async_copy(
            source, right_buf.at[pl.ds(at * slots_b, slots_b)], load_sems.at[2 * pieces + at]
        )
        for at, source in enumerate(rights)
    ]
    if not first:
        restore = pltpu.make_async_copy(before, total.at[pl.ds(0, outs)], out_sem)
        restore.start()
    for load in loads:
        load.start()
    if first:

        def clear(at):
            total[at] = jnp.zeros((edge, edge), jnp.float32)

        pl.loop(0, outs)(clear)
    else:
        restore.wait()
    for load in loads:
        load.wait()

    def step(at):
        codes = [items[at * unroll + lane] for lane in range(unroll)]
        sums = []
        for code in codes:
            slot_a = code // 16384
            slot_b = (code // 128) % 128
            piece = slot_a // slots_a
            swap = order[piece]
            slot_a = slot_a % slots_a
            left = jnp.concatenate(
                [
                    left_buf[2 * piece + swap, slot_a],
                    left_buf[2 * piece + 1 - swap, slot_a],
                ],
                axis=0,
            )
            a_hi, a_lo = split(left)
            b_hi, b_lo = split(right_buf[slot_b])
            sums.append(
                jnp.dot(
                    jnp.concatenate([a_hi, a_lo], axis=1),
                    jnp.concatenate([b_hi, b_hi], axis=0),
                    preferred_element_type=jnp.float32,
                )
                + jnp.dot(a_hi, b_lo, preferred_element_type=jnp.float32)
            )
        for code, value in zip(codes, sums):
            total[code % 128] += value

    pl.loop(0, counts[0])(step)
    save = pltpu.make_async_copy(total.at[pl.ds(0, outs)], out, out_sem)
    save.start()
    save.wait()


UNROLL = 8
CHUNKS = 2


def products(counts, items, order, halves, rights, before, outs):
    pieces, parts = len(halves) // 2, len(rights)
    slots_b, edge, _ = rights[0].shape
    slots_a, part, _ = halves[0].shape
    first = before is None
    extra = [] if first else [before]
    return pl.pallas_call(
        functools.partial(product_kernel, pieces, parts, first, UNROLL),
        out_shape=jax.ShapeDtypeStruct((outs, edge, edge), jnp.float32),
        in_specs=[SMEM] * 3 + [HBM] * (2 * pieces + parts + len(extra)),
        out_specs=HBM,
        scratch_shapes=[
            pltpu.VMEM((2 * pieces, slots_a, part, edge), jnp.float32),
            pltpu.VMEM((parts * slots_b, edge, edge), jnp.float32),
            pltpu.VMEM((outs + 1, edge, edge), jnp.float32),
            pltpu.SemaphoreType.DMA((2 * pieces + parts,)),
            pltpu.SemaphoreType.DMA,
        ],
        compiler_params=pltpu.CompilerParams(vmem_limit_bytes=40 * 1024 * 1024),
        cost_estimate=pl.CostEstimate(
            flops=pieces * 600_000_000, bytes_accessed=pieces * 8_000_000, transcendentals=0
        ),
        name="products",
    )(counts, items, order, *halves, *rights, *extra)


def work_list(lefts, rights, places, kept, first_row):
    rows, width = kept.shape
    pieces, inner, _ = rights.shape
    outs = rows * width
    slots = rows * WA
    rel = lefts - first_row
    here = rel[:, :, None] == jnp.arange(inner, dtype=jnp.int32)
    chosen = (
        jnp.sum(jnp.where(here[:, :, :, None], rights[:, None, :, :] + 1, 0), axis=2) - 1
    )
    at_row = jnp.repeat(kept, WA, axis=0)
    match = (chosen[:, :, :, None] == at_row[None, :, None, :]) & (chosen >= 0)[:, :, :, None]
    target = jnp.sum(jnp.where(match, jnp.arange(width, dtype=jnp.int32) + 1, 0), axis=3) - 1
    live = target >= 0
    slot = jnp.arange(slots, dtype=jnp.int32)[None, :, None]
    slot_a = slot + slots * jnp.arange(pieces, dtype=jnp.int32)[:, None, None]
    slot_b = (places[:, None, None] * inner + rel[:, :, None]) * WB + jnp.arange(WB, dtype=jnp.int32)
    code = slot_a * 16384 + slot_b * 128 + slot // WA * width + target
    live, code = live.reshape(-1), code.reshape(-1)
    spot = jnp.cumsum(live.astype(jnp.int32)) - 1
    place = jnp.arange(live.shape[0], dtype=jnp.int32)
    here = live[None, :] & (spot[None, :] == place[:, None])
    packed = jnp.sum(jnp.where(here, code[None, :] - outs, 0), axis=1) + outs
    count = (jnp.sum(live.astype(jnp.int32)) + UNROLL - 1) // UNROLL
    return count[None], packed


def on_device(a_held, a_slot, a_col, b_held, b_slot, b_col, c_col):
    grid_rows = lax.axis_size("row")
    grid_cols = lax.axis_size("col")
    devices = grid_rows * grid_cols
    copies = grid_cols // grid_rows
    i = lax.axis_index("row")
    c = lax.axis_index("col")
    rows, width = c_col.shape
    hold_a, hold_b = a_slot.shape[0], b_slot.shape[0]
    slots_a, slots_b = rows * WA, KPB * WB

    panel = a_slot // slots_a
    at_row, inner = panel // grid_rows, panel % grid_rows
    dest = at_row * grid_cols + (inner - at_row - 1) % grid_rows
    dest_left = dest[None, :] + grid_rows * jnp.arange(copies, dtype=jnp.int32)[:, None]
    panel = b_slot // slots_b
    inner, at_col = panel // grid_cols, panel % grid_cols
    dest_right = ((inner - at_col - 1) % grid_rows) * grid_cols + at_col

    edge = a_held.shape[1]
    labels = jnp.concatenate([a_slot, a_col, b_slot, b_col]).astype(jnp.float32)
    tile = jnp.pad(labels, (0, 8 * edge - labels.shape[0])).reshape(8, edge)
    to_right, to_left = place_of(dest_right), place_of(dest_left)
    spots = jnp.stack([place_in_send(to_right, order) for order in ORDERS[:2]])
    sends = pack(b_held, spots, devices, 2)
    sends += pack(a_held, place_in_send(to_left, ORDERS[2]), devices, 1)
    received, labels = exchange(sends, tile)

    labels = labels.reshape(RING, RING, 2, 2, CORES, -1)[..., : 2 * (hold_a + hold_b)]
    labels = labels.transpose(2, 0, 1, 3, 4, 5).reshape(devices, -1)
    labels = labels.astype(jnp.int32)
    parts = [hold_a, 2 * hold_a, 2 * hold_a + hold_b]
    all_a, all_acol, all_b, all_bcol = (part.reshape(-1) for part in jnp.split(labels, parts, axis=1))

    side = 2 * (c % 2) - 1
    turns = jnp.stack([jnp.int32(1), 1 - side, 1 + side])
    k = (i + c + turns) % grid_rows

    def look_up(panels, slots, table, columns, hold):
        wanted = panels[:, None] * slots + jnp.arange(slots, dtype=jnp.int32)[None, :]
        holder = jnp.arange(table.shape[0], dtype=jnp.int32) // hold
        code = holder * 32 + columns + 1
        found = jnp.sum(jnp.where(table[None, None, :] == wanted[:, :, None], code, 0), axis=2)
        return found // 32, found % 32 - 1

    src_left, col_left = look_up(i * grid_rows + k, slots_a, all_a, all_acol, hold_a)
    src_right, col_right = look_up(k * grid_cols + c, slots_b, all_b, all_bcol, hold_b)

    here = place_of(i * grid_cols + c)
    origin = place_of(src_right[0])
    source = jnp.stack([place_received(origin, here, order) for order in ORDERS[:2]])
    right = collect(received[:2], source, CHUNKS)
    (own,) = collect(received[2:], place_received(place_of(src_left[0]), here, ORDERS[2])[None], 1)
    other = shifted(own, "col", grid_rows)
    cross = permuted(own, "col", lambda at: ((at - 1) ^ 1) + 1)
    mate_first = permuted(own, "col", lambda at: at ^ 1)
    mate_second = permuted(other, "col", lambda at: at ^ 1)
    cross_second = shifted(cross, "col", grid_rows)
    homes = (c + jnp.stack([jnp.int32(0), -side, side])) % grid_cols
    order = (homes >= grid_rows).astype(jnp.int32)

    outs = rows * width
    tables = col_right.reshape(STEPS, KPB, WB)
    count, items = work_list(col_left[:1], tables[:1], jnp.zeros((1,), jnp.int32), c_col, 0)
    total = products(count, items, order[:1], [own, other], right, None, outs)
    places = jnp.stack([(1 - side) // 2, (1 + side) // 2])
    lefts = [mate_first, mate_second, cross, cross_second]
    chunk = slots_b // CHUNKS
    for at in range(CHUNKS):
        shifts = [shifted(right[at], "row", 1), shifted(right[at], "row", -1)]
        first, last = at * chunk // WB, (at + 1) * chunk // WB
        count, items = work_list(col_left[1:], tables[1:, first:last], places, c_col, first)
        total = products(count, items, order[1:], lefts, shifts, total, outs)
    return total.reshape(rows, width, edge, edge)


def solution(mesh):
    return jax.shard_map(
        on_device,
        mesh=mesh,
        in_specs=(
            P(("row", "col"), None, None),
            P(("row", "col")),
            P(("row", "col")),
            P(("row", "col"), None, None),
            P(("row", "col")),
            P(("row", "col")),
            P("row", "col"),
        ),
        out_specs=P("row", "col", None, None),
        check_vma=False,
    )
```

```python
import functools

import jax
import jax.numpy as jnp
from jax import lax
from jax.experimental import pallas as pl
from jax.experimental.pallas import tpu as pltpu
from jax.sharding import PartitionSpec as P

KPB = 16
WA = 4
WB = 4
STEPS = 3
HBM = pl.BlockSpec(memory_space=pltpu.HBM)


def pack_kernel(pieces, dest, held, *refs):
    outs, buf, sems = refs[:-2], refs[-2], refs[-1]
    count, rows, _ = held.shape
    part = rows // pieces

    def load(at):
        return pltpu.make_async_copy(held.at[at], buf.at[at], sems.at[at])

    def save(at, piece):
        return pltpu.make_async_copy(
            buf.at[at, pl.ds(piece * part, part)],
            outs[piece % len(outs)].at[dest[piece, at]],
            sems.at[(1 + piece) * count + at],
        )

    pl.loop(0, count)(lambda at: load(at).start())

    def body(at):
        load(at).wait()
        for piece in range(pieces):
            save(at, piece).start()

    pl.loop(0, count)(body)
    for piece in range(pieces):
        pl.loop(0, count)(lambda at: save(at, piece).wait())


GRANT = 60 * 1024 * 1024
SMEM = pl.BlockSpec(memory_space=pltpu.SMEM)
VMEM = pl.BlockSpec(memory_space=pltpu.VMEM)


def pack(held, dest, devices, outs):
    pieces = dest.shape[0]
    count, rows, cols = held.shape
    shape = jax.ShapeDtypeStruct((devices, rows // pieces, cols), held.dtype)
    return pl.pallas_call(
        functools.partial(pack_kernel, pieces),
        out_shape=[shape] * outs,
        in_specs=[SMEM, HBM],
        out_specs=[HBM] * outs,
        scratch_shapes=[
            pltpu.VMEM(held.shape, held.dtype),
            pltpu.SemaphoreType.DMA(((1 + pieces) * count,)),
        ],
        compiler_params=pltpu.CompilerParams(vmem_limit_bytes=GRANT),
        name="pack",
    )(dest, held)


ORDERS = (("x", "y", "z"), ("y", "z", "x"), ("z", "x", "y"))
STEPS_FIRST = (1, 2, 6, 3, 7, 4, 5)
STEPS_LATER = (1, 3, 2)
RING = 4
CORES = 2


def my_place():
    row, col = lax.axis_index("row"), lax.axis_index("col")
    return {
        "x": row // RING * 2 + col // CORES % 2,
        "y": col // RING,
        "z": row % RING,
        "core": col % CORES,
    }


def coords_of(place):
    row = place["x"] // 2 * RING + place["z"]
    col = place["y"] * RING + place["x"] % 2 * CORES + place["core"]
    return row, col


def exchange_kernel(*refs):
    parts = len(ORDERS)
    sends, refs = refs[:parts], refs[parts:]
    tile, refs = refs[0], refs[1:]
    stages = [refs[3 * part : 3 * part + 3] for part in range(parts)]
    labels = refs[3 * parts]
    first_recv, second_recv, third_recv, send_sems, label_send, label_recv = refs[3 * parts + 1 :]
    place = my_place()

    def moved(axis, steps, flip):
        there = dict(place)
        there[axis] = (place[axis] + steps) % RING
        there["core"] = (place["core"] + flip) % CORES
        return there

    def copy(source, target, send_sem, recv_sem, there):
        return pltpu.make_async_remote_copy(
            src_ref=source,
            dst_ref=target,
            send_sem=send_sem,
            recv_sem=recv_sem,
            device_id=coords_of(there),
            device_id_type=pl.DeviceIdType.MESH,
        )

    def spot(there, axis):
        return there[axis] * CORES + there["core"]

    def arrived(like, sem):
        pltpu.make_async_copy(like, like, sem).wait()

    peers = [moved("x", 0, 1)]
    for axis in ("x", "y", "z"):
        for steps in range(1, RING):
            for flip in range(CORES):
                peers.append(moved(axis, steps, flip))
    barrier = pltpu.get_barrier_semaphore()
    for there in peers:
        pl.semaphore_signal(
            barrier, inc=1, device_id=coords_of(there), device_id_type=pl.DeviceIdType.MESH
        )
    pl.semaphore_wait(barrier, len(peers))

    x, y, z = spot(place, "x"), place["y"], place["z"]
    labels[z, y, x] = tile[...]
    for steps in STEPS_FIRST:
        copy(
            labels.at[z, y, x],
            labels.at[z, y, x],
            label_send.at[0],
            label_recv.at[0],
            moved("x", steps // CORES, steps % CORES),
        ).start()
    for steps in STEPS_FIRST:
        for part, (one, two, three) in enumerate(ORDERS):
            there = moved(one, steps // CORES, steps % CORES)
            copy(
                sends[part].at[spot(there, one)],
                stages[part][0].at[spot(place, one)],
                send_sems.at[part, 0],
                first_recv.at[part, steps],
                there,
            ).start()
    arrived(labels.at[0, 0, pl.ds(0, 7)], label_recv.at[0])
    for steps in STEPS_LATER:
        copy(
            labels.at[z, y], labels.at[z, y], label_send.at[1], label_recv.at[1], moved("y", steps, 0)
        ).start()
    arrived(labels.at[0, pl.ds(0, 3)], label_recv.at[1])
    for steps in STEPS_LATER:
        copy(
            labels.at[z], labels.at[z], label_send.at[2], label_recv.at[2], moved("z", steps, 0)
        ).start()

    for steps in (0,) + STEPS_FIRST:
        for part, (one, two, three) in enumerate(ORDERS):
            origin = spot(moved(one, RING - steps // CORES, steps % CORES), one)
            if steps:
                source = stages[part][0]
                arrived(source.at[0], first_recv.at[part, steps])
            else:
                source = sends[part]
            for later in STEPS_LATER:
                there = moved(two, later, 0)
                copy(
                    source.at[origin, there[two]],
                    stages[part][1].at[place[two], origin],
                    send_sems.at[part, 1],
                    second_recv.at[part, later],
                    there,
                ).start()

    def last(part, source, target, there):
        copy(source, target, send_sems.at[part, 2], third_recv.at[part], there).start()

    for part, (one, two, three) in enumerate(ORDERS):
        for steps in (0,) + STEPS_FIRST:
            origin = spot(moved(one, RING - steps // CORES, steps % CORES), one)
            source = stages[part][0] if steps else sends[part]
            for later in STEPS_LATER:
                there = moved(three, later, 0)
                last(
                    part,
                    source.at[origin, place[two], there[three]],
                    stages[part][2].at[place[three], place[two], origin],
                    there,
                )
    for steps in STEPS_LATER:
        for part, (one, two, three) in enumerate(ORDERS):
            origin = moved(two, RING - steps, 0)[two]
            arrived(stages[part][1].at[0], second_recv.at[part, steps])
            for later in STEPS_LATER:
                there = moved(three, later, 0)
                last(
                    part,
                    stages[part][1].at[origin, :, there[three]],
                    stages[part][2].at[place[three], origin],
                    there,
                )
    for part in range(parts):
        arrived(stages[part][2].at[pl.ds(0, 3)], third_recv.at[part])
        arrived(sends[part].at[pl.ds(0, 7)], send_sems.at[part, 0])
        arrived(stages[part][2].at[pl.ds(0, 3)], send_sems.at[part, 1])
        arrived(stages[part][2].at[pl.ds(0, 3)], send_sems.at[part, 2])
    arrived(labels.at[pl.ds(0, 3)], label_recv.at[2])
    arrived(labels.at[0, 0, pl.ds(0, 7)], label_send.at[0])
    arrived(labels.at[0, pl.ds(0, 3)], label_send.at[1])
    arrived(labels.at[pl.ds(0, 3)], label_send.at[2])


def exchange(sends, tile):
    parts = len(sends)
    _, rows, cols = sends[0].shape
    kind = sends[0].dtype
    block = (rows, cols)
    eight = RING * CORES
    shapes = [
        (eight, RING, RING) + block,
        (RING, eight, RING) + block,
        (RING, RING, eight) + block,
    ]
    outs = pl.pallas_call(
        exchange_kernel,
        out_shape=[jax.ShapeDtypeStruct(shape, kind) for shape in shapes] * parts
        + [jax.ShapeDtypeStruct((RING, RING, eight) + tile.shape, tile.dtype)],
        in_specs=[HBM] * parts + [VMEM],
        out_specs=[HBM] * (3 * parts) + [VMEM],
        scratch_shapes=[
            pltpu.SemaphoreType.DMA((parts, eight)),
            pltpu.SemaphoreType.DMA((parts, RING)),
            pltpu.SemaphoreType.DMA((parts,)),
            pltpu.SemaphoreType.DMA((parts, 3)),
            pltpu.SemaphoreType.DMA((3,)),
            pltpu.SemaphoreType.DMA((3,)),
        ],
        compiler_params=pltpu.CompilerParams(
            collective_id=0, has_side_effects=True, vmem_limit_bytes=GRANT
        ),
        name="exchange",
    )(*(send.reshape((eight, RING, RING) + block) for send in sends), tile)
    flat = [out.reshape((-1,) + block) for out in outs[: 3 * parts]]
    groups = [
        [sends[part]] + flat[3 * part : 3 * part + 3] for part in range(parts)
    ]
    return groups, outs[-1]


def place_in_send(place, order):
    one, two, three = (place[axis] for axis in order)
    return ((one * CORES + place["core"]) * RING + two) * RING + three


def place_received(origin, here, order):
    one, two, three = ((origin[axis], here[axis]) for axis in order)
    first = one[0] * CORES + origin["core"]
    same_first = (one[0] == one[1]) & (origin["core"] == here["core"])
    same_two, same_three = two[0] == two[1], three[0] == three[1]
    early = (first * RING + two[0]) * RING + three[0]
    middle = (two[0] * RING * CORES + first) * RING + three[0]
    late = (three[0] * RING + two[0]) * RING * CORES + first
    buffer = jnp.where(
        same_three, jnp.where(same_two, jnp.where(same_first, 0, 1), 2), 3
    )
    at = jnp.where(buffer == 3, late, jnp.where(buffer == 2, middle, early))
    return buffer * 128 + at


def place_of(device):
    row, col = device // (RING * RING), device % (RING * RING)
    return {
        "x": row // RING * 2 + col // CORES % 2,
        "y": col // RING,
        "z": row % RING,
        "core": col % CORES,
    }


def collect_kernel(source, lefts, rights, kept, *refs):
    groups = [refs[4 * piece : 4 * piece + 4] for piece in range(3)]
    right_out, left_out, items, counts, right_buf, left_buf, sems = refs[12:]
    count = right_buf.shape[0]
    part = left_buf.shape[1]

    def target(at, piece):
        if piece == 2:
            return left_buf.at[at]
        return right_buf.at[at, pl.ds(piece * part, part)]

    def load(piece):
        def body(at):
            code = source[piece * count + at]
            for which, ref in enumerate(groups[piece]):

                @pl.when(code // 128 == which)
                def _():
                    pltpu.make_async_copy(
                        ref.at[code % 128], target(at, piece), sems.at[piece * count + at]
                    ).start()

        pl.loop(0, count)(body)

    def loaded(piece):
        def body(at):
            pltpu.make_async_copy(
                groups[piece][3].at[0], target(at, piece), sems.at[piece * count + at]
            ).wait()

        pl.loop(0, count)(body)

    for piece in (2, 0, 1):
        load(piece)
    for step in range(STEPS):

        def body(slot, found):
            column = lefts[step * count + slot]
            inner = jnp.maximum(column, 0)
            for way in range(WB):
                other = rights[step * count + inner * WB + way]
                out = kept[slot // WA * (KPB + 1) + other + 1]
                items[step, found] = slot * 16384 + (inner * WB + way) * 128 + jnp.maximum(out, 0)
                found += ((column >= 0) & (out >= 0)).astype(jnp.int32)
            return found

        found = lax.fori_loop(0, count, body, jnp.int32(0))
        for lane in range(UNROLL):
            items[step, found + lane] = SPARE
        counts[step] = (found + UNROLL - 1) // UNROLL
    loaded(2)
    save_left = pltpu.make_async_copy(left_buf, left_out, sems.at[3 * count])
    save_left.start()
    loaded(0)
    loaded(1)
    save_right = pltpu.make_async_copy(right_buf, right_out, sems.at[3 * count + 1])
    save_right.start()
    save_left.wait()
    save_right.wait()


def collect(groups, source, lefts, rights, kept):
    count = source.shape[0] // 3
    _, rows, cols = groups[0][0].shape
    kind = groups[0][0].dtype
    right, left = (count, 2 * rows, cols), (count, rows, cols)
    return pl.pallas_call(
        collect_kernel,
        out_shape=[
            jax.ShapeDtypeStruct(right, kind),
            jax.ShapeDtypeStruct(left, kind),
            jax.ShapeDtypeStruct((STEPS, count * WB + UNROLL), jnp.int32),
            jax.ShapeDtypeStruct((STEPS,), jnp.int32),
        ],
        in_specs=[SMEM] * 4 + [HBM] * 12,
        out_specs=[HBM, HBM, SMEM, SMEM],
        scratch_shapes=[
            pltpu.VMEM(right, kind),
            pltpu.VMEM(left, kind),
            pltpu.SemaphoreType.DMA((3 * count + 2,)),
        ],
        compiler_params=pltpu.CompilerParams(vmem_limit_bytes=GRANT),
        name="collect",
    )(source, lefts, rights, kept, *(ref for group in groups for ref in group))


RIGHT_CHUNKS = 8
RELAYED = 3
LEFT_CHUNKS = 4


def spread_kernel(own, right, other, mate_one, mate_two, cross_one, cross_two, before, after, *sems):
    send_sems, before_sems, after_sems, other_sems, cross_sems, late_sems = sems
    row, col = lax.axis_index("row"), lax.axis_index("col")
    rows, cols = lax.axis_size("row"), lax.axis_size("col")
    half = row % RING
    up, down = ((row + 1) % rows, col), ((row + rows - 1) % rows, col)
    up_two, down_two = ((row + 2) % rows, col), ((row + rows - 2) % rows, col)
    twin = (row, (col + cols // 2) % cols)
    mate = (row, col + 1 - 2 * (col % 2))
    cross = (row, (col + cols - 1 + 2 * (col % 2)) % cols)

    barrier = pltpu.get_barrier_semaphore()
    peers = (up, down, up_two, down_two, twin, mate, cross)
    for there in peers:
        pl.semaphore_signal(
            barrier, inc=1, device_id=there, device_id_type=pl.DeviceIdType.MESH
        )
    pl.semaphore_wait(barrier, len(peers))

    right_size = right.shape[0] // RIGHT_CHUNKS
    left_size = own.shape[0] // LEFT_CHUNKS

    def cut(ref, at, size):
        return ref.at[pl.ds(at * size, size)]

    def send(source, target, at, size, send_sem, recv_sem, there):
        return pltpu.make_async_remote_copy(
            src_ref=cut(source, at, size),
            dst_ref=cut(target, at, size),
            send_sem=send_sem,
            recv_sem=recv_sem,
            device_id=there,
            device_id_type=pl.DeviceIdType.MESH,
        )

    def raise_chunk(at):
        return send(right, before, at, right_size, send_sems.at[0, at], before_sems.at[at], up)

    def lower_chunk(at):
        return send(right, after, at, right_size, send_sems.at[1, at], after_sems.at[at], down)

    def relay_up(at):
        return send(after, before, at, right_size, send_sems.at[2, at], before_sems.at[at], up_two)

    def relay_down(at):
        return send(before, after, at, right_size, send_sems.at[2, at], after_sems.at[at], down_two)

    def to_twin(at):
        return send(own, other, at, left_size, send_sems.at[3, at], other_sems.at[at], twin)

    def to_cross(at):
        return send(own, cross_one, at, left_size, send_sems.at[4, at], cross_sems.at[at], cross)

    def to_mate(at):
        return send(own, mate_one, at, left_size, send_sems.at[5, at], late_sems.at[0, at], mate)

    def pass_mate(at):
        return send(other, mate_two, at, left_size, send_sems.at[6, at], late_sems.at[1, at], mate)

    def pass_twin(at):
        return send(
            cross_one, cross_two, at, left_size, send_sems.at[7, at], late_sems.at[2, at], twin
        )

    last = half == RING - 1
    first = half == 0
    for at in range(RELAYED):

        @pl.when(jnp.logical_not(last))
        def _():
            raise_chunk(at).start()

        @pl.when(jnp.logical_not(first))
        def _():
            lower_chunk(at).start()

    for at in range(LEFT_CHUNKS):
        to_cross(at).start()
        to_twin(at).start()
        to_mate(at).start()
    for at in range(RELAYED, RIGHT_CHUNKS):
        raise_chunk(at).start()
        lower_chunk(at).start()
    for at in range(RELAYED):

        @pl.when(half == RING - 2)
        def _():
            lower_chunk(at).wait_recv()
            relay_up(at).start()

        @pl.when(half == 1)
        def _():
            raise_chunk(at).wait_recv()
            relay_down(at).start()

    for at in range(LEFT_CHUNKS):
        to_cross(at).wait_recv()
        pass_twin(at).start()
        to_twin(at).wait_recv()
        pass_mate(at).start()

    for at in range(RELAYED):

        @pl.when(half != 1)
        def _():
            raise_chunk(at).wait_recv()

        @pl.when(half != RING - 2)
        def _():
            lower_chunk(at).wait_recv()

        @pl.when(jnp.logical_not(last))
        def _():
            raise_chunk(at).wait_send()

        @pl.when(jnp.logical_not(first))
        def _():
            lower_chunk(at).wait_send()

        @pl.when(half == RING - 2)
        def _():
            relay_up(at).wait_send()

        @pl.when(half == 1)
        def _():
            relay_down(at).wait_send()

    for at in range(RELAYED, RIGHT_CHUNKS):
        raise_chunk(at).wait()
        lower_chunk(at).wait()
    for at in range(LEFT_CHUNKS):
        to_mate(at).wait()
        pass_mate(at).wait()
        pass_twin(at).wait()
        to_twin(at).wait_send()
        to_cross(at).wait_send()


def spread(own, right):
    left_shape = jax.ShapeDtypeStruct(own.shape, own.dtype)
    right_shape = jax.ShapeDtypeStruct(right.shape, right.dtype)
    dma = pltpu.SemaphoreType.DMA
    return pl.pallas_call(
        spread_kernel,
        out_shape=[left_shape] * 5 + [right_shape] * 2,
        in_specs=[HBM] * 2,
        out_specs=[HBM] * 7,
        scratch_shapes=[
            dma((8, RIGHT_CHUNKS)),
            dma((RIGHT_CHUNKS,)),
            dma((RIGHT_CHUNKS,)),
            dma((LEFT_CHUNKS,)),
            dma((LEFT_CHUNKS,)),
            dma((3, LEFT_CHUNKS)),
        ],
        compiler_params=pltpu.CompilerParams(
            collective_id=1, has_side_effects=True, vmem_limit_bytes=GRANT
        ),
        name="spread",
    )(own, right)


def split(value):
    high = value.astype(jnp.bfloat16)
    low = (value - high.astype(jnp.float32)).astype(jnp.bfloat16)
    return high, low


UNROLL = 8
SPARE = 96


def product_kernel(counts, items, order, places, *refs):
    lefts = refs[: 2 * STEPS]
    right, before, after, out, left_buf, right_buf, total, load_sems, out_sem = refs[2 * STEPS :]
    outs, edge, _ = out.shape

    def right_load(step, source):
        return pltpu.make_async_copy(source, right_buf.at[step], load_sems.at[2 * STEPS + step])

    left_loads = [
        pltpu.make_async_copy(source, left_buf.at[at], load_sems.at[at])
        for at, source in enumerate(lefts)
    ]
    for step in range(STEPS):
        left_loads[2 * step].start()
        left_loads[2 * step + 1].start()
        if step == 0:
            right_load(0, right).start()
        else:
            for place, source in enumerate((before, after)):

                @pl.when(places[step - 1] == place)
                def _():
                    right_load(step, source).start()

    def clear(at):
        total[at] = jnp.zeros((edge, edge), jnp.float32)

    pl.loop(0, outs + 1)(clear)

    for step in range(STEPS):
        left_loads[2 * step].wait()
        left_loads[2 * step + 1].wait()
        right_load(step, right).wait()
        swap = order[step]

        def body(at):
            codes = [items[step, at * UNROLL + lane] for lane in range(UNROLL)]
            sums = []
            for code in codes:
                slot_a = lax.shift_right_logical(code, 14)
                slot_b = lax.shift_right_logical(code, 7) & 127
                left = jnp.concatenate(
                    [
                        left_buf[2 * step + swap, slot_a],
                        left_buf[2 * step + 1 - swap, slot_a],
                    ],
                    axis=0,
                )
                a_hi, a_lo = split(left)
                b_hi, b_lo = split(right_buf[step, slot_b])
                sums.append(
                    jnp.dot(
                        jnp.concatenate([a_hi, a_lo], axis=1),
                        jnp.concatenate([b_hi, b_hi], axis=0),
                        preferred_element_type=jnp.float32,
                    )
                    + jnp.dot(a_hi, b_lo, preferred_element_type=jnp.float32)
                )
            for code, value in zip(codes, sums):
                total[code & 127] += value

        pl.loop(0, counts[step])(body)
    save = pltpu.make_async_copy(total.at[pl.ds(0, outs)], out, out_sem)
    save.start()
    save.wait()


def products(counts, items, order, places, lefts, rights, outs):
    slots_b, edge, _ = rights[0].shape
    slots_a, part, _ = lefts[0].shape
    return pl.pallas_call(
        product_kernel,
        out_shape=jax.ShapeDtypeStruct((outs, edge, edge), jnp.float32),
        in_specs=[SMEM] * 4 + [HBM] * (len(lefts) + len(rights)),
        out_specs=HBM,
        scratch_shapes=[
            pltpu.VMEM((2 * STEPS, slots_a, part, edge), jnp.float32),
            pltpu.VMEM((STEPS, slots_b, edge, edge), jnp.float32),
            pltpu.VMEM((outs + 1, edge, edge), jnp.float32),
            pltpu.SemaphoreType.DMA((3 * STEPS,)),
            pltpu.SemaphoreType.DMA,
        ],
        compiler_params=pltpu.CompilerParams(vmem_limit_bytes=GRANT),
        name="products",
    )(counts, items, order, places, *lefts, *rights)


def on_device(a_held, a_slot, a_col, b_held, b_slot, b_col, c_col):
    grid_rows = lax.axis_size("row")
    grid_cols = lax.axis_size("col")
    devices = grid_rows * grid_cols
    copies = grid_cols // grid_rows
    i = lax.axis_index("row")
    c = lax.axis_index("col")
    rows, width = c_col.shape
    hold_a, hold_b = a_slot.shape[0], b_slot.shape[0]
    slots_a, slots_b = rows * WA, KPB * WB

    panel = a_slot // slots_a
    at_row, inner = panel // grid_rows, panel % grid_rows
    dest = at_row * grid_cols + (inner - at_row - 1) % grid_rows
    dest_left = dest[None, :] + grid_rows * jnp.arange(copies, dtype=jnp.int32)[:, None]
    panel = b_slot // slots_b
    inner, at_col = panel // grid_cols, panel % grid_cols
    dest_right = ((inner - at_col - 1) % grid_rows) * grid_cols + at_col

    edge = a_held.shape[1]
    labels = jnp.concatenate([a_slot, a_col, b_slot, b_col]).astype(jnp.float32)
    tile = jnp.pad(labels, (0, 8 * edge - labels.shape[0])).reshape(8, edge)
    to_right, to_left = place_of(dest_right), place_of(dest_left)
    spots = jnp.stack([place_in_send(to_right, order) for order in ORDERS[:2]])
    sends = pack(b_held, spots, devices, 2)
    sends += pack(a_held, place_in_send(to_left, ORDERS[2]), devices, 1)
    received, labels = exchange(sends, tile)

    labels = labels.reshape(RING, RING, 2, 2, CORES, -1)[..., : 2 * (hold_a + hold_b)]
    labels = labels.transpose(2, 0, 1, 3, 4, 5).reshape(devices, -1)
    labels = labels.astype(jnp.int32)
    parts = [hold_a, 2 * hold_a, 2 * hold_a + hold_b]
    all_a, all_acol, all_b, all_bcol = (part.reshape(-1) for part in jnp.split(labels, parts, axis=1))

    side = 2 * (c % 2) - 1
    turns = jnp.stack([jnp.int32(1), 1 - side, 1 + side])
    k = (i + c + turns) % grid_rows

    def look_up(panels, slots, table, columns, hold):
        wanted = panels[:, None] * slots + jnp.arange(slots, dtype=jnp.int32)[None, :]
        holder = jnp.arange(table.shape[0], dtype=jnp.int32) // hold
        code = holder * 32 + columns + 1
        found = jnp.sum(jnp.where(table[None, None, :] == wanted[:, :, None], code, 0), axis=2)
        return found // 32, found % 32 - 1

    src_left, col_left = look_up(i * grid_rows + k, slots_a, all_a, all_acol, hold_a)
    src_right, col_right = look_up(k * grid_cols + c, slots_b, all_b, all_bcol, hold_b)

    here = place_of(i * grid_cols + c)
    origin = place_of(src_right[0])
    source = [place_received(origin, here, order) for order in ORDERS[:2]]
    source.append(place_received(place_of(src_left[0]), here, ORDERS[2]))
    hit = c_col[:, :, None] == jnp.arange(-1, KPB, dtype=jnp.int32)
    hit &= (c_col >= 0)[:, :, None]
    outs = jnp.arange(rows * width, dtype=jnp.int32).reshape(rows, width, 1)
    kept = jnp.sum(jnp.where(hit, outs + 1, 0), axis=1) - 1
    right, own, items, counts = collect(
        received,
        jnp.concatenate(source),
        col_left.reshape(-1),
        col_right.reshape(-1),
        kept.reshape(-1),
    )
    other, mate_one, mate_two, cross_one, cross_two, before, after = spread(own, right)

    homes = (c + jnp.stack([jnp.int32(0), -side, side])) % grid_cols
    order = (homes >= grid_rows).astype(jnp.int32)
    places = jnp.stack([(1 - side) // 2, (1 + side) // 2])
    lefts = [own, other, mate_one, mate_two, cross_one, cross_two]
    total = products(counts, items, order, places, lefts, [right, before, after], rows * width)
    return total.reshape(rows, width, edge, edge)


def solution(mesh):
    return jax.shard_map(
        on_device,
        mesh=mesh,
        in_specs=(
            P(("row", "col"), None, None),
            P(("row", "col")),
            P(("row", "col")),
            P(("row", "col"), None, None),
            P(("row", "col")),
            P(("row", "col")),
            P("row", "col"),
        ),
        out_specs=P("row", "col", None, None),
        check_vma=False,
    )
```

```python
import functools

import jax
import jax.numpy as jnp
from jax import lax
from jax.experimental import pallas as pl
from jax.experimental.pallas import tpu as pltpu
from jax.sharding import PartitionSpec as P

KPB = 16
WA = 4
WB = 4
STEPS = 3
HBM = pl.BlockSpec(memory_space=pltpu.HBM)


def pack_kernel(
    grid, a_slot, b_slot, c_col, a_held, b_held, upper, lower, halves, kept, a_buf, b_buf, sems
):
    grid_rows, grid_cols = grid
    hold_a, hold_b = a_held.shape[0], b_held.shape[0]
    rows, width = c_col.shape
    part = halves.shape[1]
    base = hold_a + hold_b

    def load_a(at):
        return pltpu.make_async_copy(a_held.at[at], a_buf.at[at], sems.at[at])

    def load_b(at):
        return pltpu.make_async_copy(b_held.at[at], b_buf.at[at], sems.at[hold_a + at])

    def save_a(at, half, spot):
        return pltpu.make_async_copy(
            a_buf.at[at, pl.ds(half * part, part)], halves.at[spot], sems.at[base + 2 * at + half]
        )

    def save_b(at, half, spot):
        return pltpu.make_async_copy(
            b_buf.at[at, pl.ds(half * part, part)],
            (upper, lower)[half].at[spot],
            sems.at[base + 2 * (hold_a + at) + half],
        )

    pl.loop(0, hold_b)(lambda at: load_b(at).start())
    pl.loop(0, hold_a)(lambda at: load_a(at).start())

    def send_b(at):
        panel = lax.div(b_slot[at], KPB * WB)
        inner, col = lax.div(panel, grid_cols), lax.rem(panel, grid_cols)
        row = lax.rem(inner - col - 1 + grid_rows + grid_cols, grid_rows)
        place = place_of(row * grid_cols + col)
        load_b(at).wait()
        for half, order in enumerate(ORDERS[:2]):
            save_b(at, half, place_in_send(place, order)).start()

    pl.loop(0, hold_b)(send_b)

    def send_a(at):
        panel = lax.div(a_slot[at], rows * WA)
        row, inner = lax.div(panel, grid_rows), lax.rem(panel, grid_rows)
        col = lax.rem(inner - row - 1 + 2 * grid_rows, grid_rows)
        load_a(at).wait()
        for half in range(2):
            place = place_of(row * grid_cols + col + half * grid_rows)
            save_a(at, half, place_in_send(place, ORDERS[2])).start()

    pl.loop(0, hold_a)(send_a)

    def empty(row):
        for column in range(KPB + 1):
            kept[row * (KPB + 1) + column] = -1

    pl.loop(0, rows)(empty)

    def keep(row):
        for at in range(width):
            column = c_col[row, at]
            kept[row * (KPB + 1) + column + 1] = jnp.where(column >= 0, row * width + at, -1)

    pl.loop(0, rows)(keep)
    for half in range(2):
        pl.loop(0, hold_b)(lambda at: save_b(at, half, 0).wait())
        pl.loop(0, hold_a)(lambda at: save_a(at, half, 0).wait())


GRANT = 60 * 1024 * 1024
SMEM = pl.BlockSpec(memory_space=pltpu.SMEM)
VMEM = pl.BlockSpec(memory_space=pltpu.VMEM)


def pack(grid, a_slot, b_slot, c_col, a_held, b_held):
    devices = grid[0] * grid[1]
    edge, cols = a_held.shape[1:]
    send = jax.ShapeDtypeStruct((devices, edge // 2, cols), a_held.dtype)
    kept = jax.ShapeDtypeStruct((c_col.shape[0] * (KPB + 1),), jnp.int32)
    *sends, kept = pl.pallas_call(
        functools.partial(pack_kernel, grid),
        out_shape=[send] * 3 + [kept],
        in_specs=[SMEM] * 3 + [HBM] * 2,
        out_specs=[HBM] * 3 + [SMEM],
        scratch_shapes=[
            pltpu.VMEM(a_held.shape, a_held.dtype),
            pltpu.VMEM(b_held.shape, b_held.dtype),
            pltpu.SemaphoreType.DMA((3 * (a_held.shape[0] + b_held.shape[0]),)),
        ],
        compiler_params=pltpu.CompilerParams(vmem_limit_bytes=GRANT),
        name="pack",
    )(a_slot, b_slot, c_col, a_held, b_held)
    return sends, kept


ORDERS = (("x", "y", "z"), ("y", "z", "x"), ("z", "x", "y"))
STEPS_FIRST = (1, 2, 6, 3, 7, 4, 5)
STEPS_LATER = (1, 3, 2)
RING = 4
CORES = 2


def my_place():
    row, col = lax.axis_index("row"), lax.axis_index("col")
    return {
        "x": row // RING * 2 + col // CORES % 2,
        "y": col // RING,
        "z": row % RING,
        "core": col % CORES,
    }


def coords_of(place):
    row = place["x"] // 2 * RING + place["z"]
    col = place["y"] * RING + place["x"] % 2 * CORES + place["core"]
    return row, col


def exchange_kernel(*refs):
    parts = len(ORDERS)
    sends, refs = refs[:parts], refs[parts:]
    tile, refs = refs[0], refs[1:]
    stages = [refs[3 * part : 3 * part + 3] for part in range(parts)]
    labels = refs[3 * parts]
    first_recv, second_recv, third_recv, send_sems, label_send, label_recv = refs[3 * parts + 1 :]
    place = my_place()

    def moved(axis, steps, flip):
        there = dict(place)
        there[axis] = (place[axis] + steps) % RING
        there["core"] = (place["core"] + flip) % CORES
        return there

    def copy(source, target, send_sem, recv_sem, there):
        return pltpu.make_async_remote_copy(
            src_ref=source,
            dst_ref=target,
            send_sem=send_sem,
            recv_sem=recv_sem,
            device_id=coords_of(there),
            device_id_type=pl.DeviceIdType.MESH,
        )

    def spot(there, axis):
        return there[axis] * CORES + there["core"]

    def arrived(like, sem):
        pltpu.make_async_copy(like, like, sem).wait()

    peers = [moved("x", 0, 1)]
    for axis in ("x", "y", "z"):
        for steps in range(1, RING):
            for flip in range(CORES):
                peers.append(moved(axis, steps, flip))
    barrier = pltpu.get_barrier_semaphore()
    for there in peers:
        pl.semaphore_signal(
            barrier, inc=1, device_id=coords_of(there), device_id_type=pl.DeviceIdType.MESH
        )
    pl.semaphore_wait(barrier, len(peers))

    x, y, z = spot(place, "x"), place["y"], place["z"]
    labels[z, y, x] = tile[...]
    for steps in STEPS_FIRST:
        copy(
            labels.at[z, y, x],
            labels.at[z, y, x],
            label_send.at[0],
            label_recv.at[0],
            moved("x", steps // CORES, steps % CORES),
        ).start()
    for steps in STEPS_FIRST:
        for part, (one, two, three) in enumerate(ORDERS):
            there = moved(one, steps // CORES, steps % CORES)
            copy(
                sends[part].at[spot(there, one)],
                stages[part][0].at[spot(place, one)],
                send_sems.at[part, 0],
                first_recv.at[part, steps],
                there,
            ).start()
    arrived(labels.at[0, 0, pl.ds(0, 7)], label_recv.at[0])
    for steps in STEPS_LATER:
        copy(
            labels.at[z, y], labels.at[z, y], label_send.at[1], label_recv.at[1], moved("y", steps, 0)
        ).start()
    arrived(labels.at[0, pl.ds(0, 3)], label_recv.at[1])
    for steps in STEPS_LATER:
        copy(
            labels.at[z], labels.at[z], label_send.at[2], label_recv.at[2], moved("z", steps, 0)
        ).start()

    for steps in (0,) + STEPS_FIRST:
        for part, (one, two, three) in enumerate(ORDERS):
            origin = spot(moved(one, RING - steps // CORES, steps % CORES), one)
            if steps:
                source = stages[part][0]
                arrived(source.at[0], first_recv.at[part, steps])
            else:
                source = sends[part]
            for later in STEPS_LATER:
                there = moved(two, later, 0)
                copy(
                    source.at[origin, there[two]],
                    stages[part][1].at[place[two], origin],
                    send_sems.at[part, 1],
                    second_recv.at[part, later],
                    there,
                ).start()

    def last(part, source, target, there):
        copy(source, target, send_sems.at[part, 2], third_recv.at[part], there).start()

    for part, (one, two, three) in enumerate(ORDERS):
        for steps in (0,) + STEPS_FIRST:
            origin = spot(moved(one, RING - steps // CORES, steps % CORES), one)
            source = stages[part][0] if steps else sends[part]
            for later in STEPS_LATER:
                there = moved(three, later, 0)
                last(
                    part,
                    source.at[origin, place[two], there[three]],
                    stages[part][2].at[place[three], place[two], origin],
                    there,
                )
    for steps in STEPS_LATER:
        for part, (one, two, three) in enumerate(ORDERS):
            origin = moved(two, RING - steps, 0)[two]
            arrived(stages[part][1].at[0], second_recv.at[part, steps])
            for later in STEPS_LATER:
                there = moved(three, later, 0)
                last(
                    part,
                    stages[part][1].at[origin, :, there[three]],
                    stages[part][2].at[place[three], origin],
                    there,
                )
    for part in range(parts):
        arrived(stages[part][2].at[pl.ds(0, 3)], third_recv.at[part])
        arrived(sends[part].at[pl.ds(0, 7)], send_sems.at[part, 0])
        arrived(stages[part][2].at[pl.ds(0, 3)], send_sems.at[part, 1])
        arrived(stages[part][2].at[pl.ds(0, 3)], send_sems.at[part, 2])
    arrived(labels.at[pl.ds(0, 3)], label_recv.at[2])
    arrived(labels.at[0, 0, pl.ds(0, 7)], label_send.at[0])
    arrived(labels.at[0, pl.ds(0, 3)], label_send.at[1])
    arrived(labels.at[pl.ds(0, 3)], label_send.at[2])


def exchange(sends, tile):
    parts = len(sends)
    _, rows, cols = sends[0].shape
    kind = sends[0].dtype
    block = (rows, cols)
    eight = RING * CORES
    shapes = [
        (eight, RING, RING) + block,
        (RING, eight, RING) + block,
        (RING, RING, eight) + block,
    ]
    outs = pl.pallas_call(
        exchange_kernel,
        out_shape=[jax.ShapeDtypeStruct(shape, kind) for shape in shapes] * parts
        + [jax.ShapeDtypeStruct((RING, RING, eight) + tile.shape, tile.dtype)],
        in_specs=[HBM] * parts + [VMEM],
        out_specs=[HBM] * (3 * parts) + [VMEM],
        scratch_shapes=[
            pltpu.SemaphoreType.DMA((parts, eight)),
            pltpu.SemaphoreType.DMA((parts, RING)),
            pltpu.SemaphoreType.DMA((parts,)),
            pltpu.SemaphoreType.DMA((parts, 3)),
            pltpu.SemaphoreType.DMA((3,)),
            pltpu.SemaphoreType.DMA((3,)),
        ],
        compiler_params=pltpu.CompilerParams(
            collective_id=0, has_side_effects=True, vmem_limit_bytes=GRANT
        ),
        name="exchange",
    )(*(send.reshape((eight, RING, RING) + block) for send in sends), tile)
    flat = [out.reshape((-1,) + block) for out in outs[: 3 * parts]]
    groups = [
        [sends[part]] + flat[3 * part : 3 * part + 3] for part in range(parts)
    ]
    return groups, outs[-1]


def place_in_send(place, order):
    one, two, three = (place[axis] for axis in order)
    return ((one * CORES + place["core"]) * RING + two) * RING + three


def place_received(origin, here, order):
    one, two, three = ((origin[axis], here[axis]) for axis in order)
    first = one[0] * CORES + origin["core"]
    same_first = (one[0] == one[1]) & (origin["core"] == here["core"])
    same_two, same_three = two[0] == two[1], three[0] == three[1]
    early = (first * RING + two[0]) * RING + three[0]
    middle = (two[0] * RING * CORES + first) * RING + three[0]
    late = (three[0] * RING + two[0]) * RING * CORES + first
    buffer = jnp.where(
        same_three, jnp.where(same_two, jnp.where(same_first, 0, 1), 2), 3
    )
    at = jnp.where(buffer == 3, late, jnp.where(buffer == 2, middle, early))
    return buffer * 128 + at


def place_of(device):
    row, col = lax.div(device, RING * RING), lax.rem(device, RING * RING)
    return {
        "x": lax.div(row, RING) * 2 + lax.rem(lax.div(col, CORES), 2),
        "y": lax.div(col, RING),
        "z": lax.rem(row, RING),
        "core": lax.rem(col, CORES),
    }


def collect_kernel(source, lefts, rights, kept, *refs):
    groups = [refs[4 * piece : 4 * piece + 4] for piece in range(3)]
    right_out, left_out, items, counts, right_buf, left_buf, sems = refs[12:]
    count = right_buf.shape[0]
    part = left_buf.shape[1]

    def target(at, piece):
        if piece == 2:
            return left_buf.at[at]
        return right_buf.at[at, pl.ds(piece * part, part)]

    def load(piece):
        def body(at):
            code = source[piece * count + at]
            for which, ref in enumerate(groups[piece]):

                @pl.when(code // 128 == which)
                def _():
                    pltpu.make_async_copy(
                        ref.at[code % 128], target(at, piece), sems.at[piece * count + at]
                    ).start()

        pl.loop(0, count)(body)

    def loaded(piece):
        def body(at):
            pltpu.make_async_copy(
                groups[piece][3].at[0], target(at, piece), sems.at[piece * count + at]
            ).wait()

        pl.loop(0, count)(body)

    for piece in (2, 0, 1):
        load(piece)
    for step in range(STEPS):

        def body(slot, found):
            column = lefts[step * count + slot]
            inner = jnp.maximum(column, 0)
            for way in range(WB):
                other = rights[step * count + inner * WB + way]
                out = kept[slot // WA * (KPB + 1) + other + 1]
                items[step, found] = slot * 16384 + (inner * WB + way) * 128 + jnp.maximum(out, 0)
                found += ((column >= 0) & (out >= 0)).astype(jnp.int32)
            return found

        found = lax.fori_loop(0, count, body, jnp.int32(0))
        for lane in range(UNROLL):
            items[step, found + lane] = SPARE
        counts[step] = (found + UNROLL - 1) // UNROLL
    loaded(2)
    save_left = pltpu.make_async_copy(left_buf, left_out, sems.at[3 * count])
    save_left.start()
    loaded(0)
    loaded(1)
    save_right = pltpu.make_async_copy(right_buf, right_out, sems.at[3 * count + 1])
    save_right.start()
    save_left.wait()
    save_right.wait()


def collect(groups, source, lefts, rights, kept):
    count = source.shape[0] // 3
    _, rows, cols = groups[0][0].shape
    kind = groups[0][0].dtype
    right, left = (count, 2 * rows, cols), (count, rows, cols)
    return pl.pallas_call(
        collect_kernel,
        out_shape=[
            jax.ShapeDtypeStruct(right, kind),
            jax.ShapeDtypeStruct(left, kind),
            jax.ShapeDtypeStruct((STEPS, count * WB + UNROLL), jnp.int32),
            jax.ShapeDtypeStruct((STEPS,), jnp.int32),
        ],
        in_specs=[SMEM] * 4 + [HBM] * 12,
        out_specs=[HBM, HBM, SMEM, SMEM],
        scratch_shapes=[
            pltpu.VMEM(right, kind),
            pltpu.VMEM(left, kind),
            pltpu.SemaphoreType.DMA((3 * count + 2,)),
        ],
        compiler_params=pltpu.CompilerParams(vmem_limit_bytes=GRANT),
        name="collect",
    )(source, lefts, rights, kept, *(ref for group in groups for ref in group))


RIGHT_CHUNKS = 8
RELAYED = 3
LEFT_CHUNKS = 4
AHEAD = 2


def spread_kernel(own, right, other, mate_one, mate_two, cross_one, cross_two, before, after, *sems):
    send_sems, before_sems, after_sems, other_sems, cross_sems, late_sems = sems
    row, col = lax.axis_index("row"), lax.axis_index("col")
    rows, cols = lax.axis_size("row"), lax.axis_size("col")
    half = row % RING
    up, down = ((row + 1) % rows, col), ((row + rows - 1) % rows, col)
    up_two, down_two = ((row + 2) % rows, col), ((row + rows - 2) % rows, col)
    twin = (row, (col + cols // 2) % cols)
    mate = (row, col + 1 - 2 * (col % 2))
    cross = (row, (col + cols - 1 + 2 * (col % 2)) % cols)

    barrier = pltpu.get_barrier_semaphore()
    peers = (up, down, up_two, down_two, twin, mate, cross)
    for there in peers:
        pl.semaphore_signal(
            barrier, inc=1, device_id=there, device_id_type=pl.DeviceIdType.MESH
        )
    pl.semaphore_wait(barrier, len(peers))

    right_size = right.shape[0] // RIGHT_CHUNKS
    left_size = own.shape[0] // LEFT_CHUNKS

    def cut(ref, at, size):
        return ref.at[pl.ds(at * size, size)]

    def send(source, target, at, size, send_sem, recv_sem, there):
        return pltpu.make_async_remote_copy(
            src_ref=cut(source, at, size),
            dst_ref=cut(target, at, size),
            send_sem=send_sem,
            recv_sem=recv_sem,
            device_id=there,
            device_id_type=pl.DeviceIdType.MESH,
        )

    def raise_chunk(at):
        return send(right, before, at, right_size, send_sems.at[0, at], before_sems.at[at], up)

    def lower_chunk(at):
        return send(right, after, at, right_size, send_sems.at[1, at], after_sems.at[at], down)

    def relay_up(at):
        return send(after, before, at, right_size, send_sems.at[2, at], before_sems.at[at], up_two)

    def relay_down(at):
        return send(before, after, at, right_size, send_sems.at[2, at], after_sems.at[at], down_two)

    def to_twin(at):
        return send(own, other, at, left_size, send_sems.at[3, at], other_sems.at[at], twin)

    def to_cross(at):
        return send(own, cross_one, at, left_size, send_sems.at[4, at], cross_sems.at[at], cross)

    def to_mate(at):
        return send(own, mate_one, at, left_size, send_sems.at[5, at], late_sems.at[0, at], mate)

    def pass_mate(at):
        return send(other, mate_two, at, left_size, send_sems.at[6, at], late_sems.at[1, at], mate)

    def pass_twin(at):
        return send(
            cross_one, cross_two, at, left_size, send_sems.at[7, at], late_sems.at[2, at], twin
        )

    last = half == RING - 1
    first = half == 0

    def on_right(at, action):
        if at >= RELAYED:
            action(raise_chunk(at))
            action(lower_chunk(at))
        else:

            @pl.when(jnp.logical_not(last))
            def _():
                action(raise_chunk(at))

            @pl.when(jnp.logical_not(first))
            def _():
                action(lower_chunk(at))

    def start(copy):
        copy.start()

    def sent(copy):
        copy.wait_send()

    for at in range(RIGHT_CHUNKS):
        if at >= AHEAD:
            on_right(at - AHEAD, sent)
            if at - AHEAD < LEFT_CHUNKS:
                to_twin(at - AHEAD).wait_send()
        if at < LEFT_CHUNKS:
            to_cross(at).start()
            to_twin(at).start()
            to_mate(at).start()
        else:
            to_cross(at - LEFT_CHUNKS).wait_recv()
            pass_twin(at - LEFT_CHUNKS).start()
        on_right(at, start)
        relay = at - AHEAD
        if 0 <= relay < RELAYED:

            @pl.when(half == RING - 2)
            def _():
                lower_chunk(relay).wait_recv()
                relay_up(relay).start()

            @pl.when(half == 1)
            def _():
                raise_chunk(relay).wait_recv()
                relay_down(relay).start()

        if at >= LEFT_CHUNKS:
            to_twin(at - LEFT_CHUNKS).wait_recv()
            pass_mate(at - LEFT_CHUNKS).start()

    for at in range(RIGHT_CHUNKS - AHEAD, RIGHT_CHUNKS):
        on_right(at, sent)
    for at in range(RELAYED):

        @pl.when(half != 1)
        def _():
            raise_chunk(at).wait_recv()

        @pl.when(half != RING - 2)
        def _():
            lower_chunk(at).wait_recv()

        @pl.when(half == RING - 2)
        def _():
            relay_up(at).wait_send()

        @pl.when(half == 1)
        def _():
            relay_down(at).wait_send()

    for at in range(RELAYED, RIGHT_CHUNKS):
        raise_chunk(at).wait_recv()
        lower_chunk(at).wait_recv()
    for at in range(LEFT_CHUNKS):
        to_mate(at).wait()
        pass_mate(at).wait()
        pass_twin(at).wait()
        to_cross(at).wait_send()
        if at + AHEAD >= RIGHT_CHUNKS:
            to_twin(at).wait_send()


def spread(own, right):
    left_shape = jax.ShapeDtypeStruct(own.shape, own.dtype)
    right_shape = jax.ShapeDtypeStruct(right.shape, right.dtype)
    dma = pltpu.SemaphoreType.DMA
    return pl.pallas_call(
        spread_kernel,
        out_shape=[left_shape] * 5 + [right_shape] * 2,
        in_specs=[HBM] * 2,
        out_specs=[HBM] * 7,
        scratch_shapes=[
            dma((8, RIGHT_CHUNKS)),
            dma((RIGHT_CHUNKS,)),
            dma((RIGHT_CHUNKS,)),
            dma((LEFT_CHUNKS,)),
            dma((LEFT_CHUNKS,)),
            dma((3, LEFT_CHUNKS)),
        ],
        compiler_params=pltpu.CompilerParams(
            collective_id=1, has_side_effects=True, vmem_limit_bytes=GRANT
        ),
        name="spread",
    )(own, right)


def split(value):
    high = value.astype(jnp.bfloat16)
    low = (value - high.astype(jnp.float32)).astype(jnp.bfloat16)
    return high, low


UNROLL = 8
SPARE = 96


def product_kernel(counts, items, *refs):
    lefts = refs[: 2 * STEPS]
    right, before, after, out, left_buf, right_buf, total, load_sems, out_sem = refs[2 * STEPS :]
    outs, edge, _ = out.shape
    col, cols = lax.axis_index("col"), lax.axis_size("col")
    side = 2 * lax.rem(col, 2) - 1
    places = (lax.rem(col + 1, 2), lax.rem(col, 2))
    homes = (col, col - side, lax.rem(col + side + cols, cols))
    order = [lax.div(home, cols // 2) for home in homes]

    def right_load(step, source):
        return pltpu.make_async_copy(source, right_buf.at[step], load_sems.at[2 * STEPS + step])

    left_loads = [
        pltpu.make_async_copy(source, left_buf.at[at], load_sems.at[at])
        for at, source in enumerate(lefts)
    ]
    for step in range(STEPS):
        left_loads[2 * step].start()
        left_loads[2 * step + 1].start()
        if step == 0:
            right_load(0, right).start()
        else:
            for place, source in enumerate((before, after)):

                @pl.when(places[step - 1] == place)
                def _():
                    right_load(step, source).start()

    def clear(at):
        total[at] = jnp.zeros((edge, edge), jnp.float32)

    pl.loop(0, outs + 1)(clear)

    for step in range(STEPS):
        left_loads[2 * step].wait()
        left_loads[2 * step + 1].wait()
        right_load(step, right).wait()
        swap = order[step]

        def body(at):
            codes = [items[step, at * UNROLL + lane] for lane in range(UNROLL)]
            sums = []
            for code in codes:
                slot_a = lax.shift_right_logical(code, 14)
                slot_b = lax.shift_right_logical(code, 7) & 127
                left = jnp.concatenate(
                    [
                        left_buf[2 * step + swap, slot_a],
                        left_buf[2 * step + 1 - swap, slot_a],
                    ],
                    axis=0,
                )
                a_hi, a_lo = split(left)
                b_hi, b_lo = split(right_buf[step, slot_b])
                sums.append(
                    jnp.dot(
                        jnp.concatenate([a_hi, a_lo], axis=1),
                        jnp.concatenate([b_hi, b_hi], axis=0),
                        preferred_element_type=jnp.float32,
                    )
                    + jnp.dot(a_hi, b_lo, preferred_element_type=jnp.float32)
                )
            for code, value in zip(codes, sums):
                total[code & 127] += value

        pl.loop(0, counts[step])(body)
    save = pltpu.make_async_copy(total.at[pl.ds(0, outs)], out, out_sem)
    save.start()
    save.wait()


def products(counts, items, lefts, rights, outs):
    slots_b, edge, _ = rights[0].shape
    slots_a, part, _ = lefts[0].shape
    return pl.pallas_call(
        product_kernel,
        out_shape=jax.ShapeDtypeStruct((outs, edge, edge), jnp.float32),
        in_specs=[SMEM] * 2 + [HBM] * (len(lefts) + len(rights)),
        out_specs=HBM,
        scratch_shapes=[
            pltpu.VMEM((2 * STEPS, slots_a, part, edge), jnp.float32),
            pltpu.VMEM((STEPS, slots_b, edge, edge), jnp.float32),
            pltpu.VMEM((outs + 1, edge, edge), jnp.float32),
            pltpu.SemaphoreType.DMA((3 * STEPS,)),
            pltpu.SemaphoreType.DMA,
        ],
        compiler_params=pltpu.CompilerParams(vmem_limit_bytes=GRANT),
        name="products",
    )(counts, items, *lefts, *rights)


def on_device(a_held, a_slot, a_col, b_held, b_slot, b_col, c_col):
    grid_rows = lax.axis_size("row")
    grid_cols = lax.axis_size("col")
    devices = grid_rows * grid_cols
    copies = grid_cols // grid_rows
    i = lax.axis_index("row")
    c = lax.axis_index("col")
    rows, width = c_col.shape
    hold_a, hold_b = a_slot.shape[0], b_slot.shape[0]
    slots_a, slots_b = rows * WA, KPB * WB

    edge = a_held.shape[1]
    labels = jnp.concatenate([a_slot, a_col, b_slot, b_col])
    tile = jnp.pad(labels, (0, 8 * edge - labels.shape[0])).reshape(8, edge)
    sends, kept = pack((grid_rows, grid_cols), a_slot, b_slot, c_col, a_held, b_held)
    received, labels = exchange(sends, tile)

    labels = labels.reshape(RING, RING, 2, 2, CORES, -1)[..., : 2 * (hold_a + hold_b)]
    labels = labels.transpose(2, 0, 1, 3, 4, 5).reshape(devices, -1)
    parts = [hold_a, 2 * hold_a, 2 * hold_a + hold_b]
    all_a, all_acol, all_b, all_bcol = (part.reshape(-1) for part in jnp.split(labels, parts, axis=1))

    side = 2 * (c % 2) - 1
    turns = jnp.stack([jnp.int32(1), 1 - side, 1 + side])
    k = (i + c + turns) % grid_rows

    def look_up(panels, slots, table, columns, hold):
        wanted = panels[:, None] * slots + jnp.arange(slots, dtype=jnp.int32)[None, :]
        holder = jnp.arange(table.shape[0], dtype=jnp.int32) // hold
        code = holder * 32 + columns + 1
        found = jnp.sum(jnp.where(table[None, None, :] == wanted[:, :, None], code, 0), axis=2)
        return found // 32, found % 32 - 1

    src_left, col_left = look_up(i * grid_rows + k, slots_a, all_a, all_acol, hold_a)
    src_right, col_right = look_up(k * grid_cols + c, slots_b, all_b, all_bcol, hold_b)

    here = place_of(i * grid_cols + c)
    origin = place_of(src_right[0])
    source = [place_received(origin, here, order) for order in ORDERS[:2]]
    source.append(place_received(place_of(src_left[0]), here, ORDERS[2]))
    right, own, items, counts = collect(
        received,
        jnp.concatenate(source),
        col_left.reshape(-1),
        col_right.reshape(-1),
        kept,
    )
    other, mate_one, mate_two, cross_one, cross_two, before, after = spread(own, right)

    lefts = [own, other, mate_one, mate_two, cross_one, cross_two]
    total = products(counts, items, lefts, [right, before, after], rows * width)
    return total.reshape(rows, width, edge, edge)


def solution(mesh):
    return jax.shard_map(
        on_device,
        mesh=mesh,
        in_specs=(
            P(("row", "col"), None, None),
            P(("row", "col")),
            P(("row", "col")),
            P(("row", "col"), None, None),
            P(("row", "col")),
            P(("row", "col")),
            P("row", "col"),
        ),
        out_specs=P("row", "col", None, None),
        check_vma=False,
    )
```

```python
import functools

import jax
import jax.numpy as jnp
from jax import lax
from jax.experimental import pallas as pl
from jax.experimental.pallas import tpu as pltpu
from jax.sharding import PartitionSpec as P

KPB = 16
WA = 4
WB = 4
STEPS = 3
HBM = pl.BlockSpec(memory_space=pltpu.HBM)


def shifted(value, axis, steps):
    count = lax.axis_size(axis)
    pairs = [(source, (source + steps) % count) for source in range(count)]
    return lax.ppermute(value, axis, pairs)


def permuted(value, axis, target):
    count = lax.axis_size(axis)
    return lax.ppermute(value, axis, [(at, target(at) % count) for at in range(count)])


def pack_kernel(
    grid, slots, a_slot, b_slot, a_held, b_held, upper, lower, halves, a_buf, b_buf, sems
):
    grid_rows, grid_cols = grid
    hold_a, hold_b = a_held.shape[0], b_held.shape[0]
    part = halves.shape[1]
    base = hold_a + hold_b

    def load_a(at):
        return pltpu.make_async_copy(a_held.at[at], a_buf.at[at], sems.at[at])

    def load_b(at):
        return pltpu.make_async_copy(b_held.at[at], b_buf.at[at], sems.at[hold_a + at])

    def save_a(at, half, spot):
        return pltpu.make_async_copy(
            a_buf.at[at, pl.ds(half * part, part)], halves.at[spot], sems.at[base + 2 * at + half]
        )

    def save_b(at, half, spot):
        return pltpu.make_async_copy(
            b_buf.at[at, pl.ds(half * part, part)],
            (upper, lower)[half].at[spot],
            sems.at[base + 2 * (hold_a + at) + half],
        )

    pl.loop(0, hold_b)(lambda at: load_b(at).start())
    pl.loop(0, hold_a)(lambda at: load_a(at).start())

    def send_b(at):
        panel = lax.div(b_slot[at], slots[1])
        inner, col = lax.div(panel, grid_cols), lax.rem(panel, grid_cols)
        row = lax.rem(inner - col - 1 + grid_rows + grid_cols, grid_rows)
        place = place_of(row * grid_cols + col)
        load_b(at).wait()
        for half, order in enumerate(ORDERS[:2]):
            save_b(at, half, place_in_send(place, order)).start()

    pl.loop(0, hold_b, unroll=4)(send_b)

    def send_a(at):
        panel = lax.div(a_slot[at], slots[0])
        row, inner = lax.div(panel, grid_rows), lax.rem(panel, grid_rows)
        col = lax.rem(inner - row - 1 + 2 * grid_rows, grid_rows)
        load_a(at).wait()
        for half in range(2):
            place = place_of(row * grid_cols + col + half * grid_rows)
            save_a(at, half, place_in_send(place, ORDERS[2])).start()

    pl.loop(0, hold_a, unroll=4)(send_a)

    for half in range(2):
        pl.loop(0, hold_b)(lambda at: save_b(at, half, 0).wait())
        pl.loop(0, hold_a)(lambda at: save_a(at, half, 0).wait())


GRANT = 60 * 1024 * 1024
SMEM = pl.BlockSpec(memory_space=pltpu.SMEM)
VMEM = pl.BlockSpec(memory_space=pltpu.VMEM)


def pack(grid, slots, a_slot, b_slot, a_held, b_held):
    devices = grid[0] * grid[1]
    edge, cols = a_held.shape[1:]
    send = jax.ShapeDtypeStruct((devices, edge // 2, cols), a_held.dtype)
    return pl.pallas_call(
        functools.partial(pack_kernel, grid, slots),
        out_shape=[send] * 3,
        in_specs=[SMEM] * 2 + [HBM] * 2,
        out_specs=[HBM] * 3,
        scratch_shapes=[
            pltpu.VMEM(a_held.shape, a_held.dtype),
            pltpu.VMEM(b_held.shape, b_held.dtype),
            pltpu.SemaphoreType.DMA((3 * (a_held.shape[0] + b_held.shape[0]),)),
        ],
        compiler_params=pltpu.CompilerParams(vmem_limit_bytes=GRANT),
        name="pack",
    )(a_slot, b_slot, a_held, b_held)


ORDERS = (("x", "y", "z"), ("y", "z", "x"), ("z", "x", "y"))
STEPS_FIRST = (1, 2, 6, 3, 7, 4, 5)
STEPS_LATER = (1, 3, 2)
RING = 4
CORES = 2


def my_place():
    row, col = lax.axis_index("row"), lax.axis_index("col")
    return {
        "x": row // RING * 2 + col // CORES % 2,
        "y": col // RING,
        "z": row % RING,
        "core": col % CORES,
    }


def coords_of(place):
    row = place["x"] // 2 * RING + place["z"]
    col = place["y"] * RING + place["x"] % 2 * CORES + place["core"]
    return row, col


def exchange_kernel(*refs):
    parts = len(ORDERS)
    sends, refs = refs[:parts], refs[parts:]
    tile, refs = refs[0], refs[1:]
    stages = [refs[3 * part : 3 * part + 3] for part in range(parts)]
    labels = refs[3 * parts]
    first_recv, second_recv, third_recv, send_sems, label_send, label_recv = refs[3 * parts + 1 :]
    place = my_place()

    def moved(axis, steps, flip):
        there = dict(place)
        there[axis] = (place[axis] + steps) % RING
        there["core"] = (place["core"] + flip) % CORES
        return there

    def copy(source, target, send_sem, recv_sem, there):
        return pltpu.make_async_remote_copy(
            src_ref=source,
            dst_ref=target,
            send_sem=send_sem,
            recv_sem=recv_sem,
            device_id=coords_of(there),
            device_id_type=pl.DeviceIdType.MESH,
        )

    def spot(there, axis):
        return there[axis] * CORES + there["core"]

    def arrived(like, sem):
        pltpu.make_async_copy(like, like, sem).wait()

    peers = [moved("x", 0, 1)]
    for axis in ("x", "y", "z"):
        for steps in range(1, RING):
            for flip in range(CORES):
                peers.append(moved(axis, steps, flip))
    barrier = pltpu.get_barrier_semaphore()
    for there in peers:
        pl.semaphore_signal(
            barrier, inc=1, device_id=coords_of(there), device_id_type=pl.DeviceIdType.MESH
        )
    pl.semaphore_wait(barrier, len(peers))

    x, y, z = spot(place, "x"), place["y"], place["z"]
    labels[z, y, x] = tile[...]
    for steps in STEPS_FIRST:
        copy(
            labels.at[z, y, x],
            labels.at[z, y, x],
            label_send.at[0],
            label_recv.at[0],
            moved("x", steps // CORES, steps % CORES),
        ).start()
    for steps in STEPS_FIRST:
        for part, (one, two, three) in enumerate(ORDERS):
            there = moved(one, steps // CORES, steps % CORES)
            copy(
                sends[part].at[spot(there, one)],
                stages[part][0].at[spot(place, one)],
                send_sems.at[part, 0],
                first_recv.at[part, steps],
                there,
            ).start()
    arrived(labels.at[0, 0, pl.ds(0, 7)], label_recv.at[0])
    for steps in STEPS_LATER:
        copy(
            labels.at[z, y], labels.at[z, y], label_send.at[1], label_recv.at[1], moved("y", steps, 0)
        ).start()
    arrived(labels.at[0, pl.ds(0, 3)], label_recv.at[1])
    for steps in STEPS_LATER:
        copy(
            labels.at[z], labels.at[z], label_send.at[2], label_recv.at[2], moved("z", steps, 0)
        ).start()

    for steps in (0,) + STEPS_FIRST:
        for part, (one, two, three) in enumerate(ORDERS):
            origin = spot(moved(one, RING - steps // CORES, steps % CORES), one)
            if steps:
                source = stages[part][0]
                arrived(source.at[0], first_recv.at[part, steps])
            else:
                source = sends[part]
            for later in STEPS_LATER:
                there = moved(two, later, 0)
                copy(
                    source.at[origin, there[two]],
                    stages[part][1].at[place[two], origin],
                    send_sems.at[part, 1],
                    second_recv.at[part, later],
                    there,
                ).start()

    def last(part, source, target, there):
        copy(source, target, send_sems.at[part, 2], third_recv.at[part], there).start()

    for part, (one, two, three) in enumerate(ORDERS):
        for steps in (0,) + STEPS_FIRST:
            origin = spot(moved(one, RING - steps // CORES, steps % CORES), one)
            source = stages[part][0] if steps else sends[part]
            for later in STEPS_LATER:
                there = moved(three, later, 0)
                last(
                    part,
                    source.at[origin, place[two], there[three]],
                    stages[part][2].at[place[three], place[two], origin],
                    there,
                )
    for steps in STEPS_LATER:
        for part, (one, two, three) in enumerate(ORDERS):
            origin = moved(two, RING - steps, 0)[two]
            arrived(stages[part][1].at[0], second_recv.at[part, steps])
            for later in STEPS_LATER:
                there = moved(three, later, 0)
                last(
                    part,
                    stages[part][1].at[origin, :, there[three]],
                    stages[part][2].at[place[three], origin],
                    there,
                )
    for part in range(parts):
        arrived(stages[part][2].at[pl.ds(0, 3)], third_recv.at[part])
        arrived(sends[part].at[pl.ds(0, 7)], send_sems.at[part, 0])
        arrived(stages[part][2].at[pl.ds(0, 3)], send_sems.at[part, 1])
        arrived(stages[part][2].at[pl.ds(0, 3)], send_sems.at[part, 2])
    arrived(labels.at[pl.ds(0, 3)], label_recv.at[2])
    arrived(labels.at[0, 0, pl.ds(0, 7)], label_send.at[0])
    arrived(labels.at[0, pl.ds(0, 3)], label_send.at[1])
    arrived(labels.at[pl.ds(0, 3)], label_send.at[2])


def exchange(sends, tile):
    parts = len(sends)
    _, rows, cols = sends[0].shape
    kind = sends[0].dtype
    block = (rows, cols)
    eight = RING * CORES
    shapes = [
        (eight, RING, RING) + block,
        (RING, eight, RING) + block,
        (RING, RING, eight) + block,
    ]
    outs = pl.pallas_call(
        exchange_kernel,
        out_shape=[jax.ShapeDtypeStruct(shape, kind) for shape in shapes] * parts
        + [jax.ShapeDtypeStruct((RING, RING, eight) + tile.shape, tile.dtype)],
        in_specs=[HBM] * parts + [VMEM],
        out_specs=[HBM] * (3 * parts) + [VMEM],
        scratch_shapes=[
            pltpu.SemaphoreType.DMA((parts, eight)),
            pltpu.SemaphoreType.DMA((parts, RING)),
            pltpu.SemaphoreType.DMA((parts,)),
            pltpu.SemaphoreType.DMA((parts, 3)),
            pltpu.SemaphoreType.DMA((3,)),
            pltpu.SemaphoreType.DMA((3,)),
        ],
        compiler_params=pltpu.CompilerParams(
            collective_id=0, has_side_effects=True, vmem_limit_bytes=GRANT
        ),
        name="exchange",
    )(*(send.reshape((eight, RING, RING) + block) for send in sends), tile)
    flat = [out.reshape((-1,) + block) for out in outs[: 3 * parts]]
    groups = [
        [sends[part]] + flat[3 * part : 3 * part + 3] for part in range(parts)
    ]
    return groups, outs[-1]


def place_in_send(place, order):
    one, two, three = (place[axis] for axis in order)
    return ((one * CORES + place["core"]) * RING + two) * RING + three


def place_received(origin, here, order):
    one, two, three = ((origin[axis], here[axis]) for axis in order)
    first = one[0] * CORES + origin["core"]
    same_first = (one[0] == one[1]) & (origin["core"] == here["core"])
    same_two, same_three = two[0] == two[1], three[0] == three[1]
    early = (first * RING + two[0]) * RING + three[0]
    middle = (two[0] * RING * CORES + first) * RING + three[0]
    late = (three[0] * RING + two[0]) * RING * CORES + first
    buffer = jnp.where(
        same_three, jnp.where(same_two, jnp.where(same_first, 0, 1), 2), 3
    )
    at = jnp.where(buffer == 3, late, jnp.where(buffer == 2, middle, early))
    return buffer * 128 + at


def place_of(device):
    row, col = lax.div(device, RING * RING), lax.rem(device, RING * RING)
    return {
        "x": lax.div(row, RING) * 2 + lax.rem(lax.div(col, CORES), 2),
        "y": lax.div(col, RING),
        "z": lax.rem(row, RING),
        "core": lax.rem(col, CORES),
    }


def collect_kernel(pieces, source, *refs):
    groups = [refs[4 * piece : 4 * piece + 4] for piece in range(pieces)]
    buf, sems = refs[-2:]
    outs = refs[4 * pieces : -2]
    count, rows, _ = buf.shape
    part = rows // pieces
    chunk = count // len(outs)

    def target(at, piece):
        return buf.at[at, pl.ds(piece * part, part)]

    def load(at):
        for piece, group in enumerate(groups):
            code = source[piece, at]
            for which, ref in enumerate(group):

                @pl.when(code // 128 == which)
                def _():
                    pltpu.make_async_copy(
                        ref.at[code % 128], target(at, piece), sems.at[piece * count + at]
                    ).start()

    def loaded(at):
        for piece, group in enumerate(groups):
            pltpu.make_async_copy(
                group[3].at[0], target(at, piece), sems.at[piece * count + at]
            ).wait()

    pl.loop(0, count, unroll=2)(load)
    saves = [
        pltpu.make_async_copy(
            buf.at[pl.ds(part * chunk, chunk)], out, sems.at[pieces * count + part]
        )
        for part, out in enumerate(outs)
    ]
    for at, save in enumerate(saves):
        pl.loop(at * chunk, (at + 1) * chunk)(loaded)
        save.start()
    for save in saves:
        save.wait()


def collect(groups, source, chunks):
    pieces = len(groups)
    count = source.shape[1]
    _, rows, cols = groups[0][0].shape
    kind = groups[0][0].dtype
    part = jax.ShapeDtypeStruct((count // chunks, pieces * rows, cols), kind)
    return pl.pallas_call(
        functools.partial(collect_kernel, pieces),
        out_shape=[part] * chunks,
        in_specs=[SMEM] + [HBM] * (4 * pieces),
        out_specs=[HBM] * chunks,
        scratch_shapes=[
            pltpu.VMEM((count, pieces * rows, cols), kind),
            pltpu.SemaphoreType.DMA((pieces * count + chunks,)),
        ],
        compiler_params=pltpu.CompilerParams(vmem_limit_bytes=GRANT),
        name="collect",
    )(source, *(ref for group in groups for ref in group))


def split(value):
    high = value.astype(jnp.bfloat16)
    low = (value - high.astype(jnp.float32)).astype(jnp.bfloat16)
    return high, low


def product_kernel(pieces, parts, first, unroll, counts, items, order, *refs):
    lefts = refs[: 2 * pieces]
    rights = refs[2 * pieces : 2 * pieces + parts]
    refs = refs[2 * pieces + parts :]
    if not first:
        before, refs = refs[0], refs[1:]
    out, left_buf, right_buf, total, load_sems, out_sem = refs
    outs, edge, _ = out.shape
    slots_a = lefts[0].shape[0]
    slots_b = rights[0].shape[0]

    loads = [
        pltpu.make_async_copy(source, left_buf.at[at], load_sems.at[at])
        for at, source in enumerate(lefts)
    ] + [
        pltpu.make_async_copy(
            source, right_buf.at[pl.ds(at * slots_b, slots_b)], load_sems.at[2 * pieces + at]
        )
        for at, source in enumerate(rights)
    ]
    if not first:
        restore = pltpu.make_async_copy(before, total.at[pl.ds(0, outs)], out_sem)
        restore.start()
    for load in loads:
        load.start()
    if first:

        def clear(at):
            total[at] = jnp.zeros((edge, edge), jnp.float32)

        pl.loop(0, outs)(clear)
    else:
        restore.wait()
    for load in loads:
        load.wait()

    def step(at):
        codes = [items[at * unroll + lane] for lane in range(unroll)]
        sums = []
        for code in codes:
            slot_a = code // 16384
            slot_b = (code // 128) % 128
            piece = slot_a // slots_a
            swap = order[piece]
            slot_a = slot_a % slots_a
            left = jnp.concatenate(
                [
                    left_buf[2 * piece + swap, slot_a],
                    left_buf[2 * piece + 1 - swap, slot_a],
                ],
                axis=0,
            )
            a_hi, a_lo = split(left)
            b_hi, b_lo = split(right_buf[slot_b])
            sums.append(
                jnp.dot(
                    jnp.concatenate([a_hi, a_lo], axis=1),
                    jnp.concatenate([b_hi, b_hi], axis=0),
                    preferred_element_type=jnp.float32,
                )
                + jnp.dot(a_hi, b_lo, preferred_element_type=jnp.float32)
            )
        for code, value in zip(codes, sums):
            total[code % 128] += value

    pl.loop(0, counts[0])(step)
    save = pltpu.make_async_copy(total.at[pl.ds(0, outs)], out, out_sem)
    save.start()
    save.wait()


UNROLL = 8
CHUNKS = 2


def products(counts, items, order, halves, rights, before, outs):
    pieces, parts = len(halves) // 2, len(rights)
    slots_b, edge, _ = rights[0].shape
    slots_a, part, _ = halves[0].shape
    first = before is None
    extra = [] if first else [before]
    return pl.pallas_call(
        functools.partial(product_kernel, pieces, parts, first, UNROLL),
        out_shape=jax.ShapeDtypeStruct((outs, edge, edge), jnp.float32),
        in_specs=[SMEM] * 3 + [HBM] * (2 * pieces + parts + len(extra)),
        out_specs=HBM,
        scratch_shapes=[
            pltpu.VMEM((2 * pieces, slots_a, part, edge), jnp.float32),
            pltpu.VMEM((parts * slots_b, edge, edge), jnp.float32),
            pltpu.VMEM((outs + 1, edge, edge), jnp.float32),
            pltpu.SemaphoreType.DMA((2 * pieces + parts,)),
            pltpu.SemaphoreType.DMA,
        ],
        compiler_params=pltpu.CompilerParams(vmem_limit_bytes=GRANT),
        cost_estimate=pl.CostEstimate(
            flops=pieces * 600_000_000, bytes_accessed=pieces * 8_000_000, transcendentals=0
        ),
        name="products",
    )(counts, items, order, *halves, *rights, *extra)


def work_list(lefts, rights, places, kept, first_row):
    rows, width = kept.shape
    pieces, inner, _ = rights.shape
    outs = rows * width
    slots = rows * WA
    rel = lefts - first_row
    here = rel[:, :, None] == jnp.arange(inner, dtype=jnp.int32)
    chosen = (
        jnp.sum(jnp.where(here[:, :, :, None], rights[:, None, :, :] + 1, 0), axis=2) - 1
    )
    at_row = jnp.repeat(kept, WA, axis=0)
    match = (chosen[:, :, :, None] == at_row[None, :, None, :]) & (chosen >= 0)[:, :, :, None]
    target = jnp.sum(jnp.where(match, jnp.arange(width, dtype=jnp.int32) + 1, 0), axis=3) - 1
    live = target >= 0
    slot = jnp.arange(slots, dtype=jnp.int32)[None, :, None]
    slot_a = slot + slots * jnp.arange(pieces, dtype=jnp.int32)[:, None, None]
    slot_b = (places[:, None, None] * inner + rel[:, :, None]) * WB + jnp.arange(WB, dtype=jnp.int32)
    code = slot_a * 16384 + slot_b * 128 + slot // WA * width + target
    live, code = live.reshape(-1), code.reshape(-1)
    spot = jnp.cumsum(live.astype(jnp.int32)) - 1
    place = jnp.arange(live.shape[0], dtype=jnp.int32)
    here = live[None, :] & (spot[None, :] == place[:, None])
    packed = jnp.sum(jnp.where(here, code[None, :] - outs, 0), axis=1) + outs
    count = (jnp.sum(live.astype(jnp.int32)) + UNROLL - 1) // UNROLL
    return count[None], packed


def on_device(a_held, a_slot, a_col, b_held, b_slot, b_col, c_col):
    grid_rows = lax.axis_size("row")
    grid_cols = lax.axis_size("col")
    devices = grid_rows * grid_cols
    copies = grid_cols // grid_rows
    i = lax.axis_index("row")
    c = lax.axis_index("col")
    rows, width = c_col.shape
    hold_a, hold_b = a_slot.shape[0], b_slot.shape[0]
    slots_a, slots_b = rows * WA, KPB * WB

    edge = a_held.shape[1]
    labels = jnp.concatenate([a_slot, a_col, b_slot, b_col])
    tile = jnp.pad(labels, (0, 8 * edge - labels.shape[0])).reshape(8, edge)
    grid, slots = (grid_rows, grid_cols), (slots_a, slots_b)
    sends = pack(grid, slots, a_slot, b_slot, a_held, b_held)
    received, labels = exchange(sends, tile)

    labels = labels.reshape(RING, RING, 2, 2, CORES, -1)[..., : 2 * (hold_a + hold_b)]
    labels = labels.transpose(2, 0, 1, 3, 4, 5).reshape(devices, -1)
    parts = [hold_a, 2 * hold_a, 2 * hold_a + hold_b]
    all_a, all_acol, all_b, all_bcol = (part.reshape(-1) for part in jnp.split(labels, parts, axis=1))

    side = 2 * (c % 2) - 1
    turns = jnp.stack([jnp.int32(1), 1 - side, 1 + side])
    k = (i + c + turns) % grid_rows

    def look_up(panels, slots, table, columns, hold):
        wanted = panels[:, None] * slots + jnp.arange(slots, dtype=jnp.int32)[None, :]
        holder = jnp.arange(table.shape[0], dtype=jnp.int32) // hold
        code = holder * 32 + columns + 1
        found = jnp.sum(jnp.where(table[None, None, :] == wanted[:, :, None], code, 0), axis=2)
        return found // 32, found % 32 - 1

    src_left, col_left = look_up(i * grid_rows + k, slots_a, all_a, all_acol, hold_a)
    src_right, col_right = look_up(k * grid_cols + c, slots_b, all_b, all_bcol, hold_b)

    here = place_of(i * grid_cols + c)
    origin = place_of(src_right[0])
    source = jnp.stack([place_received(origin, here, order) for order in ORDERS[:2]])
    right = collect(received[:2], source, CHUNKS)
    (own,) = collect(received[2:], place_received(place_of(src_left[0]), here, ORDERS[2])[None], 1)
    other = shifted(own, "col", grid_rows)
    cross = permuted(own, "col", lambda at: ((at - 1) ^ 1) + 1)
    mate_first = permuted(own, "col", lambda at: at ^ 1)
    mate_second = permuted(other, "col", lambda at: at ^ 1)
    cross_second = shifted(cross, "col", grid_rows)
    homes = (c + jnp.stack([jnp.int32(0), -side, side])) % grid_cols
    order = (homes >= grid_rows).astype(jnp.int32)

    outs = rows * width
    tables = col_right.reshape(STEPS, KPB, WB)
    count, items = work_list(col_left[:1], tables[:1], jnp.zeros((1,), jnp.int32), c_col, 0)
    total = products(count, items, order[:1], [own, other], right, None, outs)
    places = jnp.stack([(1 - side) // 2, (1 + side) // 2])
    lefts = [mate_first, mate_second, cross, cross_second]
    chunk = slots_b // CHUNKS
    for at in range(CHUNKS):
        shifts = [shifted(right[at], "row", 1), shifted(right[at], "row", -1)]
        first, last = at * chunk // WB, (at + 1) * chunk // WB
        count, items = work_list(col_left[1:], tables[1:, first:last], places, c_col, first)
        total = products(count, items, order[1:], lefts, shifts, total, outs)
    return total.reshape(rows, width, edge, edge)


def solution(mesh):
    return jax.shard_map(
        on_device,
        mesh=mesh,
        in_specs=(
            P(("row", "col"), None, None),
            P(("row", "col")),
            P(("row", "col")),
            P(("row", "col"), None, None),
            P(("row", "col")),
            P(("row", "col")),
            P("row", "col"),
        ),
        out_specs=P("row", "col", None, None),
        check_vma=False,
    )
```

```python
import functools

import jax
import jax.numpy as jnp
from jax import lax
from jax.experimental import pallas as pl
from jax.experimental.pallas import tpu as pltpu
from jax.sharding import PartitionSpec as P

KPB = 16
WA = 4
WB = 4
STEPS = 3
HBM = pl.BlockSpec(memory_space=pltpu.HBM)


def shifted(value, axis, steps):
    count = lax.axis_size(axis)
    pairs = [(source, (source + steps) % count) for source in range(count)]
    return lax.ppermute(value, axis, pairs)


def permuted(value, axis, target):
    count = lax.axis_size(axis)
    return lax.ppermute(value, axis, [(at, target(at) % count) for at in range(count)])


def pack_kernel(
    grid, slots, a_slot, b_slot, a_held, b_held, upper, lower, halves, a_buf, b_buf, sems
):
    grid_rows, grid_cols = grid
    hold_a, hold_b = a_held.shape[0], b_held.shape[0]
    part = halves.shape[1]
    base = hold_a + hold_b

    def load_a(at):
        return pltpu.make_async_copy(a_held.at[at], a_buf.at[at], sems.at[at])

    def load_b(at):
        return pltpu.make_async_copy(b_held.at[at], b_buf.at[at], sems.at[hold_a + at])

    def save_a(at, half, spot):
        return pltpu.make_async_copy(
            a_buf.at[at, pl.ds(half * part, part)], halves.at[spot], sems.at[base + 2 * at + half]
        )

    def save_b(at, half, spot):
        return pltpu.make_async_copy(
            b_buf.at[at, pl.ds(half * part, part)],
            (upper, lower)[half].at[spot],
            sems.at[base + 2 * (hold_a + at) + half],
        )

    pl.loop(0, hold_b)(lambda at: load_b(at).start())
    pl.loop(0, hold_a)(lambda at: load_a(at).start())

    def send_b(at):
        inner, col = over(over(b_slot[at], slots[1])[0], grid_cols)
        row = (inner - col - 1 + grid_rows + grid_cols) & (grid_rows - 1)
        place = place_of(row * grid_cols + col)
        load_b(at).wait()
        for half, order in enumerate(ORDERS[:2]):
            save_b(at, half, place_in_send(place, order)).start()

    pl.loop(0, hold_b, unroll=4)(send_b)

    def send_a(at):
        row, inner = over(over(a_slot[at], slots[0])[0], grid_rows)
        col = (inner - row - 1 + 2 * grid_rows) & (grid_rows - 1)
        load_a(at).wait()
        for half in range(2):
            place = place_of(row * grid_cols + col + half * grid_rows)
            save_a(at, half, place_in_send(place, ORDERS[2])).start()

    pl.loop(0, hold_a, unroll=4)(send_a)

    for half in range(2):
        pl.loop(0, hold_b)(lambda at: save_b(at, half, 0).wait())
        pl.loop(0, hold_a)(lambda at: save_a(at, half, 0).wait())


GRANT = 60 * 1024 * 1024
SMEM = pl.BlockSpec(memory_space=pltpu.SMEM)
VMEM = pl.BlockSpec(memory_space=pltpu.VMEM)


def pack(grid, slots, a_slot, b_slot, a_held, b_held):
    devices = grid[0] * grid[1]
    edge, cols = a_held.shape[1:]
    send = jax.ShapeDtypeStruct((devices, edge // 2, cols), a_held.dtype)
    return pl.pallas_call(
        functools.partial(pack_kernel, grid, slots),
        out_shape=[send] * 3,
        in_specs=[SMEM] * 2 + [HBM] * 2,
        out_specs=[HBM] * 3,
        scratch_shapes=[
            pltpu.VMEM(a_held.shape, a_held.dtype),
            pltpu.VMEM(b_held.shape, b_held.dtype),
            pltpu.SemaphoreType.DMA((3 * (a_held.shape[0] + b_held.shape[0]),)),
        ],
        compiler_params=pltpu.CompilerParams(vmem_limit_bytes=GRANT),
        name="pack",
    )(a_slot, b_slot, a_held, b_held)


ORDERS = (("x", "y", "z"), ("y", "z", "x"), ("z", "x", "y"))
STEPS_FIRST = (1, 2, 6, 3, 7, 4, 5)
STEPS_LATER = (1, 3, 2)
RING = 4
CORES = 2


def my_place():
    row, col = lax.axis_index("row"), lax.axis_index("col")
    return {
        "x": row // RING * 2 + col // CORES % 2,
        "y": col // RING,
        "z": row % RING,
        "core": col % CORES,
    }


def coords_of(place):
    row = place["x"] // 2 * RING + place["z"]
    col = place["y"] * RING + place["x"] % 2 * CORES + place["core"]
    return row, col


def exchange_kernel(*refs):
    parts = len(ORDERS)
    sends, refs = refs[:parts], refs[parts:]
    tile, refs = refs[0], refs[1:]
    stages = [refs[3 * part : 3 * part + 3] for part in range(parts)]
    labels = refs[3 * parts]
    first_recv, second_recv, third_recv, send_sems, label_send, label_recv = refs[3 * parts + 1 :]
    place = my_place()

    def moved(axis, steps, flip):
        there = dict(place)
        there[axis] = (place[axis] + steps) % RING
        there["core"] = (place["core"] + flip) % CORES
        return there

    def copy(source, target, send_sem, recv_sem, there):
        return pltpu.make_async_remote_copy(
            src_ref=source,
            dst_ref=target,
            send_sem=send_sem,
            recv_sem=recv_sem,
            device_id=coords_of(there),
            device_id_type=pl.DeviceIdType.MESH,
        )

    def spot(there, axis):
        return there[axis] * CORES + there["core"]

    def arrived(like, sem):
        pltpu.make_async_copy(like, like, sem).wait()

    peers = [moved("x", 0, 1)]
    for axis in ("x", "y", "z"):
        for steps in range(1, RING):
            for flip in range(CORES):
                peers.append(moved(axis, steps, flip))
    barrier = pltpu.get_barrier_semaphore()
    for there in peers:
        pl.semaphore_signal(
            barrier, inc=1, device_id=coords_of(there), device_id_type=pl.DeviceIdType.MESH
        )
    pl.semaphore_wait(barrier, len(peers))

    x, y, z = spot(place, "x"), place["y"], place["z"]
    labels[z, y, x] = tile[...]
    for steps in STEPS_FIRST:
        copy(
            labels.at[z, y, x],
            labels.at[z, y, x],
            label_send.at[0],
            label_recv.at[0],
            moved("x", steps // CORES, steps % CORES),
        ).start()
    for steps in STEPS_FIRST:
        for part, (one, two, three) in enumerate(ORDERS):
            there = moved(one, steps // CORES, steps % CORES)
            copy(
                sends[part].at[spot(there, one)],
                stages[part][0].at[spot(place, one)],
                send_sems.at[part, 0],
                first_recv.at[part, steps],
                there,
            ).start()
    arrived(labels.at[0, 0, pl.ds(0, 7)], label_recv.at[0])
    for steps in STEPS_LATER:
        copy(
            labels.at[z, y], labels.at[z, y], label_send.at[1], label_recv.at[1], moved("y", steps, 0)
        ).start()
    arrived(labels.at[0, pl.ds(0, 3)], label_recv.at[1])
    for steps in STEPS_LATER:
        copy(
            labels.at[z], labels.at[z], label_send.at[2], label_recv.at[2], moved("z", steps, 0)
        ).start()

    for steps in (0,) + STEPS_FIRST:
        for part, (one, two, three) in enumerate(ORDERS):
            origin = spot(moved(one, RING - steps // CORES, steps % CORES), one)
            if steps:
                source = stages[part][0]
                arrived(source.at[0], first_recv.at[part, steps])
            else:
                source = sends[part]
            for later in STEPS_LATER:
                there = moved(two, later, 0)
                copy(
                    source.at[origin, there[two]],
                    stages[part][1].at[place[two], origin],
                    send_sems.at[part, 1],
                    second_recv.at[part, later],
                    there,
                ).start()

    def last(part, source, target, there):
        copy(source, target, send_sems.at[part, 2], third_recv.at[part], there).start()

    for part, (one, two, three) in enumerate(ORDERS):
        for steps in (0,) + STEPS_FIRST:
            origin = spot(moved(one, RING - steps // CORES, steps % CORES), one)
            source = stages[part][0] if steps else sends[part]
            for later in STEPS_LATER:
                there = moved(three, later, 0)
                last(
                    part,
                    source.at[origin, place[two], there[three]],
                    stages[part][2].at[place[three], place[two], origin],
                    there,
                )
    for steps in STEPS_LATER:
        for part, (one, two, three) in enumerate(ORDERS):
            origin = moved(two, RING - steps, 0)[two]
            arrived(stages[part][1].at[0], second_recv.at[part, steps])
            for later in STEPS_LATER:
                there = moved(three, later, 0)
                last(
                    part,
                    stages[part][1].at[origin, :, there[three]],
                    stages[part][2].at[place[three], origin],
                    there,
                )
    for part in range(parts):
        arrived(stages[part][2].at[pl.ds(0, 3)], third_recv.at[part])
        arrived(sends[part].at[pl.ds(0, 7)], send_sems.at[part, 0])
        arrived(stages[part][2].at[pl.ds(0, 3)], send_sems.at[part, 1])
        arrived(stages[part][2].at[pl.ds(0, 3)], send_sems.at[part, 2])
    arrived(labels.at[pl.ds(0, 3)], label_recv.at[2])
    arrived(labels.at[0, 0, pl.ds(0, 7)], label_send.at[0])
    arrived(labels.at[0, pl.ds(0, 3)], label_send.at[1])
    arrived(labels.at[pl.ds(0, 3)], label_send.at[2])


def exchange(sends, tile):
    parts = len(sends)
    _, rows, cols = sends[0].shape
    kind = sends[0].dtype
    block = (rows, cols)
    eight = RING * CORES
    shapes = [
        (eight, RING, RING) + block,
        (RING, eight, RING) + block,
        (RING, RING, eight) + block,
    ]
    outs = pl.pallas_call(
        exchange_kernel,
        out_shape=[jax.ShapeDtypeStruct(shape, kind) for shape in shapes] * parts
        + [jax.ShapeDtypeStruct((RING, RING, eight) + tile.shape, tile.dtype)],
        in_specs=[HBM] * parts + [VMEM],
        out_specs=[HBM] * (3 * parts) + [VMEM],
        scratch_shapes=[
            pltpu.SemaphoreType.DMA((parts, eight)),
            pltpu.SemaphoreType.DMA((parts, RING)),
            pltpu.SemaphoreType.DMA((parts,)),
            pltpu.SemaphoreType.DMA((parts, 3)),
            pltpu.SemaphoreType.DMA((3,)),
            pltpu.SemaphoreType.DMA((3,)),
        ],
        compiler_params=pltpu.CompilerParams(
            collective_id=0, has_side_effects=True, vmem_limit_bytes=GRANT
        ),
        name="exchange",
    )(*(send.reshape((eight, RING, RING) + block) for send in sends), tile)
    flat = [out.reshape((-1,) + block) for out in outs[: 3 * parts]]
    groups = [
        [sends[part]] + flat[3 * part : 3 * part + 3] for part in range(parts)
    ]
    return groups, outs[-1]


def place_in_send(place, order):
    one, two, three = (place[axis] for axis in order)
    return ((one * CORES + place["core"]) * RING + two) * RING + three


def place_received(origin, here, order):
    one, two, three = ((origin[axis], here[axis]) for axis in order)
    first = one[0] * CORES + origin["core"]
    same_first = (one[0] == one[1]) & (origin["core"] == here["core"])
    same_two, same_three = two[0] == two[1], three[0] == three[1]
    early = (first * RING + two[0]) * RING + three[0]
    middle = (two[0] * RING * CORES + first) * RING + three[0]
    late = (three[0] * RING + two[0]) * RING * CORES + first
    buffer = jnp.where(
        same_three, jnp.where(same_two, jnp.where(same_first, 0, 1), 2), 3
    )
    at = jnp.where(buffer == 3, late, jnp.where(buffer == 2, middle, early))
    return buffer * 128 + at


def over(value, size):
    return lax.shift_right_logical(value, jnp.int32(size.bit_length() - 1)), value & (size - 1)


def place_of(device):
    row, col = over(device, RING * RING)
    x_high, z = over(row, RING)
    y, rest = over(col, RING)
    x_low, core = over(rest, CORES)
    return {"x": x_high * 2 + x_low, "y": y, "z": z, "core": core}


def collect_kernel(pieces, source, *refs):
    groups = [refs[4 * piece : 4 * piece + 4] for piece in range(pieces)]
    buf, sems = refs[-2:]
    outs = refs[4 * pieces : -2]
    count, rows, _ = buf.shape
    part = rows // pieces
    chunk = count // len(outs)

    def target(at, piece):
        return buf.at[at, pl.ds(piece * part, part)]

    def load(at):
        for piece, group in enumerate(groups):
            code = source[piece, at]
            for which, ref in enumerate(group):

                @pl.when(code // 128 == which)
                def _():
                    pltpu.make_async_copy(
                        ref.at[code % 128], target(at, piece), sems.at[piece * count + at]
                    ).start()

    def loaded(at):
        for piece, group in enumerate(groups):
            pltpu.make_async_copy(
                group[3].at[0], target(at, piece), sems.at[piece * count + at]
            ).wait()

    pl.loop(0, count, unroll=2)(load)
    saves = [
        pltpu.make_async_copy(
            buf.at[pl.ds(part * chunk, chunk)], out, sems.at[pieces * count + part]
        )
        for part, out in enumerate(outs)
    ]
    for at, save in enumerate(saves):
        pl.loop(at * chunk, (at + 1) * chunk)(loaded)
        save.start()
    for save in saves:
        save.wait()


def collect(groups, source, chunks):
    pieces = len(groups)
    count = source.shape[1]
    _, rows, cols = groups[0][0].shape
    kind = groups[0][0].dtype
    part = jax.ShapeDtypeStruct((count // chunks, pieces * rows, cols), kind)
    return pl.pallas_call(
        functools.partial(collect_kernel, pieces),
        out_shape=[part] * chunks,
        in_specs=[SMEM] + [HBM] * (4 * pieces),
        out_specs=[HBM] * chunks,
        scratch_shapes=[
            pltpu.VMEM((count, pieces * rows, cols), kind),
            pltpu.SemaphoreType.DMA((pieces * count + chunks,)),
        ],
        compiler_params=pltpu.CompilerParams(vmem_limit_bytes=GRANT),
        name="collect",
    )(source, *(ref for group in groups for ref in group))


def split(value):
    high = value.astype(jnp.bfloat16)
    low = (value - high.astype(jnp.float32)).astype(jnp.bfloat16)
    return high, low


def product_kernel(pieces, parts, first, unroll, counts, items, order, *refs):
    lefts = refs[: 2 * pieces]
    rights = refs[2 * pieces : 2 * pieces + parts]
    refs = refs[2 * pieces + parts :]
    if not first:
        before, refs = refs[0], refs[1:]
    out, left_buf, right_buf, total, load_sems, out_sem = refs
    outs, edge, _ = out.shape
    slots_a = lefts[0].shape[0]
    slots_b = rights[0].shape[0]

    loads = [
        pltpu.make_async_copy(source, left_buf.at[at], load_sems.at[at])
        for at, source in enumerate(lefts)
    ] + [
        pltpu.make_async_copy(
            source, right_buf.at[pl.ds(at * slots_b, slots_b)], load_sems.at[2 * pieces + at]
        )
        for at, source in enumerate(rights)
    ]
    if not first:
        restore = pltpu.make_async_copy(before, total.at[pl.ds(0, outs)], out_sem)
        restore.start()
    for load in loads:
        load.start()
    if first:

        def clear(at):
            total[at] = jnp.zeros((edge, edge), jnp.float32)

        pl.loop(0, outs)(clear)
    else:
        restore.wait()
    for load in loads:
        load.wait()

    def step(at):
        codes = [items[at * unroll + lane] for lane in range(unroll)]
        sums = []
        for code in codes:
            slot_a = code // 16384
            slot_b = (code // 128) % 128
            piece = slot_a // slots_a
            swap = order[piece]
            slot_a = slot_a % slots_a
            left = jnp.concatenate(
                [
                    left_buf[2 * piece + swap, slot_a],
                    left_buf[2 * piece + 1 - swap, slot_a],
                ],
                axis=0,
            )
            a_hi, a_lo = split(left)
            b_hi, b_lo = split(right_buf[slot_b])
            sums.append(
                jnp.dot(
                    jnp.concatenate([a_hi, a_lo], axis=1),
                    jnp.concatenate([b_hi, b_hi], axis=0),
                    preferred_element_type=jnp.float32,
                )
                + jnp.dot(a_hi, b_lo, preferred_element_type=jnp.float32)
            )
        for code, value in zip(codes, sums):
            total[code % 128] += value

    pl.loop(0, counts[0])(step)
    save = pltpu.make_async_copy(total.at[pl.ds(0, outs)], out, out_sem)
    save.start()
    save.wait()


UNROLL = 8
CHUNKS = 2


def products(counts, items, order, halves, rights, before, outs):
    pieces, parts = len(halves) // 2, len(rights)
    slots_b, edge, _ = rights[0].shape
    slots_a, part, _ = halves[0].shape
    first = before is None
    extra = [] if first else [before]
    return pl.pallas_call(
        functools.partial(product_kernel, pieces, parts, first, UNROLL),
        out_shape=jax.ShapeDtypeStruct((outs, edge, edge), jnp.float32),
        in_specs=[SMEM] * 3 + [HBM] * (2 * pieces + parts + len(extra)),
        out_specs=HBM,
        scratch_shapes=[
            pltpu.VMEM((2 * pieces, slots_a, part, edge), jnp.float32),
            pltpu.VMEM((parts * slots_b, edge, edge), jnp.float32),
            pltpu.VMEM((outs + 1, edge, edge), jnp.float32),
            pltpu.SemaphoreType.DMA((2 * pieces + parts,)),
            pltpu.SemaphoreType.DMA,
        ],
        compiler_params=pltpu.CompilerParams(vmem_limit_bytes=GRANT),
        cost_estimate=pl.CostEstimate(
            flops=pieces * 600_000_000, bytes_accessed=pieces * 8_000_000, transcendentals=0
        ),
        name="products",
    )(counts, items, order, *halves, *rights, *extra)


def matched_kernel(counts, items, order, *refs):
    lefts, rights = (refs[0:2], refs[2:4]), refs[4:6]
    before, out, left_buf, right_buf, total, load_sems, io_sem = refs[6:]
    outs = out.shape[0]
    slots_a, part, _ = lefts[0][0].shape
    slots_b = rights[0].shape[0]
    batches = counts[0]
    restore = pltpu.make_async_copy(before, total.at[pl.ds(0, outs)], io_sem)
    restore.start()

    def fetch(at):
        buffer = at & 1
        for lane in range(UNROLL):
            code = items[at * UNROLL + lane]
            slot_a = lax.shift_right_logical(code, 14)
            slot_b = lax.shift_right_logical(code, 7) & 127
            for piece, halves in enumerate(lefts):

                @pl.when(lax.div(slot_a, slots_a) == piece)
                def _():
                    swap = order[piece]
                    for half, source in enumerate(halves):
                        rows = pl.multiple_of((swap if half == 0 else 1 - swap) * part, part)
                        pltpu.make_async_copy(
                            source.at[slot_a - piece * slots_a],
                            left_buf.at[buffer, lane, pl.ds(rows, part)],
                            load_sems.at[buffer, lane, half],
                        ).start()

            for which, source in enumerate(rights):

                @pl.when(lax.div(slot_b, slots_b) == which)
                def _():
                    pltpu.make_async_copy(
                        source.at[slot_b - which * slots_b],
                        right_buf.at[buffer, lane],
                        load_sems.at[buffer, lane, 2],
                    ).start()

    def fetched(at):
        buffer = at & 1
        for lane in range(UNROLL):
            for half in range(2):
                pltpu.make_async_copy(
                    lefts[0][0].at[0],
                    left_buf.at[buffer, lane, pl.ds(0, part)],
                    load_sems.at[buffer, lane, half],
                ).wait()
            pltpu.make_async_copy(
                rights[0].at[0], right_buf.at[buffer, lane], load_sems.at[buffer, lane, 2]
            ).wait()

    @pl.when(batches > 0)
    def _():
        fetch(jnp.int32(0))

    restore.wait()

    def step(at):
        @pl.when(at + 1 < batches)
        def _():
            fetch(at + 1)

        fetched(at)
        buffer = at & 1
        sums = []
        for lane in range(UNROLL):
            a_hi, a_lo = split(left_buf[buffer, lane])
            b_hi, b_lo = split(right_buf[buffer, lane])
            sums.append(
                jnp.dot(
                    jnp.concatenate([a_hi, a_lo], axis=1),
                    jnp.concatenate([b_hi, b_hi], axis=0),
                    preferred_element_type=jnp.float32,
                )
                + jnp.dot(a_hi, b_lo, preferred_element_type=jnp.float32)
            )
        for lane, value in enumerate(sums):
            total[items[at * UNROLL + lane] & 127] += value

    pl.loop(0, batches)(step)
    save = pltpu.make_async_copy(total.at[pl.ds(0, outs)], out, io_sem)
    save.start()
    save.wait()


def add_matched(counts, items, order, lefts, rights, before):
    outs, edge, _ = before.shape
    return pl.pallas_call(
        matched_kernel,
        out_shape=jax.ShapeDtypeStruct(before.shape, jnp.float32),
        in_specs=[SMEM] * 3 + [HBM] * (len(lefts) + len(rights) + 1),
        out_specs=HBM,
        scratch_shapes=[
            pltpu.VMEM((2, UNROLL, edge, edge), jnp.float32),
            pltpu.VMEM((2, UNROLL, edge, edge), jnp.float32),
            pltpu.VMEM((outs + 1, edge, edge), jnp.float32),
            pltpu.SemaphoreType.DMA((2, UNROLL, 3)),
            pltpu.SemaphoreType.DMA,
        ],
        compiler_params=pltpu.CompilerParams(vmem_limit_bytes=GRANT),
        cost_estimate=pl.CostEstimate(
            flops=600_000_000, bytes_accessed=16_000_000, transcendentals=0
        ),
        name="add_matched",
    )(counts, items, order, *lefts, *rights, before)


def work_list(lefts, rights, places, kept, first_row):
    rows, width = kept.shape
    pieces, inner, _ = rights.shape
    outs = rows * width
    slots = rows * WA
    rel = lefts - first_row
    here = rel[:, :, None] == jnp.arange(inner, dtype=jnp.int32)
    chosen = (
        jnp.sum(jnp.where(here[:, :, :, None], rights[:, None, :, :] + 1, 0), axis=2) - 1
    )
    at_row = jnp.repeat(kept, WA, axis=0)
    match = (chosen[:, :, :, None] == at_row[None, :, None, :]) & (chosen >= 0)[:, :, :, None]
    target = jnp.sum(jnp.where(match, jnp.arange(width, dtype=jnp.int32) + 1, 0), axis=3) - 1
    live = target >= 0
    slot = jnp.arange(slots, dtype=jnp.int32)[None, :, None]
    slot_a = slot + slots * jnp.arange(pieces, dtype=jnp.int32)[:, None, None]
    slot_b = (places[:, None, None] * inner + rel[:, :, None]) * WB + jnp.arange(WB, dtype=jnp.int32)
    code = slot_a * 16384 + slot_b * 128 + slot // WA * width + target
    live, code = live.reshape(-1), code.reshape(-1)
    spot = jnp.cumsum(live.astype(jnp.int32)) - 1
    place = jnp.arange(live.shape[0], dtype=jnp.int32)
    here = live[None, :] & (spot[None, :] == place[:, None])
    packed = jnp.sum(jnp.where(here, code[None, :] - outs, 0), axis=1) + outs
    count = (jnp.sum(live.astype(jnp.int32)) + UNROLL - 1) // UNROLL
    return count[None], packed


def on_device(a_held, a_slot, a_col, b_held, b_slot, b_col, c_col):
    grid_rows = lax.axis_size("row")
    grid_cols = lax.axis_size("col")
    devices = grid_rows * grid_cols
    copies = grid_cols // grid_rows
    i = lax.axis_index("row")
    c = lax.axis_index("col")
    rows, width = c_col.shape
    hold_a, hold_b = a_slot.shape[0], b_slot.shape[0]
    slots_a, slots_b = rows * WA, KPB * WB

    edge = a_held.shape[1]
    labels = jnp.concatenate([a_slot, a_col, b_slot, b_col])
    tile = jnp.pad(labels, (0, 8 * edge - labels.shape[0])).reshape(8, edge)
    grid, slots = (grid_rows, grid_cols), (slots_a, slots_b)
    sends = pack(grid, slots, a_slot, b_slot, a_held, b_held)
    received, labels = exchange(sends, tile)

    labels = labels.reshape(RING, RING, 2, 2, CORES, -1)[..., : 2 * (hold_a + hold_b)]
    labels = labels.transpose(2, 0, 1, 3, 4, 5).reshape(devices, -1)
    parts = [hold_a, 2 * hold_a, 2 * hold_a + hold_b]
    all_a, all_acol, all_b, all_bcol = (part.reshape(-1) for part in jnp.split(labels, parts, axis=1))

    side = 2 * (c % 2) - 1
    turns = jnp.stack([jnp.int32(1), 1 - side, 1 + side])
    k = (i + c + turns) % grid_rows

    def look_up(panels, slots, table, columns, hold):
        wanted = panels[:, None] * slots + jnp.arange(slots, dtype=jnp.int32)[None, :]
        holder = jnp.arange(table.shape[0], dtype=jnp.int32) // hold
        code = holder * 32 + columns + 1
        found = jnp.sum(jnp.where(table[None, None, :] == wanted[:, :, None], code, 0), axis=2)
        return found // 32, found % 32 - 1

    src_left, col_left = look_up(i * grid_rows + k, slots_a, all_a, all_acol, hold_a)
    src_right, col_right = look_up(k * grid_cols + c, slots_b, all_b, all_bcol, hold_b)

    here = place_of(i * grid_cols + c)
    origin = place_of(src_right[0])
    source = jnp.stack([place_received(origin, here, order) for order in ORDERS[:2]])
    right = collect(received[:2], source, CHUNKS)
    (own,) = collect(received[2:], place_received(place_of(src_left[0]), here, ORDERS[2])[None], 1)
    other = shifted(own, "col", grid_rows)
    cross = permuted(own, "col", lambda at: ((at - 1) ^ 1) + 1)
    mate_first = permuted(own, "col", lambda at: at ^ 1)
    mate_second = permuted(other, "col", lambda at: at ^ 1)
    cross_second = shifted(cross, "col", grid_rows)
    homes = (c + jnp.stack([jnp.int32(0), -side, side])) % grid_cols
    order = (homes >= grid_rows).astype(jnp.int32)

    outs = rows * width
    tables = col_right.reshape(STEPS, KPB, WB)
    count, items = work_list(col_left[:1], tables[:1], jnp.zeros((1,), jnp.int32), c_col, 0)
    total = products(count, items, order[:1], [own, other], right, None, outs)
    places = jnp.stack([(1 - side) // 2, (1 + side) // 2])
    lefts = [mate_first, mate_second, cross, cross_second]
    chunk = slots_b // CHUNKS
    for at in range(CHUNKS):
        shifts = [shifted(right[at], "row", 1), shifted(right[at], "row", -1)]
        first, last = at * chunk // WB, (at + 1) * chunk // WB
        count, items = work_list(col_left[1:], tables[1:, first:last], places, c_col, first)
        total = add_matched(count, items, order[1:], lefts, shifts, total)
    return total.reshape(rows, width, edge, edge)


def solution(mesh):
    return jax.shard_map(
        on_device,
        mesh=mesh,
        in_specs=(
            P(("row", "col"), None, None),
            P(("row", "col")),
            P(("row", "col")),
            P(("row", "col"), None, None),
            P(("row", "col")),
            P(("row", "col")),
            P("row", "col"),
        ),
        out_specs=P("row", "col", None, None),
        check_vma=False,
    )
```

```python
import functools

import jax
import jax.numpy as jnp
from jax import lax
from jax.experimental import pallas as pl
from jax.experimental.pallas import tpu as pltpu
from jax.sharding import PartitionSpec as P

KPB = 16
WA = 4
WB = 4
STEPS = 3
HBM = pl.BlockSpec(memory_space=pltpu.HBM)


def shifted(value, axis, steps):
    count = lax.axis_size(axis)
    pairs = [(source, (source + steps) % count) for source in range(count)]
    return lax.ppermute(value, axis, pairs)


def permuted(value, axis, target):
    count = lax.axis_size(axis)
    return lax.ppermute(value, axis, [(at, target(at) % count) for at in range(count)])


def pack_kernel(
    grid, slots, a_slot, b_slot, a_held, b_held, upper, lower, halves, a_buf, b_buf, sems
):
    grid_rows, grid_cols = grid
    hold_a, hold_b = a_held.shape[0], b_held.shape[0]
    part = halves.shape[1]
    base = hold_a + hold_b

    def load_a(at):
        return pltpu.make_async_copy(a_held.at[at], a_buf.at[at], sems.at[at])

    def load_b(at):
        return pltpu.make_async_copy(b_held.at[at], b_buf.at[at], sems.at[hold_a + at])

    def save_a(at, half, spot):
        return pltpu.make_async_copy(
            a_buf.at[at, pl.ds(half * part, part)], halves.at[spot], sems.at[base + 2 * at + half]
        )

    def save_b(at, half, spot):
        return pltpu.make_async_copy(
            b_buf.at[at, pl.ds(half * part, part)],
            (upper, lower)[half].at[spot],
            sems.at[base + 2 * (hold_a + at) + half],
        )

    pl.loop(0, hold_b)(lambda at: load_b(at).start())
    pl.loop(0, hold_a)(lambda at: load_a(at).start())

    def send_b(at):
        panel = lax.div(b_slot[at], slots[1])
        inner, col = lax.div(panel, grid_cols), lax.rem(panel, grid_cols)
        row = lax.rem(inner - col - 1 + grid_rows + grid_cols, grid_rows)
        place = place_of(row * grid_cols + col)
        load_b(at).wait()
        for half, order in enumerate(ORDERS[:2]):
            save_b(at, half, place_in_send(place, order)).start()

    pl.loop(0, hold_b, unroll=4)(send_b)

    def send_a(at):
        panel = lax.div(a_slot[at], slots[0])
        row, inner = lax.div(panel, grid_rows), lax.rem(panel, grid_rows)
        col = lax.rem(inner - row - 1 + 2 * grid_rows, grid_rows)
        load_a(at).wait()
        for half in range(2):
            place = place_of(row * grid_cols + col + half * grid_rows)
            save_a(at, half, place_in_send(place, ORDERS[2])).start()

    pl.loop(0, hold_a, unroll=4)(send_a)

    for half in range(2):
        pl.loop(0, hold_b)(lambda at: save_b(at, half, 0).wait())
        pl.loop(0, hold_a)(lambda at: save_a(at, half, 0).wait())


GRANT = 60 * 1024 * 1024
SMEM = pl.BlockSpec(memory_space=pltpu.SMEM)
VMEM = pl.BlockSpec(memory_space=pltpu.VMEM)


def pack(grid, slots, a_slot, b_slot, a_held, b_held):
    devices = grid[0] * grid[1]
    edge, cols = a_held.shape[1:]
    send = jax.ShapeDtypeStruct((devices, edge // 2, cols), a_held.dtype)
    return pl.pallas_call(
        functools.partial(pack_kernel, grid, slots),
        out_shape=[send] * 3,
        in_specs=[SMEM] * 2 + [HBM] * 2,
        out_specs=[HBM] * 3,
        scratch_shapes=[
            pltpu.VMEM(a_held.shape, a_held.dtype),
            pltpu.VMEM(b_held.shape, b_held.dtype),
            pltpu.SemaphoreType.DMA((3 * (a_held.shape[0] + b_held.shape[0]),)),
        ],
        compiler_params=pltpu.CompilerParams(vmem_limit_bytes=GRANT),
        name="pack",
    )(a_slot, b_slot, a_held, b_held)


ORDERS = (("x", "y", "z"), ("y", "z", "x"), ("z", "x", "y"))
STEPS_FIRST = (1, 2, 6, 3, 7, 4, 5)
STEPS_LATER = (1, 3, 2)
RING = 4
CORES = 2


def my_place():
    row, col = lax.axis_index("row"), lax.axis_index("col")
    return {
        "x": row // RING * 2 + col // CORES % 2,
        "y": col // RING,
        "z": row % RING,
        "core": col % CORES,
    }


def coords_of(place):
    row = place["x"] // 2 * RING + place["z"]
    col = place["y"] * RING + place["x"] % 2 * CORES + place["core"]
    return row, col


def exchange_kernel(*refs):
    parts = len(ORDERS)
    sends, refs = refs[:parts], refs[parts:]
    tile, refs = refs[0], refs[1:]
    stages = [refs[3 * part : 3 * part + 3] for part in range(parts)]
    labels = refs[3 * parts]
    first_recv, second_recv, third_recv, send_sems, label_send, label_recv = refs[3 * parts + 1 :]
    place = my_place()

    def moved(axis, steps, flip):
        there = dict(place)
        there[axis] = (place[axis] + steps) % RING
        there["core"] = (place["core"] + flip) % CORES
        return there

    def copy(source, target, send_sem, recv_sem, there):
        return pltpu.make_async_remote_copy(
            src_ref=source,
            dst_ref=target,
            send_sem=send_sem,
            recv_sem=recv_sem,
            device_id=coords_of(there),
            device_id_type=pl.DeviceIdType.MESH,
        )

    def spot(there, axis):
        return there[axis] * CORES + there["core"]

    def arrived(like, sem):
        pltpu.make_async_copy(like, like, sem).wait()

    peers = [moved("x", 0, 1)]
    for axis in ("x", "y", "z"):
        for steps in range(1, RING):
            for flip in range(CORES):
                peers.append(moved(axis, steps, flip))
    barrier = pltpu.get_barrier_semaphore()
    for there in peers:
        pl.semaphore_signal(
            barrier, inc=1, device_id=coords_of(there), device_id_type=pl.DeviceIdType.MESH
        )
    pl.semaphore_wait(barrier, len(peers))

    x, y, z = spot(place, "x"), place["y"], place["z"]
    labels[z, y, x] = tile[...]
    for steps in STEPS_FIRST:
        copy(
            labels.at[z, y, x],
            labels.at[z, y, x],
            label_send.at[0],
            label_recv.at[0],
            moved("x", steps // CORES, steps % CORES),
        ).start()
    for steps in STEPS_FIRST:
        for part, (one, two, three) in enumerate(ORDERS):
            there = moved(one, steps // CORES, steps % CORES)
            copy(
                sends[part].at[spot(there, one)],
                stages[part][0].at[spot(place, one)],
                send_sems.at[part, 0],
                first_recv.at[part, steps],
                there,
            ).start()
    arrived(labels.at[0, 0, pl.ds(0, 7)], label_recv.at[0])
    for steps in STEPS_LATER:
        copy(
            labels.at[z, y], labels.at[z, y], label_send.at[1], label_recv.at[1], moved("y", steps, 0)
        ).start()
    arrived(labels.at[0, pl.ds(0, 3)], label_recv.at[1])
    for steps in STEPS_LATER:
        copy(
            labels.at[z], labels.at[z], label_send.at[2], label_recv.at[2], moved("z", steps, 0)
        ).start()

    for steps in (0,) + STEPS_FIRST:
        for part, (one, two, three) in enumerate(ORDERS):
            origin = spot(moved(one, RING - steps // CORES, steps % CORES), one)
            if steps:
                source = stages[part][0]
                arrived(source.at[0], first_recv.at[part, steps])
            else:
                source = sends[part]
            for later in STEPS_LATER:
                there = moved(two, later, 0)
                copy(
                    source.at[origin, there[two]],
                    stages[part][1].at[place[two], origin],
                    send_sems.at[part, 1],
                    second_recv.at[part, later],
                    there,
                ).start()

    def last(part, source, target, there):
        copy(source, target, send_sems.at[part, 2], third_recv.at[part], there).start()

    for part, (one, two, three) in enumerate(ORDERS):
        for steps in (0,) + STEPS_FIRST:
            origin = spot(moved(one, RING - steps // CORES, steps % CORES), one)
            source = stages[part][0] if steps else sends[part]
            for later in STEPS_LATER:
                there = moved(three, later, 0)
                last(
                    part,
                    source.at[origin, place[two], there[three]],
                    stages[part][2].at[place[three], place[two], origin],
                    there,
                )
    for steps in STEPS_LATER:
        for part, (one, two, three) in enumerate(ORDERS):
            origin = moved(two, RING - steps, 0)[two]
            arrived(stages[part][1].at[0], second_recv.at[part, steps])
            for later in STEPS_LATER:
                there = moved(three, later, 0)
                last(
                    part,
                    stages[part][1].at[origin, :, there[three]],
                    stages[part][2].at[place[three], origin],
                    there,
                )
    for part in range(parts):
        arrived(stages[part][2].at[pl.ds(0, 3)], third_recv.at[part])
        arrived(sends[part].at[pl.ds(0, 7)], send_sems.at[part, 0])
        arrived(stages[part][2].at[pl.ds(0, 3)], send_sems.at[part, 1])
        arrived(stages[part][2].at[pl.ds(0, 3)], send_sems.at[part, 2])
    arrived(labels.at[pl.ds(0, 3)], label_recv.at[2])
    arrived(labels.at[0, 0, pl.ds(0, 7)], label_send.at[0])
    arrived(labels.at[0, pl.ds(0, 3)], label_send.at[1])
    arrived(labels.at[pl.ds(0, 3)], label_send.at[2])


def exchange(sends, tile):
    parts = len(sends)
    _, rows, cols = sends[0].shape
    kind = sends[0].dtype
    block = (rows, cols)
    eight = RING * CORES
    shapes = [
        (eight, RING, RING) + block,
        (RING, eight, RING) + block,
        (RING, RING, eight) + block,
    ]
    outs = pl.pallas_call(
        exchange_kernel,
        out_shape=[jax.ShapeDtypeStruct(shape, kind) for shape in shapes] * parts
        + [jax.ShapeDtypeStruct((RING, RING, eight) + tile.shape, tile.dtype)],
        in_specs=[HBM] * parts + [VMEM],
        out_specs=[HBM] * (3 * parts) + [VMEM],
        scratch_shapes=[
            pltpu.SemaphoreType.DMA((parts, eight)),
            pltpu.SemaphoreType.DMA((parts, RING)),
            pltpu.SemaphoreType.DMA((parts,)),
            pltpu.SemaphoreType.DMA((parts, 3)),
            pltpu.SemaphoreType.DMA((3,)),
            pltpu.SemaphoreType.DMA((3,)),
        ],
        compiler_params=pltpu.CompilerParams(
            collective_id=0, has_side_effects=True, vmem_limit_bytes=GRANT
        ),
        name="exchange",
    )(*(send.reshape((eight, RING, RING) + block) for send in sends), tile)
    flat = [out.reshape((-1,) + block) for out in outs[: 3 * parts]]
    groups = [
        [sends[part]] + flat[3 * part : 3 * part + 3] for part in range(parts)
    ]
    return groups, outs[-1]


def place_in_send(place, order):
    one, two, three = (place[axis] for axis in order)
    return ((one * CORES + place["core"]) * RING + two) * RING + three


def place_received(origin, here, order):
    one, two, three = ((origin[axis], here[axis]) for axis in order)
    first = one[0] * CORES + origin["core"]
    same_first = (one[0] == one[1]) & (origin["core"] == here["core"])
    same_two, same_three = two[0] == two[1], three[0] == three[1]
    early = (first * RING + two[0]) * RING + three[0]
    middle = (two[0] * RING * CORES + first) * RING + three[0]
    late = (three[0] * RING + two[0]) * RING * CORES + first
    buffer = jnp.where(
        same_three, jnp.where(same_two, jnp.where(same_first, 0, 1), 2), 3
    )
    at = jnp.where(buffer == 3, late, jnp.where(buffer == 2, middle, early))
    return buffer * 128 + at


def place_of(device):
    row, col = lax.div(device, RING * RING), lax.rem(device, RING * RING)
    return {
        "x": lax.div(row, RING) * 2 + lax.rem(lax.div(col, CORES), 2),
        "y": lax.div(col, RING),
        "z": lax.rem(row, RING),
        "core": lax.rem(col, CORES),
    }


def collect_kernel(pieces, source, *refs):
    groups = [refs[4 * piece : 4 * piece + 4] for piece in range(pieces)]
    buf, sems = refs[-2:]
    outs = refs[4 * pieces : -2]
    count, rows, _ = buf.shape
    part = rows // pieces
    chunk = count // len(outs)

    def target(at, piece):
        return buf.at[at, pl.ds(piece * part, part)]

    def load(at):
        for piece, group in enumerate(groups):
            code = source[piece, at]
            for which, ref in enumerate(group):

                @pl.when(code // 128 == which)
                def _():
                    pltpu.make_async_copy(
                        ref.at[code % 128], target(at, piece), sems.at[piece * count + at]
                    ).start()

    def loaded(at):
        for piece, group in enumerate(groups):
            pltpu.make_async_copy(
                group[3].at[0], target(at, piece), sems.at[piece * count + at]
            ).wait()

    pl.loop(0, count, unroll=2)(load)
    saves = [
        pltpu.make_async_copy(
            buf.at[pl.ds(part * chunk, chunk)], out, sems.at[pieces * count + part]
        )
        for part, out in enumerate(outs)
    ]
    for at, save in enumerate(saves):
        pl.loop(at * chunk, (at + 1) * chunk)(loaded)
        save.start()
    for save in saves:
        save.wait()


def collect(groups, source, chunks):
    pieces = len(groups)
    count = source.shape[1]
    _, rows, cols = groups[0][0].shape
    kind = groups[0][0].dtype
    part = jax.ShapeDtypeStruct((count // chunks, pieces * rows, cols), kind)
    return pl.pallas_call(
        functools.partial(collect_kernel, pieces),
        out_shape=[part] * chunks,
        in_specs=[SMEM] + [HBM] * (4 * pieces),
        out_specs=[HBM] * chunks,
        scratch_shapes=[
            pltpu.VMEM((count, pieces * rows, cols), kind),
            pltpu.SemaphoreType.DMA((pieces * count + chunks,)),
        ],
        compiler_params=pltpu.CompilerParams(vmem_limit_bytes=GRANT),
        name="collect",
    )(source, *(ref for group in groups for ref in group))


def split(value):
    high = value.astype(jnp.bfloat16)
    low = (value - high.astype(jnp.float32)).astype(jnp.bfloat16)
    return high, low


def product_kernel(pieces, parts, first, unroll, counts, items, order, *refs):
    lefts = refs[: 2 * pieces]
    rights = refs[2 * pieces : 2 * pieces + parts]
    refs = refs[2 * pieces + parts :]
    if not first:
        before, refs = refs[0], refs[1:]
    out, left_buf, right_buf, total, load_sems, out_sem = refs
    outs, edge, _ = out.shape
    slots_a = lefts[0].shape[0]
    slots_b = rights[0].shape[0]

    loads = [
        pltpu.make_async_copy(source, left_buf.at[at], load_sems.at[at])
        for at, source in enumerate(lefts)
    ] + [
        pltpu.make_async_copy(
            source, right_buf.at[pl.ds(at * slots_b, slots_b)], load_sems.at[2 * pieces + at]
        )
        for at, source in enumerate(rights)
    ]
    if not first:
        restore = pltpu.make_async_copy(before, total.at[pl.ds(0, outs)], out_sem)
        restore.start()
    for load in loads:
        load.start()
    if first:

        def clear(at):
            total[at] = jnp.zeros((edge, edge), jnp.float32)

        pl.loop(0, outs)(clear)
    else:
        restore.wait()
    for load in loads:
        load.wait()

    def step(at):
        codes = [items[at * unroll + lane] for lane in range(unroll)]
        sums = []
        for code in codes:
            slot_a = code // 16384
            slot_b = (code // 128) % 128
            piece = slot_a // slots_a
            swap = order[piece]
            slot_a = slot_a % slots_a
            left = jnp.concatenate(
                [
                    left_buf[2 * piece + swap, slot_a],
                    left_buf[2 * piece + 1 - swap, slot_a],
                ],
                axis=0,
            )
            a_hi, a_lo = split(left)
            b_hi, b_lo = split(right_buf[slot_b])
            sums.append(
                jnp.dot(
                    jnp.concatenate([a_hi, a_lo], axis=1),
                    jnp.concatenate([b_hi, b_hi], axis=0),
                    preferred_element_type=jnp.float32,
                )
                + jnp.dot(a_hi, b_lo, preferred_element_type=jnp.float32)
            )
        for code, value in zip(codes, sums):
            total[code % 128] += value

    pl.loop(0, counts[0])(step)
    save = pltpu.make_async_copy(total.at[pl.ds(0, outs)], out, out_sem)
    save.start()
    save.wait()


UNROLL = 8
CHUNKS = 2


def products(counts, items, order, halves, rights, before, outs):
    pieces, parts = len(halves) // 2, len(rights)
    slots_b, edge, _ = rights[0].shape
    slots_a, part, _ = halves[0].shape
    first = before is None
    extra = [] if first else [before]
    return pl.pallas_call(
        functools.partial(product_kernel, pieces, parts, first, UNROLL),
        out_shape=jax.ShapeDtypeStruct((outs, edge, edge), jnp.float32),
        in_specs=[SMEM] * 3 + [HBM] * (2 * pieces + parts + len(extra)),
        out_specs=HBM,
        scratch_shapes=[
            pltpu.VMEM((2 * pieces, slots_a, part, edge), jnp.float32),
            pltpu.VMEM((parts * slots_b, edge, edge), jnp.float32),
            pltpu.VMEM((outs + 1, edge, edge), jnp.float32),
            pltpu.SemaphoreType.DMA((2 * pieces + parts,)),
            pltpu.SemaphoreType.DMA,
        ],
        compiler_params=pltpu.CompilerParams(vmem_limit_bytes=24 * 1024 * 1024),
        cost_estimate=pl.CostEstimate(
            flops=pieces * 600_000_000, bytes_accessed=pieces * 8_000_000, transcendentals=0
        ),
        name="products",
    )(counts, items, order, *halves, *rights, *extra)


def work_list(lefts, rights, places, kept, first_row):
    rows, width = kept.shape
    pieces, inner, _ = rights.shape
    outs = rows * width
    slots = rows * WA
    rel = lefts - first_row
    here = rel[:, :, None] == jnp.arange(inner, dtype=jnp.int32)
    chosen = (
        jnp.sum(jnp.where(here[:, :, :, None], rights[:, None, :, :] + 1, 0), axis=2) - 1
    )
    at_row = jnp.repeat(kept, WA, axis=0)
    match = (chosen[:, :, :, None] == at_row[None, :, None, :]) & (chosen >= 0)[:, :, :, None]
    target = jnp.sum(jnp.where(match, jnp.arange(width, dtype=jnp.int32) + 1, 0), axis=3) - 1
    live = target >= 0
    slot = jnp.arange(slots, dtype=jnp.int32)[None, :, None]
    slot_a = slot + slots * jnp.arange(pieces, dtype=jnp.int32)[:, None, None]
    slot_b = (places[:, None, None] * inner + rel[:, :, None]) * WB + jnp.arange(WB, dtype=jnp.int32)
    code = slot_a * 16384 + slot_b * 128 + slot // WA * width + target
    live, code = live.reshape(-1), code.reshape(-1)
    spot = jnp.cumsum(live.astype(jnp.int32)) - 1
    place = jnp.arange(live.shape[0], dtype=jnp.int32)
    here = live[None, :] & (spot[None, :] == place[:, None])
    packed = jnp.sum(jnp.where(here, code[None, :] - outs, 0), axis=1) + outs
    count = (jnp.sum(live.astype(jnp.int32)) + UNROLL - 1) // UNROLL
    return count[None], packed


def on_device(a_held, a_slot, a_col, b_held, b_slot, b_col, c_col):
    grid_rows = lax.axis_size("row")
    grid_cols = lax.axis_size("col")
    devices = grid_rows * grid_cols
    copies = grid_cols // grid_rows
    i = lax.axis_index("row")
    c = lax.axis_index("col")
    rows, width = c_col.shape
    hold_a, hold_b = a_slot.shape[0], b_slot.shape[0]
    slots_a, slots_b = rows * WA, KPB * WB

    edge = a_held.shape[1]
    labels = jnp.concatenate([a_slot, a_col, b_slot, b_col])
    tile = jnp.pad(labels, (0, 8 * edge - labels.shape[0])).reshape(8, edge)
    grid, slots = (grid_rows, grid_cols), (slots_a, slots_b)
    sends = pack(grid, slots, a_slot, b_slot, a_held, b_held)
    received, labels = exchange(sends, tile)

    labels = labels.reshape(RING, RING, 2, 2, CORES, -1)[..., : 2 * (hold_a + hold_b)]
    labels = labels.transpose(2, 0, 1, 3, 4, 5).reshape(devices, -1)
    parts = [hold_a, 2 * hold_a, 2 * hold_a + hold_b]
    all_a, all_acol, all_b, all_bcol = (part.reshape(-1) for part in jnp.split(labels, parts, axis=1))

    side = 2 * (c % 2) - 1
    turns = jnp.stack([jnp.int32(1), 1 - side, 1 + side])
    k = (i + c + turns) % grid_rows

    def look_up(panels, slots, table, columns, hold):
        wanted = panels[:, None] * slots + jnp.arange(slots, dtype=jnp.int32)[None, :]
        holder = jnp.arange(table.shape[0], dtype=jnp.int32) // hold
        code = holder * 32 + columns + 1
        found = jnp.sum(jnp.where(table[None, None, :] == wanted[:, :, None], code, 0), axis=2)
        return found // 32, found % 32 - 1

    src_left, col_left = look_up(i * grid_rows + k, slots_a, all_a, all_acol, hold_a)
    src_right, col_right = look_up(k * grid_cols + c, slots_b, all_b, all_bcol, hold_b)

    here = place_of(i * grid_cols + c)
    origin = place_of(src_right[0])
    source = jnp.stack([place_received(origin, here, order) for order in ORDERS[:2]])
    right = collect(received[:2], source, CHUNKS)
    (own,) = collect(received[2:], place_received(place_of(src_left[0]), here, ORDERS[2])[None], 1)
    other = shifted(own, "col", grid_rows)
    cross = permuted(own, "col", lambda at: ((at - 1) ^ 1) + 1)
    mate_first = permuted(own, "col", lambda at: at ^ 1)
    mate_second = permuted(other, "col", lambda at: at ^ 1)
    cross_second = shifted(cross, "col", grid_rows)
    homes = (c + jnp.stack([jnp.int32(0), -side, side])) % grid_cols
    order = (homes >= grid_rows).astype(jnp.int32)

    outs = rows * width
    tables = col_right.reshape(STEPS, KPB, WB)
    count, items = work_list(col_left[:1], tables[:1], jnp.zeros((1,), jnp.int32), c_col, 0)
    total = products(count, items, order[:1], [own, other], right, None, outs)
    places = jnp.stack([(1 - side) // 2, (1 + side) // 2])
    lefts = [mate_first, mate_second, cross, cross_second]
    chunk = slots_b // CHUNKS
    for at in range(CHUNKS):
        shifts = [shifted(right[at], "row", 1), shifted(right[at], "row", -1)]
        first, last = at * chunk // WB, (at + 1) * chunk // WB
        count, items = work_list(col_left[1:], tables[1:, first:last], places, c_col, first)
        total = products(count, items, order[1:], lefts, shifts, total, outs)
    return total.reshape(rows, width, edge, edge)


def solution(mesh):
    return jax.shard_map(
        on_device,
        mesh=mesh,
        in_specs=(
            P(("row", "col"), None, None),
            P(("row", "col")),
            P(("row", "col")),
            P(("row", "col"), None, None),
            P(("row", "col")),
            P(("row", "col")),
            P("row", "col"),
        ),
        out_specs=P("row", "col", None, None),
        check_vma=False,
    )
```
